256 devices in a mesh: ctx: 16 (over x, y_hi, core), chan: 16 (over z, y_lo).
Axes of the slice: x: 4, y: 4 (y_hi: 2, y_lo: 2; y = y_hi * 2 + y_lo), z: 8, core: 2. Of those that a mesh axis runs over, the one named last changes fastest.
Arguments:
- inputs: bfloat16 [256, 4096], P('ctx', 'chan'), may hold values from -6 to 6
- gain: float32 [4096], replicated, may hold values from 0.25 to 1.75
- w_in: bfloat16 [4096, 3, 4096], P(None, None, 'chan'), may hold values from -0.09375 to 0.09375
- w_out: bfloat16 [4096, 4096], P('chan'), may hold values from -0.125 to 0.125
- history: bfloat16 [4096, 2, 4096], P('ctx', None, 'chan'), may hold values from -6 to 6
- filt_far: bfloat16 [4096, 2, 4096], P('ctx', None, 'chan'), may hold values from -0.09375 to 0.09375
- filt_near: bfloat16 [256, 2, 4096], P(None, None, 'chan'), may hold values from -0.09375 to 0.09375
Outputs:
- mixed: bfloat16 [256, 4096], P('ctx', 'chan')
- gated: bfloat16 [256, 4096], P('ctx', 'chan')
The draws below stay inside these ranges and needn't reach their ends.
All inputs are finite; a program needn't handle non-finite values.
Results may differ from the reference program's by a relative error of at most 0.0066.
Values may be sent and summed in bfloat16 or wider, within the bound.
No kernel may reach another device: no remote copies, remote signals or barrier semaphores. Data moves between devices by JAX's collectives and lax.ppermute only.
A program may use at most 64 MiB of HBM per device.

```python
import jax
import jax.numpy as jnp
from jax import lax

D = 4096
NEW = 256
H = 4096


def strengthened(drawn, key, source, target, parts, factor):
    owner, partner = [(jnp.arange(drawn.shape[position]) // (drawn.shape[position] // parts)).reshape([-1 if axis == position else 1 for axis in range(drawn.ndim)]) for position in (source, target)]
    chosen = jax.random.permutation(key, parts)[partner]
    strong = (owner == chosen) | (owner == (partner + parts // 2) % parts)
    return jnp.where(strong, factor * drawn, drawn)


def levels(stream_key, dims, pieces, smallest, largest):
    def one(dim, parts):
        steps = jax.random.uniform(jax.random.fold_in(jax.random.fold_in(stream_key, 6), dim), (parts,), jnp.float32, smallest / len(pieces), largest / len(pieces))
        return jnp.repeat(jnp.exp(steps), dims[dim] // parts).reshape((-1,) + (1,) * (len(dims) - dim - 1))

    factor_of = one(*pieces[0])
    for cut in pieces[1:]:
        factor_of = factor_of * one(*cut)
    return factor_of


def centred(own_key, extent, deviation, reach, pieces=(), kind=jnp.bfloat16):
    entries = jax.random.normal(own_key, extent, jnp.float32) * deviation
    if len(pieces) > 0:
        entries = levels(own_key, extent, pieces, -0.22, 0.18) * entries
    return jnp.clip(entries, min=-reach, max=reach).astype(kind)


def heavy_noise(key, dims, width, limit, pieces, heavy, kind=jnp.bfloat16):
    values = width * jax.random.normal(key, dims, jnp.float32)
    if pieces:
        values = values * levels(key, dims, pieces, -0.22, 0.18)
    return jnp.clip(strengthened(values, jax.random.fold_in(key, 3), *heavy), -limit, limit).astype(kind)


def setup_inputs(seed: int = 0) -> dict:
    seeds = jax.random.split(jax.random.key(seed), 8)
    return {
        "inputs": centred(seeds[0], (NEW, D), 1.0, 6.0, ((0, 16), (1, 16))),
        "gain": jnp.clip(1.0 + 0.15 * jax.random.normal(seeds[1], (D,), jnp.float32), 0.25, 1.75),
        "w_in": centred(seeds[2], (D, 3, D), D ** -0.5, 0.09375, ((2, 16),)),
        "w_out": heavy_noise(seeds[3], (D, D), D ** -0.5, 0.125, ((0, 16),), (0, 1, 16, 2.0)),
        "history": centred(seeds[4], (H, 2, D), 1.0, 6.0, ((0, 16), (2, 16))),
        "filt_far": centred(seeds[5], (H, 2, D), (H + NEW) ** -0.5, 0.09375, ((0, 16), (2, 16))),
        "filt_near": centred(seeds[6], (NEW, 2, D), (H + NEW) ** -0.5, 0.09375, ((2, 16),)),
    }


def split_blocks(array, groups, chan_block):
    return array.reshape(array.shape[0], groups, chan_block).transpose(1, 0, 2)

def history_conv(taps_far, taps_near, past_rows, fresh_rows):
    taps = jnp.concatenate([taps_far, taps_near], 0).astype(jnp.float32)[::-1]
    signal = jnp.concatenate([past_rows, fresh_rows], 0).astype(jnp.float32)
    total_len = taps.shape[0]
    fresh_len = fresh_rows.shape[0]
    chan_block = min(taps.shape[1], 256)
    groups = taps.shape[1] // chan_block

    def one_block(pair):
        kernel_block, signal_block = pair
        spectra = jnp.fft.rfft(kernel_block, n=2 * total_len, axis=0) * jnp.fft.rfft(signal_block, n=2 * total_len, axis=0)
        circular = jnp.fft.irfft(spectra, n=2 * total_len, axis=0)
        return circular[total_len - fresh_len:total_len]
    blocks = lax.map(one_block, (split_blocks(taps, groups, chan_block), split_blocks(signal, groups, chan_block)))
    return blocks.transpose(1, 0, 2).reshape(fresh_len, groups * chan_block)

def reference(inputs, gain, w_in, w_out, history, filt_far, filt_near):
    features = inputs.astype(jnp.float32)
    mean_sq = lax.optimization_barrier(jnp.mean(features * features, axis=-1, keepdims=True))
    normed = (features * lax.rsqrt(mean_sq + 1e-06) * gain).astype(jnp.bfloat16)
    model_width = w_in.shape[0]
    projected = jnp.dot(normed, w_in.reshape(model_width, 3 * model_width), preferred_element_type=jnp.float32)
    projected = projected.reshape(normed.shape[0], 3, model_width)
    values = projected[:, 0].astype(jnp.bfloat16)
    gate_one = projected[:, 1].astype(jnp.bfloat16)
    gate_two = projected[:, 2].astype(jnp.bfloat16)
    first_conv = history_conv(filt_far[:, 0], filt_near[:, 0], history[:, 0], values)
    gated = (gate_one.astype(jnp.float32) * first_conv).astype(jnp.bfloat16)
    second_conv = history_conv(filt_far[:, 1], filt_near[:, 1], history[:, 1], gated)
    mixed_in = (gate_two.astype(jnp.float32) * second_conv).astype(jnp.bfloat16)
    mixed = jnp.dot(mixed_in, w_out, preferred_element_type=jnp.float32).astype(jnp.bfloat16)
    return (mixed, gated)
```

```python
import functools

import jax
import jax.numpy as jnp
import numpy as np
from jax import lax
from jax.experimental import pallas as pl
from jax.experimental.pallas import tpu as pltpu
from jax.sharding import PartitionSpec as P

BF16 = jnp.bfloat16
F32 = jnp.float32
VMEM = pl.BlockSpec(memory_space=pltpu.VMEM)
SMEM = pl.BlockSpec(memory_space=pltpu.SMEM)
ANY = pl.BlockSpec(memory_space=pl.ANY)
LIMIT = 24 << 20


def split_up(table):
    high = np.asarray(table, np.float32).astype(jnp.bfloat16)
    low = (table - high.astype(np.float64)).astype(np.float32).astype(jnp.bfloat16)
    return high, low


def dft_tables(length):
    order = np.concatenate([np.arange(0, length, 2), np.arange(1, length, 2)])
    theta = np.pi * (order + 0.5) / length
    angle = theta[:, None] * np.arange(length)[None, :]
    forward = np.concatenate([np.cos(angle), np.sin(angle)], 0)
    back = theta[None, :] * (length - 1 - np.arange(length))[:, None]
    inverse = np.concatenate([np.cos(back), -np.sin(back)], 1) / length
    return (*split_up(forward), *split_up(inverse))


def dot(a, b):
    return jnp.dot(a, b, preferred_element_type=F32)


def spectrum(high, low, rows):
    return dot(high[...], rows) + dot(low[...], rows)


def back_to_time(high, low, product):
    upper = product.astype(BF16)
    lower = (product - upper.astype(F32)).astype(BF16)
    return dot(high, upper) + dot(high, lower) + dot(low, upper)


def times_conjugate(window, signal):
    half = window.shape[0] // 2
    wc, ws = window[:half], window[half:]
    sc, ss = signal[:half], signal[half:]
    return jnp.concatenate([wc * sc + ws * ss, wc * ss - ws * sc], 0)


def past_kernel(which, last, own, border, near, history, fh, fl, ih, il, part):
    half = fh.shape[0] // 2
    quarter = half // 2
    after = jnp.where(last[0] > 0, near[:, which, :], border[:, which, :])
    first = spectrum(fh, fl, own[:, which, :])
    second = spectrum(fh, fl, after)
    bc, bs = second[:half], second[half:]
    window = first + jnp.concatenate([-bs[:quarter], bs[quarter:], bc[:quarter], -bc[quarter:]], 0)
    signal = spectrum(fh, fl, history[:, which, :])
    result = back_to_time(ih[...], il[...], times_conjugate(window, signal))
    part[...] = result.astype(BF16).reshape(part.shape)


def near_kernel(near, fh, fl, spectra):
    for which in range(2):
        spectra[which] = spectrum(fh, fl, near[:, which, :])


def project_kernel(gathered, gain, w_hbm, out, w, sems):
    pieces, rows, width = gathered.shape
    per = pieces // 4
    copies = []
    for q in range(4):
        span = pl.ds(q * per * width, per * width)
        copies.append(pltpu.make_async_copy(w_hbm.at[:, span, :], w.at[:, span, :], sems.at[q]))
        copies[-1].start()
    total = jnp.zeros((rows, width), F32)
    for s in range(pieces):
        x = gathered[s].astype(F32)
        total += x * x
    mean_sq = jnp.sum(total, axis=1, keepdims=True) / (pieces * width)
    scale = lax.rsqrt(mean_sq + 1e-06)
    sums = [jnp.zeros((rows, width), F32) for _ in range(3)]
    for s in range(pieces):
        if s % per == 0:
            copies[s // per].wait()
        g = jnp.concatenate([gain[2 * s : 2 * s + 1], gain[2 * s + 1 : 2 * s + 2]], 1)
        normed = (gathered[s].astype(F32) * scale * g).astype(BF16)
        for k in range(3):
            sums[k] += dot(normed, w[k, s * width : (s + 1) * width, :])
    for k in range(3):
        out[k] = sums[k].astype(BF16)


def payload_kernel(arrived, projected, part2, out):
    count = arrived.shape[0]
    past = jnp.sum(arrived[...].astype(F32), axis=0).astype(BF16)
    rows = jnp.concatenate([projected[0], projected[1], past], 0)
    for d in range(count):
        out[d, : rows.shape[0]] = rows
        out[d, rows.shape[0] :] = part2[d]


def mix_kernel(index, arrived, projected, spectra, fh, fl, ih, il, w_out, partial, gated_own, gated_all):
    count, packed, width = arrived.shape
    rows = packed // 4
    everything = count * rows
    values = arrived[:, :rows].reshape(everything, width)
    gate_one = arrived[:, rows : 2 * rows].reshape(everything, width).astype(F32)
    past_one = arrived[:, 2 * rows : 3 * rows].reshape(everything, width).astype(F32)
    first = back_to_time(ih[...], il[...], times_conjugate(spectra[0], spectrum(fh, fl, values)))
    gated = (gate_one * (past_one + first)).astype(BF16)
    gated_all[...] = gated
    own = pl.ds(pl.multiple_of(index[0] * rows, rows), rows)
    gated_own[...] = gated_all[own, :]
    second = back_to_time(ih[own, :], il[own, :], times_conjugate(spectra[1], spectrum(fh, fl, gated)))
    past_two = jnp.sum(arrived[:, 3 * rows :].astype(F32), axis=0)
    mixed_in = (projected[2].astype(F32) * (past_two + second)).astype(BF16)
    for d in range(partial.shape[0]):
        cols = dot(mixed_in, w_out[:, d * width : (d + 1) * width])
        partial[d] = cols.astype(BF16)


def total_kernel(arrived, out):
    out[...] = jnp.sum(arrived[...].astype(F32), axis=0).astype(BF16)


def call(kernel, out_shape, in_specs, flops, nbytes, scratch=(), name=None, limit=LIMIT):
    return pl.pallas_call(
        kernel,
        out_shape=out_shape,
        in_specs=in_specs,
        out_specs=jax.tree.map(lambda _: VMEM, out_shape),
        scratch_shapes=list(scratch),
        cost_estimate=pl.CostEstimate(flops=flops, bytes_accessed=nbytes, transcendentals=0),
        compiler_params=pltpu.CompilerParams(vmem_limit_bytes=limit),
        name=name,
    )


def exchanged(array, axis):
    return lax.all_to_all(array, axis, split_axis=0, concat_axis=0, tiled=True)


def per_device(inputs, gain, w_in, w_out, history, filt_far, filt_near):
    rows, width = inputs.shape
    fresh = filt_near.shape[0]
    ctx_count = lax.axis_size("ctx")
    chan_count = lax.axis_size("chan")
    ctx_index = lax.axis_index("ctx")
    tables = [jnp.asarray(t) for t in dft_tables(fresh)]
    index = ctx_index.reshape(1).astype(jnp.int32)
    last = (index == ctx_count - 1).astype(jnp.int32)

    border = lax.ppermute(filt_far, "ctx", [(i, i - 1) for i in range(1, ctx_count)])
    gathered = exchanged(jnp.broadcast_to(inputs, (chan_count, rows, width)), "chan")

    unit = fresh * fresh * 4 * width
    blocks = jax.ShapeDtypeStruct((ctx_count, rows, width), BF16)
    parts = [
        call(
            functools.partial(past_kernel, which),
            blocks,
            [SMEM] + [VMEM] * 8,
            unit * 9,
            4 << 20,
            name=f"past{which}",
        )(last, filt_far, border, filt_near, history, *tables)
        for which in range(2)
    ]
    spectra = call(
        near_kernel,
        jax.ShapeDtypeStruct((2, 2 * fresh, width), F32),
        [VMEM] * 3,
        unit * 4,
        2 << 20,
        name="near",
    )(filt_near, *tables[:2])
    arrived_one = exchanged(parts[0], "ctx")

    w_three = w_in.transpose(1, 0, 2)
    projected = call(
        project_kernel,
        jax.ShapeDtypeStruct((3, rows, width), BF16),
        [VMEM, VMEM, ANY],
        2 * rows * w_in.size,
        2 * w_in.size,
        scratch=[pltpu.VMEM(w_three.shape, BF16), pltpu.SemaphoreType.DMA((4,))],
        name="project",
    )(gathered, gain.reshape(-1, 128), w_three)

    packed = call(
        payload_kernel,
        jax.ShapeDtypeStruct((ctx_count, 4 * rows, width), BF16),
        [VMEM] * 3,
        1 << 20,
        1 << 20,
        name="payload",
    )(arrived_one, projected, parts[1])
    everyone = exchanged(packed, "ctx")

    partial, gated = call(
        mix_kernel,
        (
            jax.ShapeDtypeStruct((chan_count, rows, width), BF16),
            jax.ShapeDtypeStruct((rows, width), BF16),
        ),
        [SMEM] + [VMEM] * 8,
        unit * 8,
        4 << 20,
        scratch=[pltpu.VMEM((fresh, width), BF16)],
        name="mix",
    )(index, everyone, projected, spectra, *tables, w_out)
    mixed = call(
        total_kernel,
        jax.ShapeDtypeStruct((rows, width), BF16),
        [VMEM],
        1 << 16,
        1 << 17,
        name="total",
    )(exchanged(partial, "chan"))
    return (mixed, gated)


def solution(mesh):
    placed = (
        P("ctx", "chan"),
        P(),
        P(None, None, "chan"),
        P("chan", None),
        P("ctx", None, "chan"),
        P("ctx", None, "chan"),
        P(None, None, "chan"),
    )
    return jax.shard_map(
        per_device,
        mesh=mesh,
        in_specs=placed,
        out_specs=(P("ctx", "chan"), P("ctx", "chan")),
        check_vma=False,
    )
```

```python
import jax
import jax.numpy as jnp
import numpy as np
from jax import lax
from jax.experimental import pallas as pl
from jax.experimental.pallas import tpu as pltpu
from jax.sharding import PartitionSpec as P

BF16 = jnp.bfloat16
F32 = jnp.float32
VMEM = pl.BlockSpec(memory_space=pltpu.VMEM)
SMEM = pl.BlockSpec(memory_space=pltpu.SMEM)
HBM = pl.BlockSpec(memory_space=pltpu.HBM)
LIMIT = 24 << 20


def split_up(table):
    high = np.asarray(table, np.float32).astype(jnp.bfloat16)
    low = (table - high.astype(np.float64)).astype(np.float32).astype(jnp.bfloat16)
    return np.stack([high, low])


def dft_tables(length):
    order = np.concatenate([np.arange(0, length, 2), np.arange(1, length, 2)])
    theta = np.pi * (order + 0.5) / length
    angle = theta[:, None] * np.arange(length)[None, :]
    forward = np.concatenate([np.cos(angle), np.sin(angle)], 0)
    back = theta[None, :] * (length - 1 - np.arange(length))[:, None]
    inverse = np.concatenate([np.cos(back), -np.sin(back)], 1) / length
    return split_up(forward), split_up(inverse)


def dot(a, b):
    return jnp.dot(a, b, preferred_element_type=F32)


def spectrum(forward, rows):
    return dot(forward[0], rows) + dot(forward[1], rows)


def back_to_time(high, low, product):
    upper = product.astype(BF16)
    lower = (product - upper.astype(F32)).astype(BF16)
    return dot(high, upper) + dot(high, lower) + dot(low, upper)


def times_conjugate(window, signal):
    half = window.shape[0] // 2
    wc, ws = window[:half], window[half:]
    sc, ss = signal[:half], signal[half:]
    return jnp.concatenate([wc * sc + ws * ss, wc * ss - ws * sc], 0)


def past_kernel(last, border, own, near, history, f_hbm, i_hbm, gain_hbm, products, near_v, f, i, gain, own_v, history_v, sems):
    pairs = [(own, own_v), (f_hbm, f), (near, near_v), (history, history_v), (i_hbm, i), (gain_hbm, gain)]
    copies = [pltpu.make_async_copy(a, b, sems.at[n]) for n, (a, b) in enumerate(pairs)]
    for copy in copies:
        copy.start()
    half = f.shape[1] // 2
    quarter = half // 2
    for copy in copies[:4]:
        copy.wait()
    for which in range(2):
        first = spectrum(f, own_v[:, which, :])
        second = spectrum(f, jnp.where(last[0] > 0, near_v[:, which, :], border[:, which, :]))
        bc, bs = second[:half], second[half:]
        window = first + jnp.concatenate([-bs[:quarter], bs[quarter:], bc[:quarter], -bc[quarter:]], 0)
        products[which] = times_conjugate(window, spectrum(f, history_v[:, which, :]))
    for copy in copies[4:]:
        copy.wait()


def project_kernel(
    index, gathered, gain, w_hbm, f, i, near, products, out, gates, spectrum_two, padded, w, sems
):
    pieces, rows, width = gathered.shape
    steps = sems.shape[0]
    per = pieces // steps
    copies = []
    for q in range(steps):
        span = pl.ds(q * per * width, per * width)
        copies.append(pltpu.make_async_copy(w_hbm.at[:, span, :], w.at[:, span, :], sems.at[q]))
        copies[-1].start()
    part_two = back_to_time(i[0], i[1], products[1]).astype(BF16)
    out[:, rows:] = part_two.reshape(out.shape[0], rows, width)
    spectrum_two[...] = spectrum(f, near[:, 1, :])
    spectrum_one = spectrum(f, near[:, 0, :])
    total = jnp.zeros((rows, width), F32)
    for s in range(pieces):
        x = gathered[s].astype(F32)
        total += x * x
    mean_sq = jnp.sum(total, axis=1, keepdims=True) / (pieces * width)
    scale = lax.rsqrt(mean_sq + 1e-06)
    sums = [jnp.zeros((rows, width), F32) for _ in range(3)]
    for s in range(pieces):
        if s % per == 0:
            copies[s // per].wait()
        g = jnp.concatenate([gain[2 * s : 2 * s + 1], gain[2 * s + 1 : 2 * s + 2]], 1)
        normed = (gathered[s].astype(F32) * scale * g).astype(BF16)
        for k in range(3):
            sums[k] += dot(normed, w[k, s * width : (s + 1) * width, :])
    gates[0] = sums[1].astype(BF16)
    gates[1] = sums[2].astype(BF16)
    padded[...] = jnp.zeros_like(padded)
    padded[pl.ds(pl.multiple_of(index[0] * rows, rows), rows), :] = sums[0].astype(BF16)
    product = products[0] + times_conjugate(spectrum_one, spectrum(f, padded[...]))
    part_one = back_to_time(i[0], i[1], product).astype(BF16)
    out[:, :rows] = part_one.reshape(out.shape[0], rows, width)


def gate_kernel(arrived, gates, copies, gated, past_two):
    sums = jnp.sum(arrived[...].astype(F32), axis=0)
    rows = sums.shape[0] // 2
    own = (gates[0].astype(F32) * sums[:rows]).astype(BF16)
    gated[...] = own
    past_two[...] = sums[rows:]
    for d in range(copies.shape[0]):
        copies[d] = own


def mix_kernel(index, gated, gates, past_two, spectrum_two, f, i, w_hbm, partial, w_out, sem):
    load = pltpu.make_async_copy(w_hbm, w_out, sem)
    load.start()
    count, rows, width = gated.shape
    own = pl.ds(pl.multiple_of(index[0] * rows, rows), rows)
    signal = spectrum(f, gated[...].reshape(count * rows, width))
    second = back_to_time(i[0, own, :], i[1, own, :], times_conjugate(spectrum_two[...], signal))
    mixed_in = (gates[1].astype(F32) * (past_two[...] + second)).astype(BF16)
    load.wait()
    for d in range(partial.shape[0]):
        partial[d] = dot(mixed_in, w_out[:, d * width : (d + 1) * width]).astype(BF16)


def total_kernel(arrived, out):
    out[...] = jnp.sum(arrived[...].astype(F32), axis=0).astype(BF16)


def call(kernel, out_shape, in_specs, flops, nbytes, scratch=(), name=None, limit=LIMIT):
    return pl.pallas_call(
        kernel,
        out_shape=out_shape,
        in_specs=in_specs,
        out_specs=jax.tree.map(lambda _: VMEM, out_shape),
        scratch_shapes=list(scratch),
        cost_estimate=pl.CostEstimate(flops=flops, bytes_accessed=nbytes, transcendentals=0),
        compiler_params=pltpu.CompilerParams(vmem_limit_bytes=limit),
        name=name,
    )


def in_hbm(array):
    return pltpu.with_memory_space_constraint(array, pltpu.HBM)


def exchanged(array, axis):
    return lax.all_to_all(array, axis, split_axis=0, concat_axis=0, tiled=True)


def per_device(inputs, gain, w_in, w_out, history, filt_far, filt_near):
    rows, width = inputs.shape
    fresh = filt_near.shape[0]
    ctx_count = lax.axis_size("ctx")
    chan_count = lax.axis_size("chan")
    ctx_index = lax.axis_index("ctx")
    forward, inverse = [jnp.asarray(t) for t in dft_tables(fresh)]
    index = ctx_index.reshape(1).astype(jnp.int32)
    last = (index == ctx_count - 1).astype(jnp.int32)

    border = lax.ppermute(filt_far, "ctx", [(i, i - 1) for i in range(1, ctx_count)])
    gathered = exchanged(jnp.broadcast_to(inputs, (chan_count, rows, width)), "chan")

    unit = fresh * fresh * 4 * width
    w_three = w_in.transpose(1, 0, 2)
    scales = gain.reshape(-1, 128)
    whole = jax.ShapeDtypeStruct((2, 2 * fresh, width), F32)
    products, near, f, i, scales = call(
        past_kernel,
        (whole, *(jax.ShapeDtypeStruct(a.shape, a.dtype) for a in (filt_near, forward, inverse, scales))),
        [SMEM, VMEM] + [HBM] * 6,
        unit * 12,
        2 << 20,
        scratch=[pltpu.VMEM(filt_far.shape, BF16)] * 2 + [pltpu.SemaphoreType.DMA((6,))],
        name="past",
    )(last, border, *(in_hbm(a) for a in (filt_far, filt_near, history, forward, inverse, scales)))

    blocks = jax.ShapeDtypeStruct((ctx_count, rows, width), BF16)
    payload, gates, spectrum_two = call(
        project_kernel,
        (
            jax.ShapeDtypeStruct((ctx_count, 2 * rows, width), BF16),
            jax.ShapeDtypeStruct((2, rows, width), BF16),
            jax.ShapeDtypeStruct(whole.shape[1:], F32),
        ),
        [SMEM, VMEM, VMEM, HBM] + [VMEM] * 4,
        2 * rows * w_in.size + unit * 12,
        2 * w_in.size,
        scratch=[
            pltpu.VMEM((fresh, width), BF16),
            pltpu.VMEM(w_three.shape, BF16),
            pltpu.SemaphoreType.DMA((8,)),
        ],
        name="project",
    )(index, gathered, scales, in_hbm(w_three), f, i, near, products)

    copies, gated, past_two = call(
        gate_kernel,
        (blocks, jax.ShapeDtypeStruct((rows, width), BF16), jax.ShapeDtypeStruct((rows, width), F32)),
        [VMEM] * 2,
        1 << 20,
        1 << 19,
        name="gate",
    )(exchanged(payload, "ctx"), gates)

    partial = call(
        mix_kernel,
        jax.ShapeDtypeStruct((chan_count, rows, width), BF16),
        [SMEM] + [VMEM] * 6 + [HBM],
        unit * 5,
        4 << 20,
        scratch=[pltpu.VMEM(w_out.shape, BF16), pltpu.SemaphoreType.DMA],
        name="mix",
    )(index, exchanged(copies, "ctx"), gates, past_two, spectrum_two, f, i, in_hbm(w_out))
    mixed = call(
        total_kernel,
        jax.ShapeDtypeStruct((rows, width), BF16),
        [VMEM],
        1 << 16,
        1 << 17,
        name="total",
    )(exchanged(partial, "chan"))
    return (mixed, gated)


def solution(mesh):
    placed = (
        P("ctx", "chan"),
        P(),
        P(None, None, "chan"),
        P("chan", None),
        P("ctx", None, "chan"),
        P("ctx", None, "chan"),
        P(None, None, "chan"),
    )
    return jax.shard_map(
        per_device,
        mesh=mesh,
        in_specs=placed,
        out_specs=(P("ctx", "chan"), P("ctx", "chan")),
        check_vma=False,
    )
```

```python
import jax
import jax.numpy as jnp
import numpy as np
from jax import lax
from jax.experimental import pallas as pl
from jax.experimental.pallas import tpu as pltpu
from jax.sharding import PartitionSpec as P

BF16 = jnp.bfloat16
F32 = jnp.float32
VMEM = pl.BlockSpec(memory_space=pltpu.VMEM)
SMEM = pl.BlockSpec(memory_space=pltpu.SMEM)
HBM = pl.BlockSpec(memory_space=pltpu.HBM)
LIMIT = 24 << 20


def split_up(table):
    high = np.asarray(table, np.float32).astype(jnp.bfloat16)
    low = (table - high.astype(np.float64)).astype(np.float32).astype(jnp.bfloat16)
    return np.stack([high, low])


def dft_tables(length):
    order = np.concatenate([np.arange(0, length, 2), np.arange(1, length, 2)])
    theta = np.pi * (order + 0.5) / length
    angle = theta[:, None] * np.arange(length)[None, :]
    forward = np.concatenate([np.cos(angle), np.sin(angle)], 0)
    back = theta[None, :] * (length - 1 - np.arange(length))[:, None]
    inverse = np.concatenate([np.cos(back), -np.sin(back)], 1) / length
    return split_up(forward), split_up(inverse)


def dot(a, b):
    return jnp.dot(a, b, preferred_element_type=F32)


def spectrum(forward, rows):
    return dot(forward[0], rows) + dot(forward[1], rows)


def back_to_time(high, low, product):
    upper = product.astype(BF16)
    lower = (product - upper.astype(F32)).astype(BF16)
    return dot(high, upper) + dot(high, lower) + dot(low, upper)


def times_conjugate(window, signal):
    half = window.shape[0] // 2
    wc, ws = window[:half], window[half:]
    sc, ss = signal[:half], signal[half:]
    return jnp.concatenate([wc * sc + ws * ss, wc * ss - ws * sc], 0)


def past_part(which, last, own, border, near, history, f, i):
    half = f.shape[1] // 2
    quarter = half // 2
    first = spectrum(f, own[:, which, :])
    second = spectrum(f, jnp.where(last[0] > 0, near[:, which, :], border[:, which, :]))
    bc, bs = second[:half], second[half:]
    window = first + jnp.concatenate([-bs[:quarter], bs[quarter:], bc[:quarter], -bc[quarter:]], 0)
    return back_to_time(i[0], i[1], times_conjugate(window, spectrum(f, history[:, which, :]))).astype(BF16)


def past_kernel(
    last, border, own_hbm, near_hbm, history_hbm, f_hbm, i_hbm, gain_hbm,
    part_one, own, near, history, f, i, gain, sems,
):
    pairs = [(own_hbm, own), (f_hbm, f), (near_hbm, near), (history_hbm, history), (i_hbm, i), (gain_hbm, gain)]
    copies = [pltpu.make_async_copy(a, b, sems.at[n]) for n, (a, b) in enumerate(pairs)]
    for copy in copies:
        copy.start()
    for copy in copies:
        copy.wait()
    part_one[...] = past_part(0, last, own, border, near, history, f, i)


def project_kernel(last, gathered, gain, w_hbm, own, border, near, history, f, i, out, gate_two, w, sems):
    pieces, rows, width = gathered.shape
    steps = sems.shape[0]
    per = pieces // steps
    copies = []
    for q in range(steps):
        span = pl.ds(q * per * width, per * width)
        copies.append(pltpu.make_async_copy(w_hbm.at[:, span, :], w.at[:, span, :], sems.at[q]))
        copies[-1].start()
    part_two = past_part(1, last, own, border, near, history, f, i)
    out[:, 2 * rows :] = part_two.reshape(out.shape[0], rows, width)
    total = jnp.zeros((rows, width), F32)
    for s in range(pieces):
        x = gathered[s].astype(F32)
        total += x * x
    mean_sq = jnp.sum(total, axis=1, keepdims=True) / (pieces * width)
    scale = lax.rsqrt(mean_sq + 1e-06)
    sums = [jnp.zeros((rows, width), F32) for _ in range(3)]
    for s in range(pieces):
        if s % per == 0:
            copies[s // per].wait()
        g = jnp.concatenate([gain[2 * s : 2 * s + 1], gain[2 * s + 1 : 2 * s + 2]], 1)
        normed = (gathered[s].astype(F32) * scale * g).astype(BF16)
        for k in range(3):
            sums[k] += dot(normed, w[k, s * width : (s + 1) * width, :])
    gate_two[...] = sums[2].astype(BF16)
    shared = jnp.concatenate([sums[0].astype(BF16), sums[1].astype(BF16)], 0)
    for d in range(out.shape[0]):
        out[d, : 2 * rows] = shared


def near_kernel(near, f, spectra):
    for which in range(2):
        spectra[which] = spectrum(f, near[:, which, :])


def mix_kernel(
    index, arrived, gate_two, sum_here, sum_there, spectra, f, i, w_hbm, partial, gated_own, gated_all, w_out, sem
):
    load = pltpu.make_async_copy(w_hbm, w_out, sem)
    load.start()
    count, packed, width = arrived.shape
    rows = packed // 3
    fresh = count * rows
    values = arrived[:, :rows].reshape(fresh, width)
    gate_one = arrived[:, rows : 2 * rows].reshape(fresh, width).astype(F32)
    past_one = sum_here[...].astype(F32) + sum_there[...].astype(F32)
    first = back_to_time(i[0], i[1], times_conjugate(spectra[0], spectrum(f, values)))
    gated = (gate_one * (past_one + first)).astype(BF16)
    gated_all[...] = gated
    own = pl.ds(pl.multiple_of(index[0] * rows, rows), rows)
    gated_own[...] = gated_all[own, :]
    second = back_to_time(i[0, own, :], i[1, own, :], times_conjugate(spectra[1], spectrum(f, gated)))
    past_two = jnp.sum(arrived[:, 2 * rows :].astype(F32), axis=0)
    mixed_in = (gate_two[...].astype(F32) * (past_two + second)).astype(BF16)
    load.wait()
    for d in range(partial.shape[0]):
        partial[d] = dot(mixed_in, w_out[:, d * width : (d + 1) * width]).astype(BF16)


def total_kernel(arrived, out):
    out[...] = jnp.sum(arrived[...].astype(F32), axis=0).astype(BF16)


def call(kernel, out_shape, in_specs, flops, nbytes, scratch=(), limit=LIMIT):
    return pl.pallas_call(
        kernel,
        out_shape=out_shape,
        in_specs=in_specs,
        out_specs=jax.tree.map(lambda _: VMEM, out_shape),
        scratch_shapes=list(scratch),
        cost_estimate=pl.CostEstimate(flops=flops, bytes_accessed=nbytes, transcendentals=0),
        compiler_params=pltpu.CompilerParams(vmem_limit_bytes=limit),
    )


def in_hbm(array):
    return pltpu.with_memory_space_constraint(array, pltpu.HBM)


def exchanged(array, axis):
    return lax.all_to_all(array, axis, split_axis=0, concat_axis=0, tiled=True)


def swapped(array, axis, step):
    return lax.ppermute(array, axis, [(i, i ^ step) for i in range(lax.axis_size(axis))])


def added(a, b):
    return (a.astype(F32) + b.astype(F32)).astype(BF16)


def layer(inputs, gain, w_in, w_out, history, filt_far, filt_near):
    rows, width = inputs.shape
    fresh = filt_near.shape[0]
    ctx_count = lax.axis_size("ctx")
    chan_count = lax.axis_size("chan")
    ctx_index = lax.axis_index("ctx")
    forward, inverse = [jnp.asarray(t) for t in dft_tables(fresh)]
    index = ctx_index.reshape(1).astype(jnp.int32)
    last = (index == ctx_count - 1).astype(jnp.int32)

    border = lax.ppermute(filt_far, "ctx", [(i, i - 1) for i in range(1, ctx_count)])
    gathered = exchanged(jnp.broadcast_to(inputs, (chan_count, rows, width)), "chan")

    unit = fresh * fresh * 4 * width
    w_three = w_in.transpose(1, 0, 2)
    scales = gain.reshape(-1, 128)
    part_one, own, near, history, f, i, scales = call(
        past_kernel,
        (
            jax.ShapeDtypeStruct((fresh, width), BF16),
            *(
                jax.ShapeDtypeStruct(a.shape, a.dtype)
                for a in (filt_far, filt_near, history, forward, inverse, scales)
            ),
        ),
        [SMEM, VMEM] + [HBM] * 6,
        unit * 9,
        2 << 20,
        scratch=[pltpu.SemaphoreType.DMA((6,))],
    )(last, border, *(in_hbm(a) for a in (filt_far, filt_near, history, forward, inverse, scales)))

    here = part_one
    there = swapped(here, "ctx", 1)
    here = added(here, there)
    there = swapped(here, "ctx", 4)

    payload, gate_two = call(
        project_kernel,
        (
            jax.ShapeDtypeStruct((ctx_count, 3 * rows, width), BF16),
            jax.ShapeDtypeStruct((rows, width), BF16),
        ),
        [SMEM, VMEM, VMEM, HBM] + [VMEM] * 6,
        2 * rows * w_in.size + unit * 9,
        2 * w_in.size,
        scratch=[pltpu.VMEM(w_three.shape, BF16), pltpu.SemaphoreType.DMA((8,))],
    )(last, gathered, scales, in_hbm(w_three), own, border, near, history, f, i)

    here = added(here, there)
    payload, here = lax.optimization_barrier((payload, here))
    there = swapped(here, "ctx", 8)
    arrived = exchanged(payload, "ctx")
    here = added(here, there)
    there = swapped(here, "ctx", 2)
    spectra = call(
        near_kernel, jax.ShapeDtypeStruct((2, 2 * fresh, width), F32), [VMEM] * 2, unit * 4, 2 << 20
    )(near, f)

    partial, gated = call(
        mix_kernel,
        (
            jax.ShapeDtypeStruct((chan_count, rows, width), BF16),
            jax.ShapeDtypeStruct((rows, width), BF16),
        ),
        [SMEM] + [VMEM] * 7 + [HBM],
        unit * 8,
        4 << 20,
        scratch=[pltpu.VMEM((fresh, width), BF16), pltpu.VMEM(w_out.shape, BF16), pltpu.SemaphoreType.DMA],
    )(index, arrived, gate_two, here, there, spectra, f, i, in_hbm(w_out))
    mixed = call(
        total_kernel, jax.ShapeDtypeStruct((rows, width), BF16), [VMEM], 1 << 16, 1 << 17
    )(exchanged(partial, "chan"))
    return (mixed, gated)


def solution(mesh):
    placed = (
        P("ctx", "chan"),
        P(),
        P(None, None, "chan"),
        P("chan", None),
        P("ctx", None, "chan"),
        P("ctx", None, "chan"),
        P(None, None, "chan"),
    )
    return jax.shard_map(
        layer,
        mesh=mesh,
        in_specs=placed,
        out_specs=(P("ctx", "chan"), P("ctx", "chan")),
        check_vma=False,
    )
```

```python
import jax
import jax.numpy as jnp
import numpy as np
from jax import lax
from jax.experimental import pallas as pl
from jax.experimental.pallas import tpu as pltpu
from jax.sharding import PartitionSpec as P

BF16 = jnp.bfloat16
F32 = jnp.float32
VMEM = pl.BlockSpec(memory_space=pltpu.VMEM)
SMEM = pl.BlockSpec(memory_space=pltpu.SMEM)
HBM = pl.BlockSpec(memory_space=pltpu.HBM)
LIMIT = 24 << 20


def split_up(table):
    high = np.asarray(table, np.float32).astype(jnp.bfloat16)
    low = (table - high.astype(np.float64)).astype(np.float32).astype(jnp.bfloat16)
    return np.stack([high, low])


def dft_tables(length):
    order = np.concatenate([np.arange(0, length, 2), np.arange(1, length, 2)])
    theta = np.pi * (order + 0.5) / length
    angle = theta[:, None] * np.arange(length)[None, :]
    forward = np.concatenate([np.cos(angle), np.sin(angle)], 0)
    back = theta[None, :] * (length - 1 - np.arange(length))[:, None]
    inverse = np.concatenate([np.cos(back), -np.sin(back)], 1) / length
    return split_up(forward), split_up(inverse)


def dot(a, b):
    return jnp.dot(a, b, preferred_element_type=F32)


def spectrum(forward, rows):
    return dot(forward[0], rows) + dot(forward[1], rows)


def back_to_time(high, low, product):
    upper = product.astype(BF16)
    lower = (product - upper.astype(F32)).astype(BF16)
    return dot(high, upper) + dot(high, lower) + dot(low, upper)


def times_conjugate(window, signal):
    half = window.shape[0] // 2
    wc, ws = window[:half], window[half:]
    sc, ss = signal[:half], signal[half:]
    return jnp.concatenate([wc * sc + ws * ss, wc * ss - ws * sc], 0)


def spread_out(rows, spread):
    count, kinds, width = rows.shape
    flat = rows[...].reshape(count * kinds, width)
    lanes = spread.shape[2]
    for h in range(width // lanes):
        spread[h] = flat[:, h * lanes : (h + 1) * lanes].astype(F32)


def parted(spread, kinds, which):
    count = spread.shape[1] // kinds
    rows = [spread[h, pl.ds(which, count, stride=kinds), :].astype(BF16) for h in range(spread.shape[0])]
    return jnp.concatenate(rows, 1)


def past_part(own, after, history, f, i):
    half = f.shape[1] // 2
    quarter = half // 2
    first, second = spectrum(f, own), spectrum(f, after)
    bc, bs = second[:half], second[half:]
    window = first + jnp.concatenate([-bs[:quarter], bs[quarter:], bc[:quarter], -bc[quarter:]], 0)
    return back_to_time(i[0], i[1], times_conjugate(window, spectrum(f, history)))


def past_kernel(
    index, last, border, own_hbm, near_hbm, history_hbm, f_hbm, i_hbm, gain_hbm,
    keep, send, later, near, f, i, gain,
    own, history, part, spread, sems,
):
    pairs = [(own_hbm, own), (near_hbm, near), (history_hbm, history), (f_hbm, f), (i_hbm, i), (gain_hbm, gain)]
    copies = [pltpu.make_async_copy(a, b, sems.at[n]) for n, (a, b) in enumerate(pairs)]
    for copy in copies:
        copy.start()
    for copy in copies:
        copy.wait()

    @pl.when(last[0] > 0)
    def _():
        spread_out(near, spread.at[1])

    @pl.when(last[0] == 0)
    def _():
        spread_out(border, spread.at[1])

    spread_out(own, spread.at[0])
    spread_out(history, spread.at[2])
    for n in range(3):
        later[n] = parted(spread.at[n], 2, 1)
    part[...] = past_part(*(parted(spread.at[n], 2, 0) for n in range(3)), f, i)
    half = keep.shape[0]
    mine = index[0] % 2
    keep[...] = part[pl.ds(pl.multiple_of(mine * half, half), half), :]
    send[...] = part[pl.ds(pl.multiple_of((1 - mine) * half, half), half), :]


def project_kernel(gathered, gain, w_hbm, later, f, i, out, gate_two, w, sems):
    pieces, rows, width = gathered.shape
    steps = sems.shape[0]
    per = pieces // steps
    copies = []
    for q in range(steps):
        span = pl.ds(q * per * width, per * width)
        copies.append(pltpu.make_async_copy(w_hbm.at[:, span, :], w.at[:, span, :], sems.at[q]))
        copies[-1].start()
    part_two = past_part(later[0], later[1], later[2], f, i).astype(BF16)
    out[:, 2 * rows :] = part_two.reshape(out.shape[0], rows, width)
    total = jnp.zeros((rows, width), F32)
    for s in range(pieces):
        x = gathered[s].astype(F32)
        total += x * x
    mean_sq = jnp.sum(total, axis=1, keepdims=True) / (pieces * width)
    scale = lax.rsqrt(mean_sq + 1e-06)
    sums = [jnp.zeros((rows, width), F32) for _ in range(3)]
    for s in range(pieces):
        if s % per == 0:
            copies[s // per].wait()
        g = jnp.concatenate([gain[2 * s : 2 * s + 1], gain[2 * s + 1 : 2 * s + 2]], 1)
        normed = (gathered[s].astype(F32) * scale * g).astype(BF16)
        for k in range(3):
            sums[k] += dot(normed, w[k, s * width : (s + 1) * width, :])
    gate_two[...] = sums[2].astype(BF16)
    shared = jnp.concatenate([sums[0].astype(BF16), sums[1].astype(BF16)], 0)
    for d in range(out.shape[0]):
        out[d, : 2 * rows] = shared


def near_kernel(near, f, spectra, spread):
    spread_out(near, spread)
    for which in range(2):
        spectra[which] = spectrum(f, parted(spread, 2, which))


def mix_kernel(
    index, arrived, gate_two, here, there, spectra, f, i, w_hbm,
    partial, gated_own, past_one, gated_all, w_out, sem,
):
    load = pltpu.make_async_copy(w_hbm, w_out, sem)
    load.start()
    count, packed, width = arrived.shape
    rows = packed // 3
    fresh = count * rows
    values = arrived[:, :rows].reshape(fresh, width)
    gate_one = arrived[:, rows : 2 * rows].reshape(fresh, width).astype(F32)
    half = here.shape[0]
    mine = index[0] % 2
    past_one[pl.ds(pl.multiple_of(mine * half, half), half), :] = here[...]
    past_one[pl.ds(pl.multiple_of((1 - mine) * half, half), half), :] = there[...]
    first = back_to_time(i[0], i[1], times_conjugate(spectra[0], spectrum(f, values)))
    gated = (gate_one * (past_one[...].astype(F32) + first)).astype(BF16)
    gated_all[...] = gated
    own = pl.ds(pl.multiple_of(index[0] * rows, rows), rows)
    gated_own[...] = gated_all[own, :]
    second = back_to_time(i[0, own, :], i[1, own, :], times_conjugate(spectra[1], spectrum(f, gated)))
    past_two = jnp.sum(arrived[:, 2 * rows :].astype(F32), axis=0)
    mixed_in = (gate_two[...].astype(F32) * (past_two + second)).astype(BF16)
    load.wait()
    for d in range(partial.shape[0]):
        partial[d] = dot(mixed_in, w_out[:, d * width : (d + 1) * width]).astype(BF16)


def total_kernel(arrived, out):
    out[...] = jnp.sum(arrived[...].astype(F32), axis=0).astype(BF16)


def call(kernel, out_shape, in_specs, flops, nbytes, scratch=(), limit=LIMIT):
    return pl.pallas_call(
        kernel,
        out_shape=out_shape,
        in_specs=in_specs,
        out_specs=jax.tree.map(lambda _: VMEM, out_shape),
        scratch_shapes=list(scratch),
        cost_estimate=pl.CostEstimate(flops=flops, bytes_accessed=nbytes, transcendentals=0),
        compiler_params=pltpu.CompilerParams(vmem_limit_bytes=limit),
    )


def in_hbm(array):
    return pltpu.with_memory_space_constraint(array, pltpu.HBM)


def exchanged(array, axis):
    return lax.all_to_all(array, axis, split_axis=0, concat_axis=0, tiled=True)


def swapped(array, axis, step):
    return lax.ppermute(array, axis, [(i, i ^ step) for i in range(lax.axis_size(axis))])


def added(a, b):
    return (a.astype(F32) + b.astype(F32)).astype(BF16)


def layer(inputs, gain, w_in, w_out, history, filt_far, filt_near):
    rows, width = inputs.shape
    fresh = filt_near.shape[0]
    ctx_count = lax.axis_size("ctx")
    chan_count = lax.axis_size("chan")
    ctx_index = lax.axis_index("ctx")
    forward, inverse = [jnp.asarray(t) for t in dft_tables(fresh)]
    index = ctx_index.reshape(1).astype(jnp.int32)
    last = (index == ctx_count - 1).astype(jnp.int32)

    border = lax.ppermute(filt_far, "ctx", [(i, i - 1) for i in range(1, ctx_count)])
    gathered = exchanged(jnp.broadcast_to(inputs, (chan_count, rows, width)), "chan")

    unit = fresh * fresh * 4 * width
    w_three = w_in.transpose(1, 0, 2)
    scales = gain.reshape(-1, 128)
    half = jax.ShapeDtypeStruct((fresh // 2, width), F32)
    spread = (width // 128, 2 * fresh, 128)
    keep, send, later, near, f, i, scales = call(
        past_kernel,
        (
            half,
            half,
            jax.ShapeDtypeStruct((3, fresh, width), BF16),
            *(jax.ShapeDtypeStruct(a.shape, a.dtype) for a in (filt_near, forward, inverse, scales)),
        ),
        [SMEM, SMEM, VMEM] + [HBM] * 6,
        unit * 9,
        2 << 20,
        scratch=[
            pltpu.VMEM(filt_far.shape, BF16),
            pltpu.VMEM(history.shape, BF16),
            pltpu.VMEM((fresh, width), F32),
            pltpu.VMEM((3, *spread), F32),
            pltpu.SemaphoreType.DMA((6,)),
        ],
    )(index, last, border, *(in_hbm(a) for a in (filt_far, filt_near, history, forward, inverse, scales)))

    here = added(keep, swapped(send, "ctx", 1))
    there = swapped(here, "ctx", 2)

    payload, gate_two = call(
        project_kernel,
        (
            jax.ShapeDtypeStruct((ctx_count, 3 * rows, width), BF16),
            jax.ShapeDtypeStruct((rows, width), BF16),
        ),
        [VMEM, VMEM, HBM] + [VMEM] * 3,
        2 * rows * w_in.size + unit * 9,
        2 * w_in.size,
        scratch=[pltpu.VMEM(w_three.shape, BF16), pltpu.SemaphoreType.DMA((8,))],
    )(gathered, scales, in_hbm(w_three), later, f, i)

    here = added(here, there)
    payload, here = lax.optimization_barrier((payload, here))
    there = swapped(here, "ctx", 8)
    arrived = exchanged(payload, "ctx")
    here = added(here, there)
    here = added(here, swapped(here, "ctx", 4))
    there = swapped(here, "ctx", 1)
    spectra = call(
        near_kernel,
        jax.ShapeDtypeStruct((2, 2 * fresh, width), F32),
        [VMEM] * 2,
        unit * 4,
        2 << 20,
        scratch=[pltpu.VMEM(spread, F32)],
    )(near, f)

    partial, gated = call(
        mix_kernel,
        (
            jax.ShapeDtypeStruct((chan_count, rows, width), BF16),
            jax.ShapeDtypeStruct((rows, width), BF16),
        ),
        [SMEM] + [VMEM] * 7 + [HBM],
        unit * 8,
        4 << 20,
        scratch=[pltpu.VMEM((fresh, width), BF16)] * 2
        + [pltpu.VMEM(w_out.shape, BF16), pltpu.SemaphoreType.DMA],
    )(index, arrived, gate_two, here, there, spectra, f, i, in_hbm(w_out))
    mixed = call(
        total_kernel, jax.ShapeDtypeStruct((rows, width), BF16), [VMEM], 1 << 16, 1 << 17
    )(exchanged(partial, "chan"))
    return (mixed, gated)


def solution(mesh):
    placed = (
        P("ctx", "chan"),
        P(),
        P(None, None, "chan"),
        P("chan", None),
        P("ctx", None, "chan"),
        P("ctx", None, "chan"),
        P(None, None, "chan"),
    )
    return jax.shard_map(
        layer,
        mesh=mesh,
        in_specs=placed,
        out_specs=(P("ctx", "chan"), P("ctx", "chan")),
        check_vma=False,
    )
```

```python
import jax
import jax.numpy as jnp
import numpy as np
from jax import lax
from jax.experimental import pallas as pl
from jax.experimental.pallas import tpu as pltpu
from jax.sharding import PartitionSpec as P

BF16 = jnp.bfloat16
F32 = jnp.float32
VMEM = pl.BlockSpec(memory_space=pltpu.VMEM)
SMEM = pl.BlockSpec(memory_space=pltpu.SMEM)
HBM = pl.BlockSpec(memory_space=pltpu.HBM)
LIMIT = 24 << 20


def split_up(table):
    high = np.asarray(table, np.float32).astype(jnp.bfloat16)
    low = (table - high.astype(np.float64)).astype(np.float32).astype(jnp.bfloat16)
    return np.stack([high, low])


def dft_tables(length):
    order = np.concatenate([np.arange(0, length, 2), np.arange(1, length, 2)])
    theta = np.pi * (order + 0.5) / length
    angle = theta[:, None] * np.arange(length)[None, :]
    forward = np.concatenate([np.cos(angle), np.sin(angle)], 0)
    back = theta[None, :] * (length - 1 - np.arange(length))[:, None]
    inverse = np.concatenate([np.cos(back), -np.sin(back)], 1) / length
    return split_up(forward), split_up(inverse)


def dot(a, b):
    return jnp.dot(a, b, preferred_element_type=F32)


def spectrum(forward, rows):
    return dot(forward[0], rows) + dot(forward[1], rows)


def back_to_time(high, low, product):
    upper = product.astype(BF16)
    lower = (product - upper.astype(F32)).astype(BF16)
    return dot(high, upper) + dot(high, lower) + dot(low, upper)


def times_conjugate(window, signal):
    half = window.shape[0] // 2
    wc, ws = window[:half], window[half:]
    sc, ss = signal[:half], signal[half:]
    return jnp.concatenate([wc * sc + ws * ss, wc * ss - ws * sc], 0)


def spread_out(rows, spread):
    count, kinds, width = rows.shape
    flat = rows[...].reshape(count * kinds, width)
    lanes = spread.shape[2]
    for h in range(width // lanes):
        spread[h] = flat[:, h * lanes : (h + 1) * lanes].astype(F32)


def parted(spread, kinds, which):
    count = spread.shape[1] // kinds
    rows = [spread[h, pl.ds(which, count, stride=kinds), :].astype(BF16) for h in range(spread.shape[0])]
    return jnp.concatenate(rows, 1)


def past_part(own, after, history, f, i):
    half = f.shape[1] // 2
    quarter = half // 2
    first, second = spectrum(f, own), spectrum(f, after)
    bc, bs = second[:half], second[half:]
    window = first + jnp.concatenate([-bs[:quarter], bs[quarter:], bc[:quarter], -bc[quarter:]], 0)
    return back_to_time(i[0], i[1], times_conjugate(window, spectrum(f, history)))


def past_kernel(
    index, last, border, own_hbm, near_hbm, history_hbm, f_hbm, i_hbm, gain_hbm,
    keep, send, near, f, i, gain,
    own, history, parts, spread, sems,
):
    pairs = [(own_hbm, own), (near_hbm, near), (history_hbm, history), (f_hbm, f), (i_hbm, i), (gain_hbm, gain)]
    copies = [pltpu.make_async_copy(a, b, sems.at[n]) for n, (a, b) in enumerate(pairs)]
    for copy in copies:
        copy.start()
    for copy in copies:
        copy.wait()

    @pl.when(last[0] > 0)
    def _():
        spread_out(near, spread.at[1])

    @pl.when(last[0] == 0)
    def _():
        spread_out(border, spread.at[1])

    spread_out(own, spread.at[0])
    spread_out(history, spread.at[2])
    mine = index[0] % 2
    fresh, lanes = keep.shape[0] // 2, keep.shape[1]
    for which in range(2):
        part = past_part(*(parted(spread.at[n], 2, which) for n in range(3)), f, i)
        if which == 0:
            low, high = part[:, :lanes], part[:, lanes:]
            keep[:fresh] = jnp.where(mine == 0, low, high)
            send[:fresh] = jnp.where(mine == 0, high, low)
        else:
            parts[...] = part.reshape(parts.shape)
            rows = (fresh // 2, lanes)
            for h in range(2):
                there = pl.ds(fresh + h * rows[0], rows[0])
                span = slice(h * lanes, (h + 1) * lanes)
                keep[there] = parts[:, mine, :, span].reshape(rows)
                send[there] = parts[:, 1 - mine, :, span].reshape(rows)


def project_kernel(gathered, gain, w_hbm, keep, came, out, gate_two, w, sems):
    pieces, rows, width = gathered.shape
    steps = sems.shape[0]
    per = pieces // steps
    copies = []
    for q in range(steps):
        span = pl.ds(q * per * width, per * width)
        copies.append(pltpu.make_async_copy(w_hbm.at[:, span, :], w.at[:, span, :], sems.at[q]))
        copies[-1].start()
    lanes = out.shape[2]
    fresh = keep.shape[0] // 2
    pair = (keep[fresh:] + came[fresh:]).astype(BF16)
    for d in range(out.shape[0]):
        start = (d % 2) * (fresh // 2) + (d // 2) * rows
        out[d, 2 * rows :] = pair[start : start + rows]
    total = jnp.zeros((rows, width), F32)
    for s in range(pieces):
        x = gathered[s].astype(F32)
        total += x * x
    mean_sq = jnp.sum(total, axis=1, keepdims=True) / (pieces * width)
    scale = lax.rsqrt(mean_sq + 1e-06)
    sums = [jnp.zeros((rows, width), F32) for _ in range(3)]
    for s in range(pieces):
        if s % per == 0:
            copies[s // per].wait()
        g = jnp.concatenate([gain[2 * s : 2 * s + 1], gain[2 * s + 1 : 2 * s + 2]], 1)
        normed = (gathered[s].astype(F32) * scale * g).astype(BF16)
        for k in range(3):
            sums[k] += dot(normed, w[k, s * width : (s + 1) * width, :])
    gate_two[...] = sums[2].astype(BF16)
    shared = jnp.concatenate([sums[0].astype(BF16), sums[1].astype(BF16)], 0)
    for d in range(out.shape[0]):
        out[d, : 2 * rows] = shared[:, (d % 2) * lanes : (d % 2 + 1) * lanes]


def near_kernel(index, near, f, spectra, spread):
    lanes = spectra.shape[2]
    half = pl.ds(pl.multiple_of((index[0] % 2) * lanes, lanes), lanes)
    spread_out(near.at[:, :, half], spread)
    for which in range(2):
        spectra[which] = spectrum(f, parted(spread, 2, which))


def mix_kernel(index, arrived, here, there, spectra, f, i, w_hbm, keep, send, w_out, gated_all, sums, sem):
    load = pltpu.make_async_copy(w_hbm, w_out, sem)
    load.start()
    count, packed, lanes = arrived.shape
    rows = packed // 3
    fresh = count * rows
    values = arrived[:, :rows].reshape(fresh, lanes)
    gate_one = arrived[:, rows : 2 * rows].reshape(fresh, lanes).astype(F32)
    past_one = here[...].astype(F32) + there[...].astype(F32)
    first = back_to_time(i[0], i[1], times_conjugate(spectra[0], spectrum(f, values)))
    gated = (gate_one * (past_one + first)).astype(BF16)
    gated_all[...] = gated
    mine = index[0] % 2
    chip = pl.ds(pl.multiple_of((index[0] - mine) * rows, 2 * rows), 2 * rows)
    second = back_to_time(i[0, chip, :], i[1, chip, :], times_conjugate(spectra[1], spectrum(f, gated)))
    past_two = [arrived[p, 2 * rows :].astype(F32) for p in range(2)]
    for s in range(2, count):
        past_two[s % 2] += arrived[s, 2 * rows :].astype(F32)
    sums[0] = (second + jnp.concatenate(past_two, 0)).reshape(sums.shape[1:])
    sums[1] = gated_all[chip, :].astype(F32).reshape(sums.shape[1:])
    keep[...] = sums[:, mine]
    send[...] = sums[:, 1 - mine]
    load.wait()


def finish_kernel(index, keep, came, gate_two, w_out, partial, gated):
    first = index[0] % 2 == 0
    low, high = jnp.where(first, keep[...], came[...]), jnp.where(first, came[...], keep[...])
    both = jnp.concatenate([low, high], 2)
    gated[...] = both[1].astype(BF16)
    mixed_in = (gate_two[...].astype(F32) * both[0]).astype(BF16)
    width = partial.shape[2]
    for d in range(partial.shape[0]):
        partial[d] = dot(mixed_in, w_out[:, d * width : (d + 1) * width]).astype(BF16)


def total_kernel(arrived, out):
    out[...] = jnp.sum(arrived[...].astype(F32), axis=0).astype(BF16)


def call(kernel, out_shape, in_specs, flops, nbytes, scratch=(), limit=LIMIT):
    return pl.pallas_call(
        kernel,
        out_shape=out_shape,
        in_specs=in_specs,
        out_specs=jax.tree.map(lambda _: VMEM, out_shape),
        scratch_shapes=list(scratch),
        cost_estimate=pl.CostEstimate(flops=flops, bytes_accessed=nbytes, transcendentals=0),
        compiler_params=pltpu.CompilerParams(vmem_limit_bytes=limit),
    )


def in_hbm(array):
    return pltpu.with_memory_space_constraint(array, pltpu.HBM)


def exchanged(array, axis):
    return lax.all_to_all(array, axis, split_axis=0, concat_axis=0, tiled=True)


def swapped(array, axis, step):
    return lax.ppermute(array, axis, [(i, i ^ step) for i in range(lax.axis_size(axis))])


def added(a, b):
    return (a.astype(F32) + b.astype(F32)).astype(BF16)


def layer(inputs, gain, w_in, w_out, history, filt_far, filt_near):
    rows, width = inputs.shape
    fresh = filt_near.shape[0]
    ctx_count = lax.axis_size("ctx")
    chan_count = lax.axis_size("chan")
    ctx_index = lax.axis_index("ctx")
    forward, inverse = [jnp.asarray(t) for t in dft_tables(fresh)]
    index = ctx_index.reshape(1).astype(jnp.int32)
    last = (index == ctx_count - 1).astype(jnp.int32)

    border = lax.ppermute(filt_far, "ctx", [(i, i - 1) for i in range(1, ctx_count)])
    gathered = exchanged(jnp.broadcast_to(inputs, (chan_count, rows, width)), "chan")

    unit = fresh * fresh * 4 * width
    w_three = w_in.transpose(1, 0, 2)
    scales = gain.reshape(-1, 128)
    lanes = width // 2
    half = jax.ShapeDtypeStruct((2 * fresh, lanes), F32)
    spread = (2 * fresh, lanes)
    keep, send, near, f, i, scales = call(
        past_kernel,
        (
            half,
            half,
            *(jax.ShapeDtypeStruct(a.shape, a.dtype) for a in (filt_near, forward, inverse, scales)),
        ),
        [SMEM, SMEM, VMEM] + [HBM] * 6,
        unit * 18,
        2 << 20,
        scratch=[
            pltpu.VMEM(filt_far.shape, BF16),
            pltpu.VMEM(history.shape, BF16),
            pltpu.VMEM((ctx_count // 2, 2, rows, width), F32),
            pltpu.VMEM((3, 2, *spread), F32),
            pltpu.SemaphoreType.DMA((6,)),
        ],
    )(index, last, border, *(in_hbm(a) for a in (filt_far, filt_near, history, forward, inverse, scales)))

    came = swapped(send, "ctx", 1)
    here = added(keep[:fresh], came[:fresh])
    there = swapped(here, "ctx", 2)

    payload, gate_two = call(
        project_kernel,
        (
            jax.ShapeDtypeStruct((ctx_count, 3 * rows, lanes), BF16),
            jax.ShapeDtypeStruct((rows, width), BF16),
        ),
        [VMEM, VMEM, HBM, VMEM, VMEM],
        2 * rows * w_in.size,
        2 * w_in.size,
        scratch=[pltpu.VMEM(w_three.shape, BF16), pltpu.SemaphoreType.DMA((8,))],
    )(gathered, scales, in_hbm(w_three), keep, came)

    here = added(here, there)
    payload, here = lax.optimization_barrier((payload, here))
    there = swapped(here, "ctx", 8)
    arrived = exchanged(payload, "ctx")
    here = added(here, there)
    there = swapped(here, "ctx", 4)
    spectra = call(
        near_kernel,
        jax.ShapeDtypeStruct((2, 2 * fresh, lanes), F32),
        [SMEM, VMEM, VMEM],
        unit * 2,
        2 << 20,
        scratch=[pltpu.VMEM((1, *spread), F32)],
    )(index, near, f)

    block = jax.ShapeDtypeStruct((2, rows, lanes), F32)
    keep, send, w_out = call(
        mix_kernel,
        (block, block, jax.ShapeDtypeStruct(w_out.shape, BF16)),
        [SMEM] + [VMEM] * 6 + [HBM],
        unit * 4,
        4 << 20,
        scratch=[
            pltpu.VMEM((fresh, lanes), BF16),
            pltpu.VMEM((2, 2, rows, lanes), F32),
            pltpu.SemaphoreType.DMA,
        ],
    )(index, arrived, here, there, spectra, f, i, in_hbm(w_out))
    came = swapped(send, "ctx", 1)
    partial, gated = call(
        finish_kernel,
        (
            jax.ShapeDtypeStruct((chan_count, rows, width), BF16),
            jax.ShapeDtypeStruct((rows, width), BF16),
        ),
        [SMEM] + [VMEM] * 4,
        unit,
        1 << 20,
    )(index, keep, came, gate_two, w_out)
    mixed = call(
        total_kernel, jax.ShapeDtypeStruct((rows, width), BF16), [VMEM], 1 << 16, 1 << 17
    )(exchanged(partial, "chan"))
    return (mixed, gated)


def solution(mesh):
    placed = (
        P("ctx", "chan"),
        P(),
        P(None, None, "chan"),
        P("chan", None),
        P("ctx", None, "chan"),
        P("ctx", None, "chan"),
        P(None, None, "chan"),
    )
    return jax.shard_map(
        layer,
        mesh=mesh,
        in_specs=placed,
        out_specs=(P("ctx", "chan"), P("ctx", "chan")),
        check_vma=False,
    )
```

```python
import jax
import jax.numpy as jnp
import numpy as np
from jax import lax
from jax.experimental import pallas as pl
from jax.experimental.pallas import tpu as pltpu
from jax.sharding import PartitionSpec as P

BF16 = jnp.bfloat16
F32 = jnp.float32
VMEM = pl.BlockSpec(memory_space=pltpu.VMEM)
SMEM = pl.BlockSpec(memory_space=pltpu.SMEM)
HBM = pl.BlockSpec(memory_space=pltpu.HBM)
LIMIT = 24 << 20


def split_up(table):
    high = np.asarray(table, np.float32).astype(jnp.bfloat16)
    low = (table - high.astype(np.float64)).astype(np.float32).astype(jnp.bfloat16)
    return np.stack([high, low])


def dft_tables(length):
    order = np.concatenate([np.arange(0, length, 2), np.arange(1, length, 2)])
    theta = np.pi * (order + 0.5) / length
    angle = theta[:, None] * np.arange(length)[None, :]
    forward = np.concatenate([np.cos(angle), np.sin(angle)], 0)
    back = theta[None, :] * (length - 1 - np.arange(length))[:, None]
    inverse = np.concatenate([np.cos(back), -np.sin(back)], 1) / length
    return split_up(forward), split_up(inverse)


def dot(a, b):
    return jnp.dot(a, b, preferred_element_type=F32)


def spectrum(forward, rows):
    return dot(forward[0], rows) + dot(forward[1], rows)


def back_to_time(high, low, product):
    upper = product.astype(BF16)
    lower = (product - upper.astype(F32)).astype(BF16)
    return dot(high, upper) + dot(high, lower) + dot(low, upper)


def times_conjugate(window, signal):
    half = window.shape[0] // 2
    wc, ws = window[:half], window[half:]
    sc, ss = signal[:half], signal[half:]
    return jnp.concatenate([wc * sc + ws * ss, wc * ss - ws * sc], 0)


def spread_out(rows, spread):
    count, kinds, width = rows.shape
    flat = rows[...].reshape(count * kinds, width)
    lanes = spread.shape[2]
    for h in range(width // lanes):
        spread[h] = flat[:, h * lanes : (h + 1) * lanes].astype(F32)


def parted(spread, kinds, which):
    count = spread.shape[1] // kinds
    rows = [spread[h, pl.ds(which, count, stride=kinds), :].astype(BF16) for h in range(spread.shape[0])]
    return jnp.concatenate(rows, 1)


def past_part(own, after, history, f, i):
    half = f.shape[1] // 2
    quarter = half // 2
    first, second = spectrum(f, own), spectrum(f, after)
    bc, bs = second[:half], second[half:]
    window = first + jnp.concatenate([-bs[:quarter], bs[quarter:], bc[:quarter], -bc[quarter:]], 0)
    return back_to_time(i[0], i[1], times_conjugate(window, spectrum(f, history)))


def open_kernel(*refs):
    (inputs, *loads), (copies, *kept), (held, sems) = refs[:7], refs[7:14], refs[14:]
    moves = [pltpu.make_async_copy(a, b, sems.at[n]) for n, (a, b) in enumerate(zip([inputs, *loads], [held, *kept]))]
    for move in moves:
        move.start()
    moves[0].wait()
    count = copies.shape[0]
    sent = [pltpu.make_async_copy(held, copies.at[d], sems.at[len(moves) + d]) for d in range(count)]
    for move in sent:
        move.start()
    for move in moves[1:] + sent:
        move.wait()


def second_past_kernel(index, last, border, own, near, history, f, i, keep, send, later, parts, spread):
    @pl.when(last[0] > 0)
    def _():
        spread_out(near, spread.at[1])

    @pl.when(last[0] == 0)
    def _():
        spread_out(border, spread.at[1])

    spread_out(own, spread.at[0])
    spread_out(history, spread.at[2])
    mine = index[0] % 2
    part = past_part(*(parted(spread.at[n], 2, 1) for n in range(3)), f, i)
    parts[...] = part.reshape(parts.shape)
    half, lanes = keep.shape[0] // 2, keep.shape[1]
    for h in range(2):
        there = pl.ds(h * half, half)
        span = slice(h * lanes, (h + 1) * lanes)
        keep[there] = parts[:, mine, :, span].reshape(half, lanes)
        send[there] = parts[:, 1 - mine, :, span].reshape(half, lanes)
    for n in range(3):
        later[n] = parted(spread.at[n], 2, 0)


def first_past_kernel(index, rows, f, i, keep, send):
    part = past_part(rows[0], rows[1], rows[2], f, i)
    lanes = keep.shape[1]
    low, high = part[:, :lanes], part[:, lanes:]
    mine = index[0] % 2
    keep[...] = jnp.where(mine == 0, low, high)
    send[...] = jnp.where(mine == 0, high, low)


def project_kernel(gathered, gain, w_hbm, keep, came, out, gate_two, w, sems):
    pieces, rows, width = gathered.shape
    steps = sems.shape[0]
    per = pieces // steps
    copies = []
    for q in range(steps):
        span = pl.ds(q * per * width, per * width)
        copies.append(pltpu.make_async_copy(w_hbm.at[:, span, :], w.at[:, span, :], sems.at[q]))
        copies[-1].start()
    lanes = out.shape[2]
    fresh = keep.shape[0]
    pair = (keep[...] + came[...]).astype(BF16)
    for d in range(out.shape[0]):
        start = (d % 2) * (fresh // 2) + (d // 2) * rows
        out[d, 2 * rows :] = pair[start : start + rows]
    total = jnp.zeros((rows, width), F32)
    for s in range(pieces):
        x = gathered[s].astype(F32)
        total += x * x
    mean_sq = jnp.sum(total, axis=1, keepdims=True) / (pieces * width)
    scale = lax.rsqrt(mean_sq + 1e-06)
    sums = [jnp.zeros((rows, width), F32) for _ in range(3)]
    for s in range(pieces):
        if s % per == 0:
            copies[s // per].wait()
        g = jnp.concatenate([gain[2 * s : 2 * s + 1], gain[2 * s + 1 : 2 * s + 2]], 1)
        normed = (gathered[s].astype(F32) * scale * g).astype(BF16)
        for k in range(3):
            sums[k] += dot(normed, w[k, s * width : (s + 1) * width, :])
    gate_two[...] = sums[2].astype(BF16)
    shared = jnp.concatenate([sums[0].astype(BF16), sums[1].astype(BF16)], 0)
    for d in range(out.shape[0]):
        out[d, : 2 * rows] = shared[:, (d % 2) * lanes : (d % 2 + 1) * lanes]


def near_kernel(index, near, f, spectra, spread):
    lanes = spectra.shape[2]
    half = pl.ds(pl.multiple_of((index[0] % 2) * lanes, lanes), lanes)
    spread_out(near.at[:, :, half], spread)
    for which in range(2):
        spectra[which] = spectrum(f, parted(spread, 2, which))


def mix_kernel(index, arrived, here, one, two, three, spectra, f, i, w_hbm, keep, send, w_out, gated_all, sums, sem):
    load = pltpu.make_async_copy(w_hbm, w_out, sem)
    load.start()
    count, packed, lanes = arrived.shape
    rows = packed // 3
    fresh = count * rows
    values = arrived[:, :rows].reshape(fresh, lanes)
    gate_one = arrived[:, rows : 2 * rows].reshape(fresh, lanes).astype(F32)
    past_one = here[...].astype(F32) + one[...].astype(F32) + two[...].astype(F32) + three[...].astype(F32)
    first = back_to_time(i[0], i[1], times_conjugate(spectra[0], spectrum(f, values)))
    gated = (gate_one * (past_one + first)).astype(BF16)
    gated_all[...] = gated
    mine = index[0] % 2
    chip = pl.ds(pl.multiple_of((index[0] - mine) * rows, 2 * rows), 2 * rows)
    second = back_to_time(i[0, chip, :], i[1, chip, :], times_conjugate(spectra[1], spectrum(f, gated)))
    past_two = [arrived[p, 2 * rows :].astype(F32) for p in range(2)]
    for s in range(2, count):
        past_two[s % 2] += arrived[s, 2 * rows :].astype(F32)
    sums[0] = (second + jnp.concatenate(past_two, 0)).reshape(sums.shape[1:])
    sums[1] = gated_all[chip, :].astype(F32).reshape(sums.shape[1:])
    keep[...] = sums[:, mine]
    send[...] = sums[:, 1 - mine]
    load.wait()


def finish_kernel(index, keep, came, gate_two, w_out, partial, gated):
    first = index[0] % 2 == 0
    low, high = jnp.where(first, keep[...], came[...]), jnp.where(first, came[...], keep[...])
    both = jnp.concatenate([low, high], 2)
    gated[...] = both[1].astype(BF16)
    mixed_in = (gate_two[...].astype(F32) * both[0]).astype(BF16)
    width = partial.shape[2]
    for d in range(partial.shape[0]):
        partial[d] = dot(mixed_in, w_out[:, d * width : (d + 1) * width]).astype(BF16)


def total_kernel(arrived, out):
    out[...] = jnp.sum(arrived[...].astype(F32), axis=0).astype(BF16)


def call(kernel, out_shape, in_specs, flops, nbytes, scratch=(), limit=LIMIT, out_specs=None):
    return pl.pallas_call(
        kernel,
        out_shape=out_shape,
        in_specs=in_specs,
        out_specs=out_specs or jax.tree.map(lambda _: VMEM, out_shape),
        scratch_shapes=list(scratch),
        cost_estimate=pl.CostEstimate(flops=flops, bytes_accessed=nbytes, transcendentals=0),
        compiler_params=pltpu.CompilerParams(vmem_limit_bytes=limit),
    )


def in_hbm(array):
    return pltpu.with_memory_space_constraint(array, pltpu.HBM)


def exchanged(array, axis):
    return lax.all_to_all(array, axis, split_axis=0, concat_axis=0, tiled=True)


def swapped(array, axis, step):
    return lax.ppermute(array, axis, [(i, i ^ step) for i in range(lax.axis_size(axis))])


def added(a, b):
    return (a.astype(F32) + b.astype(F32)).astype(BF16)


def layer(inputs, gain, w_in, w_out, history, filt_far, filt_near):
    rows, width = inputs.shape
    fresh = filt_near.shape[0]
    ctx_count = lax.axis_size("ctx")
    chan_count = lax.axis_size("chan")
    ctx_index = lax.axis_index("ctx")
    forward, inverse = [jnp.asarray(t) for t in dft_tables(fresh)]
    index = ctx_index.reshape(1).astype(jnp.int32)
    last = (index == ctx_count - 1).astype(jnp.int32)

    unit = fresh * fresh * 4 * width
    w_three = w_in.transpose(1, 0, 2)
    border = lax.ppermute(filt_far, "ctx", [(i, i - 1) for i in range(1, ctx_count)])
    loads = (filt_far, filt_near, history, forward, inverse, gain.reshape(-1, 128))
    copies, own, near, past, f, i, scales = call(
        open_kernel,
        (
            jax.ShapeDtypeStruct((chan_count, rows, width), BF16),
            *(jax.ShapeDtypeStruct(a.shape, a.dtype) for a in loads),
        ),
        [HBM] * 7,
        1 << 10,
        1 << 21,
        scratch=[pltpu.VMEM((rows, width), BF16), pltpu.SemaphoreType.DMA((7 + chan_count,))],
        out_specs=(pl.BlockSpec(memory_space=pl.ANY), *[VMEM] * 6),
    )(*(in_hbm(a) for a in (inputs, *loads)))
    gathered = exchanged(copies, "chan")

    lanes = width // 2
    half = jax.ShapeDtypeStruct((fresh, lanes), F32)
    spread = (2 * fresh, lanes)
    keep_two, send_two, later = call(
        second_past_kernel,
        (half, half, jax.ShapeDtypeStruct((3, fresh, width), BF16)),
        [SMEM, SMEM] + [VMEM] * 6,
        unit * 9,
        2 << 20,
        scratch=[pltpu.VMEM((ctx_count // 2, 2, rows, width), F32), pltpu.VMEM((3, 2, *spread), F32)],
    )(index, last, border, own, near, past, f, i)
    came_two = swapped(send_two, "ctx", 1)
    keep_one, send_one = call(
        first_past_kernel, (half, half), [SMEM] + [VMEM] * 3, unit * 9, 1 << 20
    )(index, later, f, i)
    came_one = swapped(send_one, "ctx", 1)

    payload, gate_two = call(
        project_kernel,
        (
            jax.ShapeDtypeStruct((ctx_count, 3 * rows, lanes), BF16),
            jax.ShapeDtypeStruct((rows, width), BF16),
        ),
        [VMEM, VMEM, HBM, VMEM, VMEM],
        2 * rows * w_in.size,
        2 * w_in.size,
        scratch=[pltpu.VMEM(w_three.shape, BF16), pltpu.SemaphoreType.DMA((8,))],
    )(gathered, scales, in_hbm(w_three), keep_two, came_two)

    here = added(keep_one, came_one)
    payload, here = lax.optimization_barrier((payload, here))
    there = swapped(here, "ctx", 2)
    arrived = exchanged(payload, "ctx")
    here = added(here, there)
    others = [swapped(here, "ctx", step) for step in (12, 8, 4)]
    spectra = call(
        near_kernel,
        jax.ShapeDtypeStruct((2, 2 * fresh, lanes), F32),
        [SMEM, VMEM, VMEM],
        unit * 2,
        2 << 20,
        scratch=[pltpu.VMEM((1, *spread), F32)],
    )(index, near, f)

    block = jax.ShapeDtypeStruct((2, rows, lanes), F32)
    keep, send, w_out = call(
        mix_kernel,
        (block, block, jax.ShapeDtypeStruct(w_out.shape, BF16)),
        [SMEM] + [VMEM] * 8 + [HBM],
        unit * 4,
        4 << 20,
        scratch=[
            pltpu.VMEM((fresh, lanes), BF16),
            pltpu.VMEM((2, 2, rows, lanes), F32),
            pltpu.SemaphoreType.DMA,
        ],
    )(index, arrived, here, *others, spectra, f, i, in_hbm(w_out))
    came = swapped(send, "ctx", 1)
    partial, gated = call(
        finish_kernel,
        (
            jax.ShapeDtypeStruct((chan_count, rows, width), BF16),
            jax.ShapeDtypeStruct((rows, width), BF16),
        ),
        [SMEM] + [VMEM] * 4,
        unit,
        1 << 20,
    )(index, keep, came, gate_two, w_out)
    mixed = call(
        total_kernel, jax.ShapeDtypeStruct((rows, width), BF16), [VMEM], 1 << 16, 1 << 17
    )(exchanged(partial, "chan"))
    return (mixed, gated)


def solution(mesh):
    placed = (
        P("ctx", "chan"),
        P(),
        P(None, None, "chan"),
        P("chan", None),
        P("ctx", None, "chan"),
        P("ctx", None, "chan"),
        P(None, None, "chan"),
    )
    return jax.shard_map(
        layer,
        mesh=mesh,
        in_specs=placed,
        out_specs=(P("ctx", "chan"), P("ctx", "chan")),
        check_vma=False,
    )
```

```python
import jax
import jax.numpy as jnp
import numpy as np
from jax import lax
from jax.experimental import pallas as pl
from jax.experimental.pallas import tpu as pltpu
from jax.sharding import PartitionSpec as P

BF16 = jnp.bfloat16
F32 = jnp.float32
VMEM = pl.BlockSpec(memory_space=pltpu.VMEM)
SMEM = pl.BlockSpec(memory_space=pltpu.SMEM)
HBM = pl.BlockSpec(memory_space=pltpu.HBM)
LIMIT = 24 << 20


def split_up(table):
    high = np.asarray(table, np.float32).astype(jnp.bfloat16)
    low = (table - high.astype(np.float64)).astype(np.float32).astype(jnp.bfloat16)
    return np.stack([high, low])


def dft_tables(length):
    order = np.concatenate([np.arange(0, length, 2), np.arange(1, length, 2)])
    theta = np.pi * (order + 0.5) / length
    angle = theta[:, None] * np.arange(length)[None, :]
    forward = np.concatenate([np.cos(angle), np.sin(angle)], 0)
    back = theta[None, :] * (length - 1 - np.arange(length))[:, None]
    inverse = np.concatenate([np.cos(back), -np.sin(back)], 1) / length
    return split_up(forward), split_up(inverse)


def dot(a, b):
    return jnp.dot(a, b, preferred_element_type=F32)


def spectrum(forward, rows):
    return dot(forward[0], rows) + dot(forward[1], rows)


def back_to_time(high, low, product):
    upper = product.astype(BF16)
    lower = (product - upper.astype(F32)).astype(BF16)
    return dot(high, upper) + dot(high, lower) + dot(low, upper)


def times_conjugate(window, signal):
    half = window.shape[0] // 2
    wc, ws = window[:half], window[half:]
    sc, ss = signal[:half], signal[half:]
    return jnp.concatenate([wc * sc + ws * ss, wc * ss - ws * sc], 0)


def spread_out(rows, spread):
    count, kinds, width = rows.shape
    flat = rows[...].reshape(count * kinds, width)
    lanes = spread.shape[2]
    for h in range(width // lanes):
        spread[h] = flat[:, h * lanes : (h + 1) * lanes].astype(F32)


def parted(spread, kinds, which):
    count = spread.shape[1] // kinds
    rows = [spread[h, pl.ds(which, count, stride=kinds), :].astype(BF16) for h in range(spread.shape[0])]
    return jnp.concatenate(rows, 1)


def past_part(own, after, history, f, i):
    half = f.shape[1] // 2
    quarter = half // 2
    first, second = spectrum(f, own), spectrum(f, after)
    bc, bs = second[:half], second[half:]
    window = first + jnp.concatenate([-bs[:quarter], bs[quarter:], bc[:quarter], -bc[quarter:]], 0)
    return back_to_time(i[0], i[1], times_conjugate(window, spectrum(f, history)))


def open_kernel(*refs):
    (inputs, *loads), (copies, *kept), (held, sems) = refs[:7], refs[7:14], refs[14:]
    moves = [pltpu.make_async_copy(a, b, sems.at[n]) for n, (a, b) in enumerate(zip([inputs, *loads], [held, *kept]))]
    for move in moves:
        move.start()
    moves[0].wait()
    count = copies.shape[0]
    sent = [pltpu.make_async_copy(held, copies.at[d], sems.at[len(moves) + d]) for d in range(count)]
    for move in sent:
        move.start()
    for move in moves[1:] + sent:
        move.wait()


def first_past_kernel(index, last, border, own, near, history, f, i, keep, send, later, spread):
    @pl.when(last[0] > 0)
    def _():
        spread_out(near, spread.at[1])

    @pl.when(last[0] == 0)
    def _():
        spread_out(border, spread.at[1])

    spread_out(own, spread.at[0])
    spread_out(history, spread.at[2])
    part = past_part(*(parted(spread.at[n], 2, 0) for n in range(3)), f, i)
    lanes = keep.shape[1]
    low, high = part[:, :lanes], part[:, lanes:]
    mine = index[0] % 2
    keep[...] = jnp.where(mine == 0, low, high)
    send[...] = jnp.where(mine == 0, high, low)
    for n in range(3):
        later[n] = parted(spread.at[n], 2, 1)


def second_past_kernel(index, rows, f, i, keep, send, parts):
    mine = index[0] % 2
    parts[...] = past_part(rows[0], rows[1], rows[2], f, i).reshape(parts.shape)
    half, lanes = keep.shape[0] // 2, keep.shape[1]
    for h in range(2):
        there = pl.ds(h * half, half)
        span = slice(h * lanes, (h + 1) * lanes)
        keep[there] = parts[:, mine, :, span].reshape(half, lanes)
        send[there] = parts[:, 1 - mine, :, span].reshape(half, lanes)


def project_kernel(gathered, gain, w_hbm, keep, came, out, gate_two, w, sems):
    pieces, rows, width = gathered.shape
    steps = sems.shape[0]
    per = pieces // steps
    copies = []
    for q in range(steps):
        span = pl.ds(q * per * width, per * width)
        copies.append(pltpu.make_async_copy(w_hbm.at[:, span, :], w.at[:, span, :], sems.at[q]))
        copies[-1].start()
    lanes = out.shape[2]
    fresh = keep.shape[0]
    pair = (keep[...] + came[...]).astype(BF16)
    for d in range(out.shape[0]):
        start = (d % 2) * (fresh // 2) + (d // 2) * rows
        out[d, 2 * rows :] = pair[start : start + rows]
    total = jnp.zeros((rows, width), F32)
    for s in range(pieces):
        x = gathered[s].astype(F32)
        total += x * x
    mean_sq = jnp.sum(total, axis=1, keepdims=True) / (pieces * width)
    scale = lax.rsqrt(mean_sq + 1e-06)
    sums = [jnp.zeros((rows, width), F32) for _ in range(3)]
    for s in range(pieces):
        if s % per == 0:
            copies[s // per].wait()
        g = jnp.concatenate([gain[2 * s : 2 * s + 1], gain[2 * s + 1 : 2 * s + 2]], 1)
        normed = (gathered[s].astype(F32) * scale * g).astype(BF16)
        for k in range(3):
            sums[k] += dot(normed, w[k, s * width : (s + 1) * width, :])
    gate_two[...] = sums[2].astype(BF16)
    shared = jnp.concatenate([sums[0].astype(BF16), sums[1].astype(BF16)], 0)
    for d in range(out.shape[0]):
        out[d, : 2 * rows] = shared[:, (d % 2) * lanes : (d % 2 + 1) * lanes]


def near_kernel(index, near, f, spectra, spread):
    lanes = spectra.shape[2]
    half = pl.ds(pl.multiple_of((index[0] % 2) * lanes, lanes), lanes)
    spread_out(near.at[:, :, half], spread)
    for which in range(2):
        spectra[which] = spectrum(f, parted(spread, 2, which))


def mix_kernel(index, arrived, here, there, spectra, f, i, w_hbm, keep, send, w_out, gated_all, sums, sem):
    load = pltpu.make_async_copy(w_hbm, w_out, sem)
    load.start()
    count, packed, lanes = arrived.shape
    rows = packed // 3
    fresh = count * rows
    values = arrived[:, :rows].reshape(fresh, lanes)
    gate_one = arrived[:, rows : 2 * rows].reshape(fresh, lanes).astype(F32)
    past_one = here[...].astype(F32) + there[...].astype(F32)
    first = back_to_time(i[0], i[1], times_conjugate(spectra[0], spectrum(f, values)))
    gated = (gate_one * (past_one + first)).astype(BF16)
    gated_all[...] = gated
    mine = index[0] % 2
    chip = pl.ds(pl.multiple_of((index[0] - mine) * rows, 2 * rows), 2 * rows)
    second = back_to_time(i[0, chip, :], i[1, chip, :], times_conjugate(spectra[1], spectrum(f, gated)))
    past_two = [arrived[p, 2 * rows :].astype(F32) for p in range(2)]
    for s in range(2, count):
        past_two[s % 2] += arrived[s, 2 * rows :].astype(F32)
    sums[0] = (second + jnp.concatenate(past_two, 0)).reshape(sums.shape[1:])
    sums[1] = gated_all[chip, :].astype(F32).reshape(sums.shape[1:])
    keep[...] = sums[:, mine]
    send[...] = sums[:, 1 - mine]
    load.wait()


def finish_kernel(index, keep, came, gate_two, w_out, partial, gated):
    first = index[0] % 2 == 0
    low, high = jnp.where(first, keep[...], came[...]), jnp.where(first, came[...], keep[...])
    both = jnp.concatenate([low, high], 2)
    gated[...] = both[1].astype(BF16)
    mixed_in = (gate_two[...].astype(F32) * both[0]).astype(BF16)
    width = partial.shape[2]
    for d in range(partial.shape[0]):
        partial[d] = dot(mixed_in, w_out[:, d * width : (d + 1) * width]).astype(BF16)


def total_kernel(arrived, out):
    out[...] = jnp.sum(arrived[...].astype(F32), axis=0).astype(BF16)


def call(kernel, out_shape, in_specs, flops, nbytes, scratch=(), limit=LIMIT, out_specs=None):
    return pl.pallas_call(
        kernel,
        out_shape=out_shape,
        in_specs=in_specs,
        out_specs=out_specs or jax.tree.map(lambda _: VMEM, out_shape),
        scratch_shapes=list(scratch),
        cost_estimate=pl.CostEstimate(flops=flops, bytes_accessed=nbytes, transcendentals=0),
        compiler_params=pltpu.CompilerParams(vmem_limit_bytes=limit),
    )


def in_hbm(array):
    return pltpu.with_memory_space_constraint(array, pltpu.HBM)


def exchanged(array, axis):
    return lax.all_to_all(array, axis, split_axis=0, concat_axis=0, tiled=True)


def swapped(array, axis, step):
    return lax.ppermute(array, axis, [(i, i ^ step) for i in range(lax.axis_size(axis))])


def added(a, b):
    return (a.astype(F32) + b.astype(F32)).astype(BF16)


def layer(inputs, gain, w_in, w_out, history, filt_far, filt_near):
    rows, width = inputs.shape
    fresh = filt_near.shape[0]
    ctx_count = lax.axis_size("ctx")
    chan_count = lax.axis_size("chan")
    ctx_index = lax.axis_index("ctx")
    forward, inverse = [jnp.asarray(t) for t in dft_tables(fresh)]
    index = ctx_index.reshape(1).astype(jnp.int32)
    last = (index == ctx_count - 1).astype(jnp.int32)

    unit = fresh * fresh * 4 * width
    w_three = w_in.transpose(1, 0, 2)
    border = lax.ppermute(filt_far, "ctx", [(i, i - 1) for i in range(1, ctx_count)])
    loads = (filt_far, filt_near, history, forward, inverse, gain.reshape(-1, 128))
    copies, own, near, past, f, i, scales = call(
        open_kernel,
        (
            jax.ShapeDtypeStruct((chan_count, rows, width), BF16),
            *(jax.ShapeDtypeStruct(a.shape, a.dtype) for a in loads),
        ),
        [HBM] * 7,
        1 << 10,
        1 << 21,
        scratch=[pltpu.VMEM((rows, width), BF16), pltpu.SemaphoreType.DMA((7 + chan_count,))],
        out_specs=(pl.BlockSpec(memory_space=pl.ANY), *[VMEM] * 6),
    )(*(in_hbm(a) for a in (inputs, *loads)))
    gathered = exchanged(copies, "chan")

    lanes = width // 2
    half = jax.ShapeDtypeStruct((fresh, lanes), F32)
    spread = (2 * fresh, lanes)
    keep_one, send_one, later = call(
        first_past_kernel,
        (half, half, jax.ShapeDtypeStruct((3, fresh, width), BF16)),
        [SMEM, SMEM] + [VMEM] * 6,
        unit * 9,
        2 << 20,
        scratch=[pltpu.VMEM((3, 2, *spread), F32)],
    )(index, last, border, own, near, past, f, i)
    came_one = swapped(send_one, "ctx", 1)
    keep_two, send_two = call(
        second_past_kernel,
        (half, half),
        [SMEM] + [VMEM] * 3,
        unit * 9,
        1 << 20,
        scratch=[pltpu.VMEM((ctx_count // 2, 2, rows, width), F32)],
    )(index, later, f, i)
    came_two = swapped(send_two, "ctx", 1)
    here = added(keep_one, came_one)
    there = swapped(here, "ctx", 2)

    payload, gate_two = call(
        project_kernel,
        (
            jax.ShapeDtypeStruct((ctx_count, 3 * rows, lanes), BF16),
            jax.ShapeDtypeStruct((rows, width), BF16),
        ),
        [VMEM, VMEM, HBM, VMEM, VMEM],
        2 * rows * w_in.size,
        2 * w_in.size,
        scratch=[pltpu.VMEM(w_three.shape, BF16), pltpu.SemaphoreType.DMA((8,))],
    )(gathered, scales, in_hbm(w_three), keep_two, came_two)

    here = added(here, there)
    payload, here = lax.optimization_barrier((payload, here))
    there = swapped(here, "ctx", 8)
    arrived = exchanged(payload, "ctx")
    here = added(here, there)
    there = swapped(here, "ctx", 4)
    spectra = call(
        near_kernel,
        jax.ShapeDtypeStruct((2, 2 * fresh, lanes), F32),
        [SMEM, VMEM, VMEM],
        unit * 2,
        2 << 20,
        scratch=[pltpu.VMEM((1, *spread), F32)],
    )(index, near, f)

    block = jax.ShapeDtypeStruct((2, rows, lanes), F32)
    keep, send, w_out = call(
        mix_kernel,
        (block, block, jax.ShapeDtypeStruct(w_out.shape, BF16)),
        [SMEM] + [VMEM] * 6 + [HBM],
        unit * 4,
        4 << 20,
        scratch=[
            pltpu.VMEM((fresh, lanes), BF16),
            pltpu.VMEM((2, 2, rows, lanes), F32),
            pltpu.SemaphoreType.DMA,
        ],
    )(index, arrived, here, there, spectra, f, i, in_hbm(w_out))
    came = swapped(send, "ctx", 1)
    partial, gated = call(
        finish_kernel,
        (
            jax.ShapeDtypeStruct((chan_count, rows, width), BF16),
            jax.ShapeDtypeStruct((rows, width), BF16),
        ),
        [SMEM] + [VMEM] * 4,
        unit,
        1 << 20,
    )(index, keep, came, gate_two, w_out)
    mixed = call(
        total_kernel, jax.ShapeDtypeStruct((rows, width), BF16), [VMEM], 1 << 16, 1 << 17
    )(exchanged(partial, "chan"))
    return (mixed, gated)


def solution(mesh):
    placed = (
        P("ctx", "chan"),
        P(),
        P(None, None, "chan"),
        P("chan", None),
        P("ctx", None, "chan"),
        P("ctx", None, "chan"),
        P(None, None, "chan"),
    )
    return jax.shard_map(
        layer,
        mesh=mesh,
        in_specs=placed,
        out_specs=(P("ctx", "chan"), P("ctx", "chan")),
        check_vma=False,
    )
```

```python
import jax
import jax.numpy as jnp
import numpy as np
from jax import lax
from jax.experimental import pallas as pl
from jax.experimental.pallas import tpu as pltpu
from jax.sharding import PartitionSpec as P

BF16 = jnp.bfloat16
F32 = jnp.float32
VMEM = pl.BlockSpec(memory_space=pltpu.VMEM)
SMEM = pl.BlockSpec(memory_space=pltpu.SMEM)
HBM = pl.BlockSpec(memory_space=pltpu.HBM)
LIMIT = 24 << 20


def split_up(table):
    high = np.asarray(table, np.float32).astype(jnp.bfloat16)
    low = (table - high.astype(np.float64)).astype(np.float32).astype(jnp.bfloat16)
    return np.stack([high, low])


def dft_tables(length):
    order = np.concatenate([np.arange(0, length, 2), np.arange(1, length, 2)])
    theta = np.pi * (order + 0.5) / length
    angle = theta[:, None] * np.arange(length)[None, :]
    forward = np.concatenate([np.cos(angle), np.sin(angle)], 0)
    back = theta[None, :] * (length - 1 - np.arange(length))[:, None]
    inverse = np.concatenate([np.cos(back), -np.sin(back)], 1) / length
    return split_up(forward), split_up(inverse)


def dot(a, b):
    return jnp.dot(a, b, preferred_element_type=F32)


def spectrum(forward, rows):
    return dot(forward[0], rows) + dot(forward[1], rows)


def back_to_time(high, low, product):
    upper = product.astype(BF16)
    lower = (product - upper.astype(F32)).astype(BF16)
    return dot(high, upper) + dot(high, lower) + dot(low, upper)


def times_conjugate(window, signal):
    half = window.shape[0] // 2
    wc, ws = window[:half], window[half:]
    sc, ss = signal[:half], signal[half:]
    return jnp.concatenate([wc * sc + ws * ss, wc * ss - ws * sc], 0)


def spread_out(rows, spread):
    count, kinds, width = rows.shape
    flat = rows[...].reshape(count * kinds, width)
    lanes = spread.shape[2]
    for h in range(width // lanes):
        spread[h] = flat[:, h * lanes : (h + 1) * lanes].astype(F32)


def parted(spread, kinds, which):
    count = spread.shape[1] // kinds
    rows = [spread[h, pl.ds(which, count, stride=kinds), :].astype(BF16) for h in range(spread.shape[0])]
    return jnp.concatenate(rows, 1)


def past_part(own, after, history, f, i):
    half = f.shape[1] // 2
    quarter = half // 2
    first, second = spectrum(f, own), spectrum(f, after)
    bc, bs = second[:half], second[half:]
    window = first + jnp.concatenate([-bs[:quarter], bs[quarter:], bc[:quarter], -bc[quarter:]], 0)
    return back_to_time(i[0], i[1], times_conjugate(window, spectrum(f, history)))


def open_kernel(*refs):
    (inputs, *loads), (copies, *kept), (held, sems) = refs[:7], refs[7:14], refs[14:]
    moves = [pltpu.make_async_copy(a, b, sems.at[n]) for n, (a, b) in enumerate(zip([inputs, *loads], [held, *kept]))]
    for move in moves:
        move.start()
    moves[0].wait()
    count = copies.shape[0]
    sent = [pltpu.make_async_copy(held, copies.at[d], sems.at[len(moves) + d]) for d in range(count)]
    for move in sent:
        move.start()
    for move in moves[1:] + sent:
        move.wait()


def first_past_kernel(
    index, last, border, own, near, history, f, i, w_hbm, keep, send, later, w_head, spread, sem
):
    load = pltpu.make_async_copy(w_hbm.at[:, pl.ds(0, w_head.shape[1]), :], w_head, sem)
    load.start()

    @pl.when(last[0] > 0)
    def _():
        spread_out(near, spread.at[1])

    @pl.when(last[0] == 0)
    def _():
        spread_out(border, spread.at[1])

    spread_out(own, spread.at[0])
    spread_out(history, spread.at[2])
    part = past_part(*(parted(spread.at[n], 2, 0) for n in range(3)), f, i)
    lanes = keep.shape[1]
    low, high = part[:, :lanes], part[:, lanes:]
    mine = index[0] % 2
    keep[...] = jnp.where(mine == 0, low, high)
    send[...] = jnp.where(mine == 0, high, low)
    for n in range(3):
        later[n] = parted(spread.at[n], 2, 1)
    load.wait()


def second_past_kernel(index, rows, f, i, keep, send, parts):
    mine = index[0] % 2
    parts[...] = past_part(rows[0], rows[1], rows[2], f, i).reshape(parts.shape)
    half, lanes = keep.shape[0] // 2, keep.shape[1]
    for h in range(2):
        there = pl.ds(h * half, half)
        span = slice(h * lanes, (h + 1) * lanes)
        keep[there] = parts[:, mine, :, span].reshape(half, lanes)
        send[there] = parts[:, 1 - mine, :, span].reshape(half, lanes)


def project_kernel(gathered, gain, w_head, w_hbm, keep, came, out, gate_two, w, sems):
    pieces, rows, width = gathered.shape
    ready = w_head.shape[1] // width
    steps = sems.shape[0]
    per = (pieces - ready) // steps
    copies = []
    for q in range(steps):
        there = pl.ds(q * per * width, per * width)
        here = pl.ds((ready + q * per) * width, per * width)
        copies.append(pltpu.make_async_copy(w_hbm.at[:, here, :], w.at[:, there, :], sems.at[q]))
        copies[-1].start()
    lanes = out.shape[2]
    fresh = keep.shape[0]
    pair = (keep[...] + came[...]).astype(BF16)
    for d in range(out.shape[0]):
        start = (d % 2) * (fresh // 2) + (d // 2) * rows
        out[d, 2 * rows :] = pair[start : start + rows]
    total = jnp.zeros((rows, width), F32)
    for s in range(pieces):
        x = gathered[s].astype(F32)
        total += x * x
    mean_sq = jnp.sum(total, axis=1, keepdims=True) / (pieces * width)
    scale = lax.rsqrt(mean_sq + 1e-06)
    sums = [jnp.zeros((rows, width), F32) for _ in range(3)]
    for s in range(pieces):
        if s >= ready and (s - ready) % per == 0:
            copies[(s - ready) // per].wait()
        block, n = (w_head, s) if s < ready else (w, s - ready)
        g = jnp.concatenate([gain[2 * s : 2 * s + 1], gain[2 * s + 1 : 2 * s + 2]], 1)
        normed = (gathered[s].astype(F32) * scale * g).astype(BF16)
        for k in range(3):
            sums[k] += dot(normed, block[k, n * width : (n + 1) * width, :])
    gate_two[...] = sums[2].astype(BF16)
    shared = jnp.concatenate([sums[0].astype(BF16), sums[1].astype(BF16)], 0)
    for d in range(out.shape[0]):
        out[d, : 2 * rows] = shared[:, (d % 2) * lanes : (d % 2 + 1) * lanes]


def near_kernel(index, near, f, w_hbm, spectra, w_out, spread, sem):
    load = pltpu.make_async_copy(w_hbm.at[:, pl.ds(0, w_out.shape[1])], w_out, sem)
    load.start()
    lanes = spectra.shape[2]
    half = pl.ds(pl.multiple_of((index[0] % 2) * lanes, lanes), lanes)
    spread_out(near.at[:, :, half], spread)
    for which in range(2):
        spectra[which] = spectrum(f, parted(spread, 2, which))
    load.wait()


def mix_kernel(index, arrived, here, there, spectra, f, i, w_hbm, keep, send, w_tail, gated_all, sums, sem):
    start = w_hbm.shape[1] - w_tail.shape[1]
    load = pltpu.make_async_copy(w_hbm.at[:, pl.ds(start, w_tail.shape[1])], w_tail, sem)
    load.start()
    count, packed, lanes = arrived.shape
    rows = packed // 3
    fresh = count * rows
    values = arrived[:, :rows].reshape(fresh, lanes)
    gate_one = arrived[:, rows : 2 * rows].reshape(fresh, lanes).astype(F32)
    past_one = here[...].astype(F32) + there[...].astype(F32)
    first = back_to_time(i[0], i[1], times_conjugate(spectra[0], spectrum(f, values)))
    gated = (gate_one * (past_one + first)).astype(BF16)
    gated_all[...] = gated
    mine = index[0] % 2
    chip = pl.ds(pl.multiple_of((index[0] - mine) * rows, 2 * rows), 2 * rows)
    second = back_to_time(i[0, chip, :], i[1, chip, :], times_conjugate(spectra[1], spectrum(f, gated)))
    past_two = [arrived[p, 2 * rows :].astype(F32) for p in range(2)]
    for s in range(2, count):
        past_two[s % 2] += arrived[s, 2 * rows :].astype(F32)
    sums[0] = (second + jnp.concatenate(past_two, 0)).reshape(sums.shape[1:])
    sums[1] = gated_all[chip, :].astype(F32).reshape(sums.shape[1:])
    keep[...] = sums[:, mine]
    send[...] = sums[:, 1 - mine]
    load.wait()


def finish_kernel(index, keep, came, gate_two, w_head, w_tail, partial, gated):
    first = index[0] % 2 == 0
    low, high = jnp.where(first, keep[...], came[...]), jnp.where(first, came[...], keep[...])
    both = jnp.concatenate([low, high], 2)
    gated[...] = both[1].astype(BF16)
    mixed_in = (gate_two[...].astype(F32) * both[0]).astype(BF16)
    width = partial.shape[2]
    for d in range(partial.shape[0]):
        start = d * width
        block = w_head
        if start >= w_head.shape[1]:
            start, block = start - w_head.shape[1], w_tail
        partial[d] = dot(mixed_in, block[:, start : start + width]).astype(BF16)


def total_kernel(arrived, out):
    out[...] = jnp.sum(arrived[...].astype(F32), axis=0).astype(BF16)


def call(kernel, out_shape, in_specs, flops, nbytes, scratch=(), limit=LIMIT, out_specs=None):
    return pl.pallas_call(
        kernel,
        out_shape=out_shape,
        in_specs=in_specs,
        out_specs=out_specs or jax.tree.map(lambda _: VMEM, out_shape),
        scratch_shapes=list(scratch),
        cost_estimate=pl.CostEstimate(flops=flops, bytes_accessed=nbytes, transcendentals=0),
        compiler_params=pltpu.CompilerParams(vmem_limit_bytes=limit),
    )


def in_hbm(array):
    return pltpu.with_memory_space_constraint(array, pltpu.HBM)


def exchanged(array, axis):
    return lax.all_to_all(array, axis, split_axis=0, concat_axis=0, tiled=True)


def swapped(array, axis, step):
    return lax.ppermute(array, axis, [(i, i ^ step) for i in range(lax.axis_size(axis))])


def added(a, b):
    return (a.astype(F32) + b.astype(F32)).astype(BF16)


def layer(inputs, gain, w_in, w_out, history, filt_far, filt_near):
    rows, width = inputs.shape
    fresh = filt_near.shape[0]
    ctx_count = lax.axis_size("ctx")
    chan_count = lax.axis_size("chan")
    ctx_index = lax.axis_index("ctx")
    forward, inverse = [jnp.asarray(t) for t in dft_tables(fresh)]
    index = ctx_index.reshape(1).astype(jnp.int32)
    last = (index == ctx_count - 1).astype(jnp.int32)

    unit = fresh * fresh * 4 * width
    w_three = w_in.transpose(1, 0, 2)
    border = lax.ppermute(filt_far, "ctx", [(i, i - 1) for i in range(1, ctx_count)])
    loads = (filt_far, filt_near, history, forward, inverse, gain.reshape(-1, 128))
    copies, own, near, past, f, i, scales = call(
        open_kernel,
        (
            jax.ShapeDtypeStruct((chan_count, rows, width), BF16),
            *(jax.ShapeDtypeStruct(a.shape, a.dtype) for a in loads),
        ),
        [HBM] * 7,
        1 << 10,
        1 << 21,
        scratch=[pltpu.VMEM((rows, width), BF16), pltpu.SemaphoreType.DMA((7 + chan_count,))],
        out_specs=(pl.BlockSpec(memory_space=pl.ANY), *[VMEM] * 6),
    )(*(in_hbm(a) for a in (inputs, *loads)))
    gathered = exchanged(copies, "chan")

    lanes = width // 2
    half = jax.ShapeDtypeStruct((fresh, lanes), F32)
    spread = (2 * fresh, lanes)
    head = jax.ShapeDtypeStruct((3, 3 * width, width), BF16)
    keep_one, send_one, later, w_head = call(
        first_past_kernel,
        (half, half, jax.ShapeDtypeStruct((3, fresh, width), BF16), head),
        [SMEM, SMEM] + [VMEM] * 6 + [HBM],
        unit * 9,
        2 << 20,
        scratch=[pltpu.VMEM((3, 2, *spread), F32), pltpu.SemaphoreType.DMA],
    )(index, last, border, own, near, past, f, i, in_hbm(w_three))
    came_one = swapped(send_one, "ctx", 1)
    keep_two, send_two = call(
        second_past_kernel,
        (half, half),
        [SMEM] + [VMEM] * 3,
        unit * 9,
        1 << 20,
        scratch=[pltpu.VMEM((ctx_count // 2, 2, rows, width), F32)],
    )(index, later, f, i)
    came_two = swapped(send_two, "ctx", 1)
    here = added(keep_one, came_one)
    there = swapped(here, "ctx", 2)

    payload, gate_two = call(
        project_kernel,
        (
            jax.ShapeDtypeStruct((ctx_count, 3 * rows, lanes), BF16),
            jax.ShapeDtypeStruct((rows, width), BF16),
        ),
        [VMEM, VMEM, VMEM, HBM, VMEM, VMEM],
        2 * rows * w_in.size,
        2 * w_in.size,
        scratch=[
            pltpu.VMEM((3, w_three.shape[1] - head.shape[1], width), BF16),
            pltpu.SemaphoreType.DMA((chan_count - 3,)),
        ],
    )(gathered, scales, w_head, in_hbm(w_three), keep_two, came_two)

    here = added(here, there)
    payload, here = lax.optimization_barrier((payload, here))
    there = swapped(here, "ctx", 8)
    arrived = exchanged(payload, "ctx")
    here = added(here, there)
    there = swapped(here, "ctx", 4)
    side = jax.ShapeDtypeStruct((width, w_out.shape[1] // 2), BF16)
    spectra, w_head = call(
        near_kernel,
        (jax.ShapeDtypeStruct((2, 2 * fresh, lanes), F32), side),
        [SMEM, VMEM, VMEM, HBM],
        unit * 2,
        2 << 20,
        scratch=[pltpu.VMEM((1, *spread), F32), pltpu.SemaphoreType.DMA],
    )(index, near, f, in_hbm(w_out))

    block = jax.ShapeDtypeStruct((2, rows, lanes), F32)
    keep, send, w_tail = call(
        mix_kernel,
        (block, block, side),
        [SMEM] + [VMEM] * 6 + [HBM],
        unit * 4,
        4 << 20,
        scratch=[
            pltpu.VMEM((fresh, lanes), BF16),
            pltpu.VMEM((2, 2, rows, lanes), F32),
            pltpu.SemaphoreType.DMA,
        ],
    )(index, arrived, here, there, spectra, f, i, in_hbm(w_out))
    came = swapped(send, "ctx", 1)
    partial, gated = call(
        finish_kernel,
        (
            jax.ShapeDtypeStruct((chan_count, rows, width), BF16),
            jax.ShapeDtypeStruct((rows, width), BF16),
        ),
        [SMEM] + [VMEM] * 5,
        unit,
        1 << 20,
    )(index, keep, came, gate_two, w_head, w_tail)
    mixed = call(
        total_kernel, jax.ShapeDtypeStruct((rows, width), BF16), [VMEM], 1 << 16, 1 << 17
    )(exchanged(partial, "chan"))
    return (mixed, gated)


def solution(mesh):
    placed = (
        P("ctx", "chan"),
        P(),
        P(None, None, "chan"),
        P("chan", None),
        P("ctx", None, "chan"),
        P("ctx", None, "chan"),
        P(None, None, "chan"),
    )
    return jax.shard_map(
        layer,
        mesh=mesh,
        in_specs=placed,
        out_specs=(P("ctx", "chan"), P("ctx", "chan")),
        check_vma=False,
    )
```

```python
import jax
import jax.numpy as jnp
import numpy as np
from jax import lax
from jax.experimental import pallas as pl
from jax.experimental.pallas import tpu as pltpu
from jax.sharding import PartitionSpec as P

BF16 = jnp.bfloat16
F32 = jnp.float32
VMEM = pl.BlockSpec(memory_space=pltpu.VMEM)
SMEM = pl.BlockSpec(memory_space=pltpu.SMEM)
HBM = pl.BlockSpec(memory_space=pltpu.HBM)
LIMIT = 24 << 20


def split_up(table):
    high = np.asarray(table, np.float32).astype(jnp.bfloat16)
    low = (table - high.astype(np.float64)).astype(np.float32).astype(jnp.bfloat16)
    return np.stack([high, low])


def dft_tables(length):
    order = np.concatenate([np.arange(0, length, 2), np.arange(1, length, 2)])
    theta = np.pi * (order + 0.5) / length
    angle = theta[:, None] * np.arange(length)[None, :]
    forward = np.concatenate([np.cos(angle), np.sin(angle)], 0)
    back = theta[None, :] * (length - 1 - np.arange(length))[:, None]
    inverse = np.concatenate([np.cos(back), -np.sin(back)], 1) / length
    return split_up(forward), split_up(inverse)


def dot(a, b):
    return jnp.dot(a, b, preferred_element_type=F32)


def spectrum(forward, rows):
    return dot(forward[0], rows) + dot(forward[1], rows)


def back_to_time(high, low, product):
    upper = product.astype(BF16)
    lower = (product - upper.astype(F32)).astype(BF16)
    return dot(high, upper) + dot(high, lower) + dot(low, upper)


def times_conjugate(window, signal):
    half = window.shape[0] // 2
    wc, ws = window[:half], window[half:]
    sc, ss = signal[:half], signal[half:]
    return jnp.concatenate([wc * sc + ws * ss, wc * ss - ws * sc], 0)


def spread_out(rows, spread):
    count, kinds, width = rows.shape
    flat = rows[...].reshape(count * kinds, width)
    lanes = spread.shape[2]
    for h in range(width // lanes):
        spread[h] = flat[:, h * lanes : (h + 1) * lanes].astype(F32)


def parted(spread, kinds, which):
    count = spread.shape[1] // kinds
    rows = [spread[h, pl.ds(which, count, stride=kinds), :].astype(BF16) for h in range(spread.shape[0])]
    return jnp.concatenate(rows, 1)


def past_part(own, after, history, f, i):
    half = f.shape[1] // 2
    quarter = half // 2
    first, second = spectrum(f, own), spectrum(f, after)
    bc, bs = second[:half], second[half:]
    window = first + jnp.concatenate([-bs[:quarter], bs[quarter:], bc[:quarter], -bc[quarter:]], 0)
    return back_to_time(i[0], i[1], times_conjugate(window, spectrum(f, history)))


def open_kernel(inputs, *refs):
    loads, copies, kept, sems = refs[:6], refs[6], refs[7:13], refs[13]
    pairs = [(inputs, copies.at[d]) for d in range(copies.shape[0])] + list(zip(loads, kept))
    moves = [pltpu.make_async_copy(a, b, sems.at[n]) for n, (a, b) in enumerate(pairs)]
    for move in moves:
        move.start()
    for move in moves:
        move.wait()


def first_past_kernel(
    index, last, border, own, near, history, f, i, w_hbm, keep, send, later, w_head, spread, sem
):
    load = pltpu.make_async_copy(w_hbm.at[:, pl.ds(0, w_head.shape[1]), :], w_head, sem)
    load.start()

    @pl.when(last[0] > 0)
    def _():
        spread_out(near, spread.at[1])

    @pl.when(last[0] == 0)
    def _():
        spread_out(border, spread.at[1])

    spread_out(own, spread.at[0])
    spread_out(history, spread.at[2])
    part = past_part(*(parted(spread.at[n], 2, 0) for n in range(3)), f, i)
    lanes = keep.shape[1]
    low, high = part[:, :lanes], part[:, lanes:]
    mine = index[0] % 2
    keep[...] = jnp.where(mine == 0, low, high)
    send[...] = jnp.where(mine == 0, high, low)
    for n in range(3):
        later[n] = parted(spread.at[n], 2, 1)
    load.wait()


def second_past_kernel(index, rows, f, i, keep, send, parts):
    mine = index[0] % 2
    parts[...] = past_part(rows[0], rows[1], rows[2], f, i).reshape(parts.shape)
    half, lanes = keep.shape[0] // 2, keep.shape[1]
    for h in range(2):
        there = pl.ds(h * half, half)
        span = slice(h * lanes, (h + 1) * lanes)
        keep[there] = parts[:, mine, :, span].reshape(half, lanes)
        send[there] = parts[:, 1 - mine, :, span].reshape(half, lanes)


def project_kernel(gathered, gain, w_head, w_hbm, keep, came, out, gate_two, w, sems):
    pieces, rows, width = gathered.shape
    ready = w_head.shape[1] // width
    steps = sems.shape[0]
    per = (pieces - ready) // steps
    copies = []
    for q in range(steps):
        there = pl.ds(q * per * width, per * width)
        here = pl.ds((ready + q * per) * width, per * width)
        copies.append(pltpu.make_async_copy(w_hbm.at[:, here, :], w.at[:, there, :], sems.at[q]))
        copies[-1].start()
    lanes = out.shape[2]
    fresh = keep.shape[0]
    pair = (keep[...] + came[...]).astype(BF16)
    for d in range(out.shape[0]):
        start = (d % 2) * (fresh // 2) + (d // 2) * rows
        out[d, 2 * rows :] = pair[start : start + rows]
    total = jnp.zeros((rows, width), F32)
    for s in range(pieces):
        x = gathered[s].astype(F32)
        total += x * x
    mean_sq = jnp.sum(total, axis=1, keepdims=True) / (pieces * width)
    scale = lax.rsqrt(mean_sq + 1e-06)
    sums = [jnp.zeros((rows, width), F32) for _ in range(3)]
    for s in range(pieces):
        if s >= ready and (s - ready) % per == 0:
            copies[(s - ready) // per].wait()
        block, n = (w_head, s) if s < ready else (w, s - ready)
        g = jnp.concatenate([gain[2 * s : 2 * s + 1], gain[2 * s + 1 : 2 * s + 2]], 1)
        normed = (gathered[s].astype(F32) * scale * g).astype(BF16)
        for k in range(3):
            sums[k] += dot(normed, block[k, n * width : (n + 1) * width, :])
    gate_two[...] = sums[2].astype(BF16)
    shared = jnp.concatenate([sums[0].astype(BF16), sums[1].astype(BF16)], 0)
    for d in range(out.shape[0]):
        out[d, : 2 * rows] = shared[:, (d % 2) * lanes : (d % 2 + 1) * lanes]


def near_kernel(index, near, f, w_hbm, spectra, w_out, spread, sem):
    load = pltpu.make_async_copy(w_hbm.at[:, pl.ds(0, w_out.shape[1])], w_out, sem)
    load.start()
    lanes = spectra.shape[2]
    half = pl.ds(pl.multiple_of((index[0] % 2) * lanes, lanes), lanes)
    spread_out(near.at[:, :, half], spread)
    for which in range(2):
        spectra[which] = spectrum(f, parted(spread, 2, which))
    load.wait()


def mix_kernel(index, arrived, here, there, spectra, f, i, w_hbm, keep, send, w_tail, gated_all, sums, sem):
    start = w_hbm.shape[1] - w_tail.shape[1]
    load = pltpu.make_async_copy(w_hbm.at[:, pl.ds(start, w_tail.shape[1])], w_tail, sem)
    load.start()
    count, packed, lanes = arrived.shape
    rows = packed // 3
    fresh = count * rows
    values = arrived[:, :rows].reshape(fresh, lanes)
    gate_one = arrived[:, rows : 2 * rows].reshape(fresh, lanes).astype(F32)
    past_one = here[...].astype(F32) + there[...].astype(F32)
    first = back_to_time(i[0], i[1], times_conjugate(spectra[0], spectrum(f, values)))
    gated = (gate_one * (past_one + first)).astype(BF16)
    gated_all[...] = gated
    mine = index[0] % 2
    chip = pl.ds(pl.multiple_of((index[0] - mine) * rows, 2 * rows), 2 * rows)
    second = back_to_time(i[0, chip, :], i[1, chip, :], times_conjugate(spectra[1], spectrum(f, gated)))
    past_two = [arrived[p, 2 * rows :].astype(F32) for p in range(2)]
    for s in range(2, count):
        past_two[s % 2] += arrived[s, 2 * rows :].astype(F32)
    sums[0] = (second + jnp.concatenate(past_two, 0)).reshape(sums.shape[1:])
    sums[1] = gated_all[chip, :].astype(F32).reshape(sums.shape[1:])
    keep[...] = sums[:, mine]
    send[...] = sums[:, 1 - mine]
    load.wait()


def finish_kernel(index, keep, came, gate_two, w_head, w_tail, partial, gated):
    first = index[0] % 2 == 0
    low, high = jnp.where(first, keep[...], came[...]), jnp.where(first, came[...], keep[...])
    both = jnp.concatenate([low, high], 2)
    gated[...] = both[1].astype(BF16)
    mixed_in = (gate_two[...].astype(F32) * both[0]).astype(BF16)
    width = partial.shape[2]
    for d in range(partial.shape[0]):
        start = d * width
        block = w_head
        if start >= w_head.shape[1]:
            start, block = start - w_head.shape[1], w_tail
        partial[d] = dot(mixed_in, block[:, start : start + width]).astype(BF16)


def total_kernel(arrived, out):
    out[...] = jnp.sum(arrived[...].astype(F32), axis=0).astype(BF16)


def call(kernel, out_shape, in_specs, flops, nbytes, scratch=(), limit=LIMIT, out_specs=None):
    return pl.pallas_call(
        kernel,
        out_shape=out_shape,
        in_specs=in_specs,
        out_specs=out_specs or jax.tree.map(lambda _: VMEM, out_shape),
        scratch_shapes=list(scratch),
        cost_estimate=pl.CostEstimate(flops=flops, bytes_accessed=nbytes, transcendentals=0),
        compiler_params=pltpu.CompilerParams(vmem_limit_bytes=limit),
    )


def in_hbm(array):
    return pltpu.with_memory_space_constraint(array, pltpu.HBM)


def exchanged(array, axis):
    return lax.all_to_all(array, axis, split_axis=0, concat_axis=0, tiled=True)


def swapped(array, axis, step):
    return lax.ppermute(array, axis, [(i, i ^ step) for i in range(lax.axis_size(axis))])


def added(a, b):
    return (a.astype(F32) + b.astype(F32)).astype(BF16)


def layer(inputs, gain, w_in, w_out, history, filt_far, filt_near):
    rows, width = inputs.shape
    fresh = filt_near.shape[0]
    ctx_count = lax.axis_size("ctx")
    chan_count = lax.axis_size("chan")
    ctx_index = lax.axis_index("ctx")
    forward, inverse = [jnp.asarray(t) for t in dft_tables(fresh)]
    index = ctx_index.reshape(1).astype(jnp.int32)
    last = (index == ctx_count - 1).astype(jnp.int32)

    unit = fresh * fresh * 4 * width
    w_three = w_in.transpose(1, 0, 2)
    border = lax.ppermute(filt_far, "ctx", [(i, i - 1) for i in range(1, ctx_count)])
    loads = (filt_far, filt_near, history, forward, inverse, gain.reshape(-1, 128))
    copies, own, near, past, f, i, scales = call(
        open_kernel,
        (
            jax.ShapeDtypeStruct((chan_count, rows, width), BF16),
            *(jax.ShapeDtypeStruct(a.shape, a.dtype) for a in loads),
        ),
        [HBM] * 7,
        1 << 10,
        1 << 21,
        scratch=[pltpu.SemaphoreType.DMA((6 + chan_count,))],
        out_specs=(pl.BlockSpec(memory_space=pl.ANY), *[VMEM] * 6),
    )(*(in_hbm(a) for a in (inputs, *loads)))
    gathered = exchanged(copies, "chan")

    lanes = width // 2
    half = jax.ShapeDtypeStruct((fresh, lanes), F32)
    spread = (2 * fresh, lanes)
    head = jax.ShapeDtypeStruct((3, 3 * width, width), BF16)
    keep_one, send_one, later, w_head = call(
        first_past_kernel,
        (half, half, jax.ShapeDtypeStruct((3, fresh, width), BF16), head),
        [SMEM, SMEM] + [VMEM] * 6 + [HBM],
        unit * 9,
        2 << 20,
        scratch=[pltpu.VMEM((3, 2, *spread), F32), pltpu.SemaphoreType.DMA],
    )(index, last, border, own, near, past, f, i, in_hbm(w_three))
    came_one = swapped(send_one, "ctx", 1)
    keep_two, send_two = call(
        second_past_kernel,
        (half, half),
        [SMEM] + [VMEM] * 3,
        unit * 9,
        1 << 20,
        scratch=[pltpu.VMEM((ctx_count // 2, 2, rows, width), F32)],
    )(index, later, f, i)
    came_two = swapped(send_two, "ctx", 1)
    here = added(keep_one, came_one)
    there = swapped(here, "ctx", 4)

    payload, gate_two = call(
        project_kernel,
        (
            jax.ShapeDtypeStruct((ctx_count, 3 * rows, lanes), BF16),
            jax.ShapeDtypeStruct((rows, width), BF16),
        ),
        [VMEM, VMEM, VMEM, HBM, VMEM, VMEM],
        2 * rows * w_in.size,
        2 * w_in.size,
        scratch=[
            pltpu.VMEM((3, w_three.shape[1] - head.shape[1], width), BF16),
            pltpu.SemaphoreType.DMA((chan_count - 3,)),
        ],
    )(gathered, scales, w_head, in_hbm(w_three), keep_two, came_two)

    here = added(here, there)
    payload, here = lax.optimization_barrier((payload, here))
    there = swapped(here, "ctx", 2)
    arrived = exchanged(payload, "ctx")
    here = added(here, there)
    there = swapped(here, "ctx", 8)
    side = jax.ShapeDtypeStruct((width, w_out.shape[1] // 2), BF16)
    spectra, w_head = call(
        near_kernel,
        (jax.ShapeDtypeStruct((2, 2 * fresh, lanes), F32), side),
        [SMEM, VMEM, VMEM, HBM],
        unit * 2,
        2 << 20,
        scratch=[pltpu.VMEM((1, *spread), F32), pltpu.SemaphoreType.DMA],
    )(index, near, f, in_hbm(w_out))

    block = jax.ShapeDtypeStruct((2, rows, lanes), F32)
    keep, send, w_tail = call(
        mix_kernel,
        (block, block, side),
        [SMEM] + [VMEM] * 6 + [HBM],
        unit * 4,
        4 << 20,
        scratch=[
            pltpu.VMEM((fresh, lanes), BF16),
            pltpu.VMEM((2, 2, rows, lanes), F32),
            pltpu.SemaphoreType.DMA,
        ],
    )(index, arrived, here, there, spectra, f, i, in_hbm(w_out))
    came = swapped(send, "ctx", 1)
    partial, gated = call(
        finish_kernel,
        (
            jax.ShapeDtypeStruct((chan_count, rows, width), BF16),
            jax.ShapeDtypeStruct((rows, width), BF16),
        ),
        [SMEM] + [VMEM] * 5,
        unit,
        1 << 20,
    )(index, keep, came, gate_two, w_head, w_tail)
    mixed = call(
        total_kernel, jax.ShapeDtypeStruct((rows, width), BF16), [VMEM], 1 << 16, 1 << 17
    )(exchanged(partial, "chan"))
    return (mixed, gated)


def solution(mesh):
    placed = (
        P("ctx", "chan"),
        P(),
        P(None, None, "chan"),
        P("chan", None),
        P("ctx", None, "chan"),
        P("ctx", None, "chan"),
        P(None, None, "chan"),
    )
    return jax.shard_map(
        layer,
        mesh=mesh,
        in_specs=placed,
        out_specs=(P("ctx", "chan"), P("ctx", "chan")),
        check_vma=False,
    )
```

```python
import jax
import jax.numpy as jnp
import numpy as np
from jax import lax
from jax.experimental import pallas as pl
from jax.experimental.pallas import tpu as pltpu
from jax.sharding import PartitionSpec as P

BF16 = jnp.bfloat16
F32 = jnp.float32
VMEM = pl.BlockSpec(memory_space=pltpu.VMEM)
SMEM = pl.BlockSpec(memory_space=pltpu.SMEM)
HBM = pl.BlockSpec(memory_space=pltpu.HBM)
LIMIT = 24 << 20


def split_up(table):
    high = np.asarray(table, np.float32).astype(jnp.bfloat16)
    low = (table - high.astype(np.float64)).astype(np.float32).astype(jnp.bfloat16)
    return np.stack([high, low])


def dft_tables(length):
    order = np.concatenate([np.arange(0, length, 2), np.arange(1, length, 2)])
    theta = np.pi * (order + 0.5) / length
    angle = theta[:, None] * np.arange(length)[None, :]
    forward = np.concatenate([np.cos(angle), np.sin(angle)], 0)
    back = theta[None, :] * (length - 1 - np.arange(length))[:, None]
    inverse = np.concatenate([np.cos(back), -np.sin(back)], 1) / length
    return split_up(forward), split_up(inverse)


def dot(a, b):
    return jnp.dot(a, b, preferred_element_type=F32)


def spectrum(forward, rows):
    return dot(forward[0], rows) + dot(forward[1], rows)


def back_to_time(high, low, product):
    upper = product.astype(BF16)
    lower = (product - upper.astype(F32)).astype(BF16)
    return dot(high, upper) + dot(high, lower) + dot(low, upper)


def near_to_time(high, product):
    upper = product.astype(BF16)
    lower = (product - upper.astype(F32)).astype(BF16)
    lanes = product.shape[1]
    both = dot(high, jnp.concatenate([upper, lower], 1))
    return both[:, :lanes] + both[:, lanes:]


def times_conjugate(window, signal):
    half = window.shape[0] // 2
    wc, ws = window[:half], window[half:]
    sc, ss = signal[:half], signal[half:]
    return jnp.concatenate([wc * sc + ws * ss, wc * ss - ws * sc], 0)


def spread_out(rows, spread):
    count, kinds, width = rows.shape
    flat = rows[...].reshape(count * kinds, width)
    lanes = spread.shape[2]
    for h in range(width // lanes):
        spread[h] = flat[:, h * lanes : (h + 1) * lanes].astype(F32)


def parted(spread, kinds, which):
    count = spread.shape[1] // kinds
    rows = [spread[h, pl.ds(which, count, stride=kinds), :].astype(BF16) for h in range(spread.shape[0])]
    return jnp.concatenate(rows, 1)


def past_part(own, after, history, f, i):
    half = f.shape[1] // 2
    quarter = half // 2
    first, second = spectrum(f, own), spectrum(f, after)
    bc, bs = second[:half], second[half:]
    window = first + jnp.concatenate([-bs[:quarter], bs[quarter:], bc[:quarter], -bc[quarter:]], 0)
    return back_to_time(i[0], i[1], times_conjugate(window, spectrum(f, history)))


def open_kernel(inputs, *refs):
    loads, copies, kept, held, sems = refs[:4], refs[4], refs[5:9], refs[9], refs[10]
    pairs = [(inputs, held), *zip(loads, kept)]
    moves = [pltpu.make_async_copy(a, b, sems.at[n]) for n, (a, b) in enumerate(pairs)]
    for move in moves:
        move.start()
    moves[0].wait()
    count = copies.shape[0]
    sent = [pltpu.make_async_copy(held, copies.at[d], sems.at[len(moves) + d]) for d in range(count)]
    for move in sent:
        move.start()
    for move in moves[1:] + sent:
        move.wait()


def first_past_kernel(
    index, last, border, own, history, f, near_hbm, i_hbm, w_hbm,
    keep, send, later, i, w_head, near, spread, sems,
):
    pairs = [(near_hbm, near), (i_hbm, i), (w_hbm.at[:, pl.ds(0, w_head.shape[1]), :], w_head)]
    loads = [pltpu.make_async_copy(a, b, sems.at[n]) for n, (a, b) in enumerate(pairs)]
    for load in loads:
        load.start()
    spread_out(own, spread.at[0])
    spread_out(history, spread.at[2])
    loads[0].wait()

    @pl.when(last[0] > 0)
    def _():
        spread_out(near, spread.at[1])

    @pl.when(last[0] == 0)
    def _():
        spread_out(border, spread.at[1])

    loads[1].wait()
    part = past_part(*(parted(spread.at[n], 2, 0) for n in range(3)), f, i)
    lanes = keep.shape[1]
    low, high = part[:, :lanes], part[:, lanes:]
    mine = index[0] % 2
    keep[...] = jnp.where(mine == 0, low, high)
    send[...] = jnp.where(mine == 0, high, low)
    for n in range(3):
        later[n] = parted(spread.at[n], 2, 1)
    loads[2].wait()


def second_past_kernel(index, rows, f, i, w_hbm, keep, send, w_next, parts, sem):
    size = w_next.shape[1]
    start = w_hbm.shape[1] - size
    load = pltpu.make_async_copy(w_hbm.at[:, pl.ds(start, size), :], w_next, sem)
    load.start()
    mine = index[0] % 2
    parts[...] = past_part(rows[0], rows[1], rows[2], f, i).reshape(parts.shape)
    half, lanes = keep.shape[0] // 2, keep.shape[1]
    for h in range(2):
        there = pl.ds(h * half, half)
        span = slice(h * lanes, (h + 1) * lanes)
        keep[there] = parts[:, mine, :, span].reshape(half, lanes)
        send[there] = parts[:, 1 - mine, :, span].reshape(half, lanes)
    load.wait()


def project_kernel(gathered, gain, w_head, w_next, w_hbm, keep, came, out, gate_two, w, sems):
    pieces, rows, width = gathered.shape
    ready = w_head.shape[1] // width
    steps = sems.shape[0]
    more = w_next.shape[1] // width
    per = (pieces - ready - more) // steps
    copies = []
    for q in range(steps):
        there = pl.ds(q * per * width, per * width)
        here = pl.ds((ready + q * per) * width, per * width)
        copies.append(pltpu.make_async_copy(w_hbm.at[:, here, :], w.at[:, there, :], sems.at[q]))
        copies[-1].start()
    lanes = out.shape[2]
    fresh = keep.shape[0]
    pair = (keep[...] + came[...]).astype(BF16)
    for d in range(out.shape[0]):
        start = (d % 2) * (fresh // 2) + (d // 2) * rows
        out[d, 2 * rows :] = pair[start : start + rows]
    total = jnp.zeros((rows, width), F32)
    for s in range(pieces):
        x = gathered[s].astype(F32)
        total += x * x
    mean_sq = jnp.sum(total, axis=1, keepdims=True) / (pieces * width)
    scale = lax.rsqrt(mean_sq + 1e-06)
    sums = [jnp.zeros((rows, width), F32) for _ in range(3)]
    streamed = range(ready, pieces - more)
    for s in [*range(ready), *range(pieces - more, pieces), *streamed]:
        block, n = w_head, s
        if s in streamed:
            block, n = w, s - ready
            if n % per == 0:
                copies[n // per].wait()
        elif s >= ready:
            block, n = w_next, s - (pieces - more)
        g = jnp.concatenate([gain[2 * s : 2 * s + 1], gain[2 * s + 1 : 2 * s + 2]], 1)
        normed = (gathered[s].astype(F32) * scale * g).astype(BF16)
        for k in range(3):
            sums[k] += dot(normed, block[k, n * width : (n + 1) * width, :])
    gate_two[...] = sums[2].astype(BF16)
    shared = jnp.concatenate([sums[0].astype(BF16), sums[1].astype(BF16)], 0)
    for d in range(out.shape[0]):
        out[d, : 2 * rows] = shared[:, (d % 2) * lanes : (d % 2 + 1) * lanes]


def near_kernel(index, near_hbm, f, w_hbm, spectra, w_out, near, spread, sems):
    first = pltpu.make_async_copy(near_hbm, near, sems.at[0])
    first.start()
    load = pltpu.make_async_copy(w_hbm.at[:, pl.ds(0, w_out.shape[1])], w_out, sems.at[1])
    load.start()
    first.wait()
    lanes = spectra.shape[2]
    half = pl.ds(pl.multiple_of((index[0] % 2) * lanes, lanes), lanes)
    spread_out(near.at[:, :, half], spread)
    for which in range(2):
        spectra[which] = spectrum(f, parted(spread, 2, which))
    load.wait()


def mix_kernel(index, arrived, here, there, spectra, f, i, w_hbm, keep, send, w_tail, gated_all, sums, sem):
    start = w_hbm.shape[1] - w_tail.shape[1]
    load = pltpu.make_async_copy(w_hbm.at[:, pl.ds(start, w_tail.shape[1])], w_tail, sem)
    load.start()
    count, packed, lanes = arrived.shape
    rows = packed // 3
    fresh = count * rows
    values = arrived[:, :rows].reshape(fresh, lanes)
    gate_one = arrived[:, rows : 2 * rows].reshape(fresh, lanes).astype(F32)
    past_one = here[...].astype(F32) + there[...].astype(F32)
    first = near_to_time(i[0], times_conjugate(spectra[0], dot(f[0], values)))
    gated = (gate_one * (past_one + first)).astype(BF16)
    gated_all[...] = gated
    mine = index[0] % 2
    chip = pl.ds(pl.multiple_of((index[0] - mine) * rows, 2 * rows), 2 * rows)
    second = near_to_time(i[0, chip, :], times_conjugate(spectra[1], dot(f[0], gated)))
    past_two = [arrived[p, 2 * rows :].astype(F32) for p in range(2)]
    for s in range(2, count):
        past_two[s % 2] += arrived[s, 2 * rows :].astype(F32)
    sums[0] = (second + jnp.concatenate(past_two, 0)).reshape(sums.shape[1:])
    sums[1] = gated_all[chip, :].astype(F32).reshape(sums.shape[1:])
    keep[...] = sums[:, mine]
    send[...] = sums[:, 1 - mine]
    load.wait()


def finish_kernel(index, keep, came, gate_two, w_head, w_tail, partial, gated):
    first = index[0] % 2 == 0
    low, high = jnp.where(first, keep[...], came[...]), jnp.where(first, came[...], keep[...])
    both = jnp.concatenate([low, high], 2)
    gated[...] = both[1].astype(BF16)
    mixed_in = (gate_two[...].astype(F32) * both[0]).astype(BF16)
    width = partial.shape[2]
    for d in range(partial.shape[0]):
        start = d * width
        block = w_head
        if start >= w_head.shape[1]:
            start, block = start - w_head.shape[1], w_tail
        partial[d] = dot(mixed_in, block[:, start : start + width]).astype(BF16)


def total_kernel(arrived, out):
    out[...] = jnp.sum(arrived[...].astype(F32), axis=0).astype(BF16)


def call(kernel, out_shape, in_specs, flops, nbytes, scratch=(), limit=LIMIT, out_specs=None):
    return pl.pallas_call(
        kernel,
        out_shape=out_shape,
        in_specs=in_specs,
        out_specs=out_specs or jax.tree.map(lambda _: VMEM, out_shape),
        scratch_shapes=list(scratch),
        cost_estimate=pl.CostEstimate(flops=flops, bytes_accessed=nbytes, transcendentals=0),
        compiler_params=pltpu.CompilerParams(vmem_limit_bytes=limit),
    )


def in_hbm(array):
    return pltpu.with_memory_space_constraint(array, pltpu.HBM)


def exchanged(array, axis):
    return lax.all_to_all(array, axis, split_axis=0, concat_axis=0, tiled=True)


def swapped(array, axis, step):
    return lax.ppermute(array, axis, [(i, i ^ step) for i in range(lax.axis_size(axis))])


def added(a, b):
    return (a.astype(F32) + b.astype(F32)).astype(BF16)


def layer(inputs, gain, w_in, w_out, history, filt_far, filt_near):
    rows, width = inputs.shape
    fresh = filt_near.shape[0]
    ctx_count = lax.axis_size("ctx")
    chan_count = lax.axis_size("chan")
    ctx_index = lax.axis_index("ctx")
    forward, inverse = [jnp.asarray(t) for t in dft_tables(fresh)]
    index = ctx_index.reshape(1).astype(jnp.int32)
    last = (index == ctx_count - 1).astype(jnp.int32)

    unit = fresh * fresh * 4 * width
    w_three = w_in.transpose(1, 0, 2)
    border = lax.ppermute(filt_far, "ctx", [(i, i - 1) for i in range(1, ctx_count)])
    loads = (filt_far, history, forward, gain.reshape(-1, 128))
    copies, own, past, f, scales = call(
        open_kernel,
        (
            jax.ShapeDtypeStruct((chan_count, rows, width), BF16),
            *(jax.ShapeDtypeStruct(a.shape, a.dtype) for a in loads),
        ),
        [HBM] * 5,
        1 << 10,
        1 << 21,
        scratch=[pltpu.VMEM((rows, width), BF16), pltpu.SemaphoreType.DMA((5 + chan_count,))],
        out_specs=(pl.BlockSpec(memory_space=pl.ANY), *[VMEM] * 4),
    )(*(in_hbm(a) for a in (inputs, *loads)))
    gathered = exchanged(copies, "chan")

    lanes = width // 2
    half = jax.ShapeDtypeStruct((fresh, lanes), F32)
    spread = (2 * fresh, lanes)
    head = jax.ShapeDtypeStruct((3, 3 * width, width), BF16)
    keep_one, send_one, later, i, w_head = call(
        first_past_kernel,
        (
            half,
            half,
            jax.ShapeDtypeStruct((3, fresh, width), BF16),
            jax.ShapeDtypeStruct(inverse.shape, inverse.dtype),
            head,
        ),
        [SMEM, SMEM] + [VMEM] * 4 + [HBM] * 3,
        unit * 9,
        2 << 20,
        scratch=[
            pltpu.VMEM(filt_near.shape, BF16),
            pltpu.VMEM((3, 2, *spread), F32),
            pltpu.SemaphoreType.DMA((3,)),
        ],
    )(index, last, border, own, past, f, *(in_hbm(a) for a in (filt_near, inverse, w_three)))
    came_one = swapped(send_one, "ctx", 1)
    next_rows = jax.ShapeDtypeStruct((3, width, width), BF16)
    keep_two, send_two, w_next = call(
        second_past_kernel,
        (half, half, next_rows),
        [SMEM] + [VMEM] * 3 + [HBM],
        unit * 9,
        1 << 20,
        scratch=[pltpu.VMEM((ctx_count // 2, 2, rows, width), F32), pltpu.SemaphoreType.DMA],
    )(index, later, f, i, in_hbm(w_three))
    came_two = swapped(send_two, "ctx", 1)
    here = added(keep_one, came_one)
    there = swapped(here, "ctx", 2)

    payload, gate_two = call(
        project_kernel,
        (
            jax.ShapeDtypeStruct((ctx_count, 3 * rows, lanes), BF16),
            jax.ShapeDtypeStruct((rows, width), BF16),
        ),
        [VMEM] * 4 + [HBM, VMEM, VMEM],
        2 * rows * w_in.size,
        2 * w_in.size,
        scratch=[
            pltpu.VMEM((3, w_three.shape[1] - head.shape[1] - next_rows.shape[1], width), BF16),
            pltpu.SemaphoreType.DMA((chan_count - 4,)),
        ],
    )(gathered, scales, w_head, w_next, in_hbm(w_three), keep_two, came_two)

    here = added(here, there)
    payload, here = lax.optimization_barrier((payload, here))
    there = swapped(here, "ctx", 8)
    arrived = exchanged(payload, "ctx")
    here = added(here, there)
    there = swapped(here, "ctx", 4)
    side = jax.ShapeDtypeStruct((width, w_out.shape[1] // 2), BF16)
    spectra, w_head = call(
        near_kernel,
        (jax.ShapeDtypeStruct((2, 2 * fresh, lanes), F32), side),
        [SMEM, HBM, VMEM, HBM],
        unit * 2,
        2 << 20,
        scratch=[pltpu.VMEM(filt_near.shape, BF16), pltpu.VMEM((1, *spread), F32), pltpu.SemaphoreType.DMA((2,))],
    )(index, in_hbm(filt_near), f, in_hbm(w_out))

    block = jax.ShapeDtypeStruct((2, rows, lanes), F32)
    keep, send, w_tail = call(
        mix_kernel,
        (block, block, side),
        [SMEM] + [VMEM] * 6 + [HBM],
        unit * 4,
        4 << 20,
        scratch=[
            pltpu.VMEM((fresh, lanes), BF16),
            pltpu.VMEM((2, 2, rows, lanes), F32),
            pltpu.SemaphoreType.DMA,
        ],
    )(index, arrived, here, there, spectra, f, i, in_hbm(w_out))
    came = swapped(send, "ctx", 1)
    partial, gated = call(
        finish_kernel,
        (
            jax.ShapeDtypeStruct((chan_count, rows, width), BF16),
            jax.ShapeDtypeStruct((rows, width), BF16),
        ),
        [SMEM] + [VMEM] * 5,
        unit,
        1 << 20,
    )(index, keep, came, gate_two, w_head, w_tail)
    mixed = call(
        total_kernel, jax.ShapeDtypeStruct((rows, width), BF16), [VMEM], 1 << 16, 1 << 17
    )(exchanged(partial, "chan"))
    return (mixed, gated)


def solution(mesh):
    placed = (
        P("ctx", "chan"),
        P(),
        P(None, None, "chan"),
        P("chan", None),
        P("ctx", None, "chan"),
        P("ctx", None, "chan"),
        P(None, None, "chan"),
    )
    return jax.shard_map(
        layer,
        mesh=mesh,
        in_specs=placed,
        out_specs=(P("ctx", "chan"), P("ctx", "chan")),
        check_vma=False,
    )
```

```python
import jax
import jax.numpy as jnp
import numpy as np
from jax import lax
from jax.experimental import pallas as pl
from jax.experimental.pallas import tpu as pltpu
from jax.sharding import PartitionSpec as P

BF16 = jnp.bfloat16
F32 = jnp.float32
VMEM = pl.BlockSpec(memory_space=pltpu.VMEM)
SMEM = pl.BlockSpec(memory_space=pltpu.SMEM)
HBM = pl.BlockSpec(memory_space=pltpu.HBM)
LIMIT = 24 << 20


def split_up(table):
    high = np.asarray(table, np.float32).astype(jnp.bfloat16)
    low = (table - high.astype(np.float64)).astype(np.float32).astype(jnp.bfloat16)
    return np.stack([high, low])


def dft_tables(length):
    order = np.concatenate([np.arange(0, length, 2), np.arange(1, length, 2)])
    theta = np.pi * (order + 0.5) / length
    angle = theta[:, None] * np.arange(length)[None, :]
    forward = np.concatenate([np.cos(angle), np.sin(angle)], 0)
    back = theta[None, :] * (length - 1 - np.arange(length))[:, None]
    inverse = np.concatenate([np.cos(back), -np.sin(back)], 1) / length
    return split_up(forward), split_up(inverse)


def dot(a, b):
    return jnp.dot(a, b, preferred_element_type=F32)


def spectrum(forward, rows):
    return dot(forward[0], rows) + dot(forward[1], rows)


def back_to_time(high, low, product):
    upper = product.astype(BF16)
    lower = (product - upper.astype(F32)).astype(BF16)
    return dot(high, upper) + dot(high, lower) + dot(low, upper)


def near_to_time(high, product):
    upper = product.astype(BF16)
    lower = (product - upper.astype(F32)).astype(BF16)
    lanes = product.shape[1]
    both = dot(high, jnp.concatenate([upper, lower], 1))
    return both[:, :lanes] + both[:, lanes:]


def times_conjugate(window, signal):
    half = window.shape[0] // 2
    wc, ws = window[:half], window[half:]
    sc, ss = signal[:half], signal[half:]
    return jnp.concatenate([wc * sc + ws * ss, wc * ss - ws * sc], 0)


def spread_out(rows, spread):
    count, kinds, width = rows.shape
    flat = rows[...].reshape(count * kinds, width)
    lanes = spread.shape[2]
    for h in range(width // lanes):
        spread[h] = flat[:, h * lanes : (h + 1) * lanes].astype(F32)


def parted(spread, kinds, which):
    count = spread.shape[1] // kinds
    rows = [spread[h, pl.ds(which, count, stride=kinds), :].astype(BF16) for h in range(spread.shape[0])]
    return jnp.concatenate(rows, 1)


def past_part(own, after, history, f, i):
    half = f.shape[1] // 2
    quarter = half // 2
    first, second = spectrum(f, own), spectrum(f, after)
    bc, bs = second[:half], second[half:]
    window = first + jnp.concatenate([-bs[:quarter], bs[quarter:], bc[:quarter], -bc[quarter:]], 0)
    return back_to_time(i[0], i[1], times_conjugate(window, spectrum(f, history)))


def open_kernel(*refs):
    (inputs, *loads), (copies, *kept), (held, sems) = refs[:7], refs[7:14], refs[14:]
    moves = [pltpu.make_async_copy(a, b, sems.at[n]) for n, (a, b) in enumerate(zip([inputs, *loads], [held, *kept]))]
    for move in moves:
        move.start()
    moves[0].wait()
    count = copies.shape[0]
    sent = [pltpu.make_async_copy(held, copies.at[d], sems.at[len(moves) + d]) for d in range(count)]
    for move in sent:
        move.start()
    for move in moves[1:] + sent:
        move.wait()


def first_past_kernel(
    index, last, border, own, near, history, f, i, w_hbm, keep, send, later, w_head, spread, sem
):
    load = pltpu.make_async_copy(w_hbm.at[0, pl.ds(0, w_head.shape[0]), :], w_head, sem)
    load.start()

    @pl.when(last[0] > 0)
    def _():
        spread_out(near, spread.at[1])

    @pl.when(last[0] == 0)
    def _():
        spread_out(border, spread.at[1])

    spread_out(own, spread.at[0])
    spread_out(history, spread.at[2])
    part = past_part(*(parted(spread.at[n], 2, 0) for n in range(3)), f, i)
    lanes = keep.shape[1]
    low, high = part[:, :lanes], part[:, lanes:]
    mine = index[0] % 2
    keep[...] = jnp.where(mine == 0, low, high)
    send[...] = jnp.where(mine == 0, high, low)
    for n in range(3):
        later[n] = parted(spread.at[n], 2, 1)
    load.wait()


def second_past_kernel(index, rows, f, i, keep, send, parts):
    mine = index[0] % 2
    parts[...] = past_part(rows[0], rows[1], rows[2], f, i).reshape(parts.shape)
    half, lanes = keep.shape[0] // 2, keep.shape[1]
    for h in range(2):
        there = pl.ds(h * half, half)
        span = slice(h * lanes, (h + 1) * lanes)
        keep[there] = parts[:, mine, :, span].reshape(half, lanes)
        send[there] = parts[:, 1 - mine, :, span].reshape(half, lanes)


def project_kernel(gathered, gain, w_head, w_hbm, keep, came, out_hbm, gate_two, out, normed, w, sems, done):
    pieces, rows, width = gathered.shape
    depth = pieces * width
    ready = w_head.shape[0]
    step = depth // 4
    chunks = []
    for k in range(3):
        edges = [*range(ready, depth, step), depth] if k == 0 else range(0, depth + 1, step)
        chunks += [(k, a, b) for a, b in zip(edges, edges[1:])]
    copies = []
    for n, (k, a, b) in enumerate(chunks):
        span = pl.ds(a, b - a)
        copies.append(pltpu.make_async_copy(w_hbm.at[k, span, :], w.at[k, span, :], sems.at[n]))
        copies[-1].start()
    lanes = out.shape[2]
    fresh = keep.shape[0]
    pair = (keep[...] + came[...]).astype(BF16)
    for d in range(out.shape[0]):
        start = (d % 2) * (fresh // 2) + (d // 2) * rows
        out[d, 2 * rows :] = pair[start : start + rows]
    total = jnp.zeros((rows, width), F32)
    for s in range(pieces):
        x = gathered[s].astype(F32)
        total += x * x
    mean_sq = jnp.sum(total, axis=1, keepdims=True) / depth
    scale = lax.rsqrt(mean_sq + 1e-06)
    for s in range(pieces):
        g = jnp.concatenate([gain[2 * s : 2 * s + 1], gain[2 * s + 1 : 2 * s + 2]], 1)
        normed[:, s * width : (s + 1) * width] = (gathered[s].astype(F32) * scale * g).astype(BF16)
    sums = [dot(normed[:, :ready], w_head[...]), jnp.zeros((rows, width), F32), jnp.zeros((rows, width), F32)]
    sent = pltpu.make_async_copy(out, out_hbm, done)
    for n, (k, a, b) in enumerate(chunks):
        copies[n].wait()
        sums[k] += dot(normed[:, a:b], w[k, a:b, :])
        if k < 2 and b == depth:
            part = sums[k].astype(BF16)
            for d in range(out.shape[0]):
                out[d, k * rows : (k + 1) * rows] = part[:, (d % 2) * lanes : (d % 2 + 1) * lanes]
            if k == 1:
                sent.start()
    gate_two[...] = sums[2].astype(BF16)
    sent.wait()


def near_kernel(index, near, f, w_hbm, spectra, w_out, spread, sem):
    load = pltpu.make_async_copy(w_hbm.at[:, pl.ds(0, w_out.shape[1])], w_out, sem)
    load.start()
    lanes = spectra.shape[2]
    half = pl.ds(pl.multiple_of((index[0] % 2) * lanes, lanes), lanes)
    spread_out(near.at[:, :, half], spread)
    for which in range(2):
        spectra[which] = spectrum(f, parted(spread, 2, which))
    load.wait()


def mix_kernel(index, arrived, here, there, spectra, f, i, w_hbm, keep, send, w_tail, gated_all, sums, sem):
    start = w_hbm.shape[1] - w_tail.shape[1]
    load = pltpu.make_async_copy(w_hbm.at[:, pl.ds(start, w_tail.shape[1])], w_tail, sem)
    load.start()
    count, packed, lanes = arrived.shape
    rows = packed // 3
    fresh = count * rows
    values = arrived[:, :rows].reshape(fresh, lanes)
    gate_one = arrived[:, rows : 2 * rows].reshape(fresh, lanes).astype(F32)
    past_one = here[...].astype(F32) + there[...].astype(F32)
    first = near_to_time(i[0], times_conjugate(spectra[0], dot(f[0], values)))
    gated = (gate_one * (past_one + first)).astype(BF16)
    gated_all[...] = gated
    mine = index[0] % 2
    chip = pl.ds(pl.multiple_of((index[0] - mine) * rows, 2 * rows), 2 * rows)
    second = near_to_time(i[0, chip, :], times_conjugate(spectra[1], dot(f[0], gated)))
    past_two = [arrived[p, 2 * rows :].astype(F32) for p in range(2)]
    for s in range(2, count):
        past_two[s % 2] += arrived[s, 2 * rows :].astype(F32)
    sums[0] = (second + jnp.concatenate(past_two, 0)).reshape(sums.shape[1:])
    sums[1] = gated_all[chip, :].astype(F32).reshape(sums.shape[1:])
    keep[...] = sums[:, mine]
    send[...] = sums[:, 1 - mine]
    load.wait()


def finish_kernel(index, keep, came, gate_two, w_head, w_tail, partial, gated):
    first = index[0] % 2 == 0
    low, high = jnp.where(first, keep[...], came[...]), jnp.where(first, came[...], keep[...])
    both = jnp.concatenate([low, high], 2)
    gated[...] = both[1].astype(BF16)
    mixed_in = (gate_two[...].astype(F32) * both[0]).astype(BF16)
    width = partial.shape[2]
    for d in range(partial.shape[0]):
        start = d * width
        block = w_head
        if start >= w_head.shape[1]:
            start, block = start - w_head.shape[1], w_tail
        partial[d] = dot(mixed_in, block[:, start : start + width]).astype(BF16)


def total_kernel(arrived, out):
    out[...] = jnp.sum(arrived[...].astype(F32), axis=0).astype(BF16)


def call(kernel, out_shape, in_specs, flops, nbytes, scratch=(), limit=LIMIT, out_specs=None):
    return pl.pallas_call(
        kernel,
        out_shape=out_shape,
        in_specs=in_specs,
        out_specs=out_specs or jax.tree.map(lambda _: VMEM, out_shape),
        scratch_shapes=list(scratch),
        cost_estimate=pl.CostEstimate(flops=flops, bytes_accessed=nbytes, transcendentals=0),
        compiler_params=pltpu.CompilerParams(vmem_limit_bytes=limit),
    )


def in_hbm(array):
    return pltpu.with_memory_space_constraint(array, pltpu.HBM)


def exchanged(array, axis):
    return lax.all_to_all(array, axis, split_axis=0, concat_axis=0, tiled=True)


def swapped(array, axis, step):
    return lax.ppermute(array, axis, [(i, i ^ step) for i in range(lax.axis_size(axis))])


def added(a, b):
    return (a.astype(F32) + b.astype(F32)).astype(BF16)


def layer(inputs, gain, w_in, w_out, history, filt_far, filt_near):
    rows, width = inputs.shape
    fresh = filt_near.shape[0]
    ctx_count = lax.axis_size("ctx")
    chan_count = lax.axis_size("chan")
    ctx_index = lax.axis_index("ctx")
    forward, inverse = [jnp.asarray(t) for t in dft_tables(fresh)]
    index = ctx_index.reshape(1).astype(jnp.int32)
    last = (index == ctx_count - 1).astype(jnp.int32)

    unit = fresh * fresh * 4 * width
    w_three = w_in.transpose(1, 0, 2)
    border = lax.ppermute(filt_far, "ctx", [(i, i - 1) for i in range(1, ctx_count)])
    loads = (filt_far, filt_near, history, forward, inverse, gain.reshape(-1, 128))
    copies, own, near, past, f, i, scales = call(
        open_kernel,
        (
            jax.ShapeDtypeStruct((chan_count, rows, width), BF16),
            *(jax.ShapeDtypeStruct(a.shape, a.dtype) for a in loads),
        ),
        [HBM] * 7,
        1 << 10,
        1 << 21,
        scratch=[pltpu.VMEM((rows, width), BF16), pltpu.SemaphoreType.DMA((7 + chan_count,))],
        out_specs=(pl.BlockSpec(memory_space=pl.ANY), *[VMEM] * 6),
    )(*(in_hbm(a) for a in (inputs, *loads)))
    gathered = exchanged(copies, "chan")

    lanes = width // 2
    half = jax.ShapeDtypeStruct((fresh, lanes), F32)
    spread = (2 * fresh, lanes)
    head = jax.ShapeDtypeStruct((9 * width, width), BF16)
    keep_one, send_one, later, w_head = call(
        first_past_kernel,
        (half, half, jax.ShapeDtypeStruct((3, fresh, width), BF16), head),
        [SMEM, SMEM] + [VMEM] * 6 + [HBM],
        unit * 9,
        2 << 20,
        scratch=[pltpu.VMEM((3, 2, *spread), F32), pltpu.SemaphoreType.DMA],
    )(index, last, border, own, near, past, f, i, in_hbm(w_three))
    came_one = swapped(send_one, "ctx", 1)
    keep_two, send_two = call(
        second_past_kernel,
        (half, half),
        [SMEM] + [VMEM] * 3,
        unit * 9,
        1 << 20,
        scratch=[pltpu.VMEM((ctx_count // 2, 2, rows, width), F32)],
    )(index, later, f, i)
    came_two = swapped(send_two, "ctx", 1)
    here = added(keep_one, came_one)
    there = swapped(here, "ctx", 2)

    payload, gate_two = call(
        project_kernel,
        (
            jax.ShapeDtypeStruct((ctx_count, 3 * rows, lanes), BF16),
            jax.ShapeDtypeStruct((rows, width), BF16),
        ),
        [VMEM, VMEM, VMEM, HBM, VMEM, VMEM],
        2 * rows * w_in.size,
        2 * w_in.size,
        scratch=[
            pltpu.VMEM((ctx_count, 3 * rows, lanes), BF16),
            pltpu.VMEM((rows, w_in.shape[0]), BF16),
            pltpu.VMEM(w_three.shape, BF16),
            pltpu.SemaphoreType.DMA((10,)),
            pltpu.SemaphoreType.DMA,
        ],
        out_specs=(pl.BlockSpec(memory_space=pl.ANY), VMEM),
    )(gathered, scales, w_head, in_hbm(w_three), keep_two, came_two)

    here = added(here, there)
    payload, here = lax.optimization_barrier((payload, here))
    there = swapped(here, "ctx", 8)
    arrived = exchanged(payload, "ctx")
    here = added(here, there)
    there = swapped(here, "ctx", 4)
    side = jax.ShapeDtypeStruct((width, w_out.shape[1] // 2), BF16)
    spectra, w_head = call(
        near_kernel,
        (jax.ShapeDtypeStruct((2, 2 * fresh, lanes), F32), side),
        [SMEM, VMEM, VMEM, HBM],
        unit * 2,
        2 << 20,
        scratch=[pltpu.VMEM((1, *spread), F32), pltpu.SemaphoreType.DMA],
    )(index, near, f, in_hbm(w_out))

    block = jax.ShapeDtypeStruct((2, rows, lanes), F32)
    keep, send, w_tail = call(
        mix_kernel,
        (block, block, side),
        [SMEM] + [VMEM] * 6 + [HBM],
        unit * 4,
        4 << 20,
        scratch=[
            pltpu.VMEM((fresh, lanes), BF16),
            pltpu.VMEM((2, 2, rows, lanes), F32),
            pltpu.SemaphoreType.DMA,
        ],
    )(index, arrived, here, there, spectra, f, i, in_hbm(w_out))
    came = swapped(send, "ctx", 1)
    partial, gated = call(
        finish_kernel,
        (
            jax.ShapeDtypeStruct((chan_count, rows, width), BF16),
            jax.ShapeDtypeStruct((rows, width), BF16),
        ),
        [SMEM] + [VMEM] * 5,
        unit,
        1 << 20,
    )(index, keep, came, gate_two, w_head, w_tail)
    mixed = call(
        total_kernel, jax.ShapeDtypeStruct((rows, width), BF16), [VMEM], 1 << 16, 1 << 17
    )(exchanged(partial, "chan"))
    return (mixed, gated)


def solution(mesh):
    placed = (
        P("ctx", "chan"),
        P(),
        P(None, None, "chan"),
        P("chan", None),
        P("ctx", None, "chan"),
        P("ctx", None, "chan"),
        P(None, None, "chan"),
    )
    return jax.shard_map(
        layer,
        mesh=mesh,
        in_specs=placed,
        out_specs=(P("ctx", "chan"), P("ctx", "chan")),
        check_vma=False,
    )
```

```python
import jax
import jax.numpy as jnp
import numpy as np
from jax import lax
from jax.experimental import pallas as pl
from jax.experimental.pallas import tpu as pltpu
from jax.sharding import PartitionSpec as P

BF16 = jnp.bfloat16
F32 = jnp.float32
VMEM = pl.BlockSpec(memory_space=pltpu.VMEM)
SMEM = pl.BlockSpec(memory_space=pltpu.SMEM)
HBM = pl.BlockSpec(memory_space=pltpu.HBM)
LIMIT = 24 << 20


def split_up(table):
    high = np.asarray(table, np.float32).astype(jnp.bfloat16)
    low = (table - high.astype(np.float64)).astype(np.float32).astype(jnp.bfloat16)
    return np.stack([high, low])


def dft_tables(length):
    order = np.concatenate([np.arange(0, length, 2), np.arange(1, length, 2)])
    theta = np.pi * (order + 0.5) / length
    angle = theta[:, None] * np.arange(length)[None, :]
    forward = np.concatenate([np.cos(angle), np.sin(angle)], 0)
    back = theta[None, :] * (length - 1 - np.arange(length))[:, None]
    inverse = np.concatenate([np.cos(back), -np.sin(back)], 1) / length
    return split_up(forward), split_up(inverse)


def dot(a, b):
    return jnp.dot(a, b, preferred_element_type=F32)


def spectrum(forward, rows):
    return dot(forward[0], rows) + dot(forward[1], rows)


def back_to_time(high, low, product):
    upper = product.astype(BF16)
    lower = (product - upper.astype(F32)).astype(BF16)
    return dot(high, upper) + dot(high, lower) + dot(low, upper)


def near_to_time(high, product):
    upper = product.astype(BF16)
    lower = (product - upper.astype(F32)).astype(BF16)
    lanes = product.shape[1]
    both = dot(high, jnp.concatenate([upper, lower], 1))
    return both[:, :lanes] + both[:, lanes:]


def times_conjugate(window, signal):
    half = window.shape[0] // 2
    wc, ws = window[:half], window[half:]
    sc, ss = signal[:half], signal[half:]
    return jnp.concatenate([wc * sc + ws * ss, wc * ss - ws * sc], 0)


def spread_out(rows, spread):
    count, kinds, width = rows.shape
    flat = rows[...].reshape(count * kinds, width)
    lanes = spread.shape[2]
    for h in range(width // lanes):
        spread[h] = flat[:, h * lanes : (h + 1) * lanes].astype(F32)


def parted(spread, kinds, which):
    count = spread.shape[1] // kinds
    rows = [spread[h, pl.ds(which, count, stride=kinds), :].astype(BF16) for h in range(spread.shape[0])]
    return jnp.concatenate(rows, 1)


def past_part(own, after, history, f, i):
    half = f.shape[1] // 2
    quarter = half // 2
    first, second = spectrum(f, own), spectrum(f, after)
    bc, bs = second[:half], second[half:]
    window = first + jnp.concatenate([-bs[:quarter], bs[quarter:], bc[:quarter], -bc[quarter:]], 0)
    return back_to_time(i[0], i[1], times_conjugate(window, spectrum(f, history)))


def open_kernel(*refs):
    (inputs, *loads), (copies, *kept), (held, sems) = refs[:7], refs[7:14], refs[14:]
    moves = [pltpu.make_async_copy(a, b, sems.at[n]) for n, (a, b) in enumerate(zip([inputs, *loads], [held, *kept]))]
    for move in moves:
        move.start()
    moves[0].wait()
    count = copies.shape[0]
    sent = [pltpu.make_async_copy(held, copies.at[d], sems.at[len(moves) + d]) for d in range(count)]
    for move in sent:
        move.start()
    for move in moves[1:] + sent:
        move.wait()


def first_past_kernel(
    index, last, border, own, near, history, f, i, w_hbm, keep, send, later, w_head, spread, sem
):
    load = pltpu.make_async_copy(w_hbm.at[0, pl.ds(0, w_head.shape[0]), :], w_head, sem)
    load.start()

    @pl.when(last[0] > 0)
    def _():
        spread_out(near, spread.at[1])

    @pl.when(last[0] == 0)
    def _():
        spread_out(border, spread.at[1])

    spread_out(own, spread.at[0])
    spread_out(history, spread.at[2])
    part = past_part(*(parted(spread.at[n], 2, 0) for n in range(3)), f, i)
    lanes = keep.shape[1]
    low, high = part[:, :lanes], part[:, lanes:]
    mine = index[0] % 2
    keep[...] = jnp.where(mine == 0, low, high)
    send[...] = jnp.where(mine == 0, high, low)
    for n in range(3):
        later[n] = parted(spread.at[n], 2, 1)
    load.wait()


def second_past_kernel(index, rows, f, i, keep, send, parts):
    mine = index[0] % 2
    parts[...] = past_part(rows[0], rows[1], rows[2], f, i).reshape(parts.shape)
    half, lanes = keep.shape[0] // 2, keep.shape[1]
    for h in range(2):
        there = pl.ds(h * half, half)
        span = slice(h * lanes, (h + 1) * lanes)
        keep[there] = parts[:, mine, :, span].reshape(half, lanes)
        send[there] = parts[:, 1 - mine, :, span].reshape(half, lanes)


def project_kernel(gathered, gain, w_head, w_hbm, keep, came, out_hbm, gate_two, out, normed, w, sems, done):
    pieces, rows, width = gathered.shape
    depth = pieces * width
    ready = w_head.shape[0]
    step = depth // 4
    chunks = []
    for k in range(3):
        edges = [*range(ready, depth, step), depth] if k == 0 else range(0, depth + 1, step)
        chunks += [(k, a, b) for a, b in zip(edges, edges[1:])]
    copies = []
    for n, (k, a, b) in enumerate(chunks):
        span = pl.ds(a, b - a)
        copies.append(pltpu.make_async_copy(w_hbm.at[k, span, :], w.at[k, span, :], sems.at[n]))
        copies[-1].start()
    lanes = out.shape[2]
    fresh = keep.shape[0]
    pair = (keep[...] + came[...]).astype(BF16)
    for d in range(out.shape[0]):
        start = (d % 2) * (fresh // 2) + (d // 2) * rows
        out[d, 2 * rows :] = pair[start : start + rows]
    total = jnp.zeros((rows, width), F32)
    for s in range(pieces):
        x = gathered[s].astype(F32)
        total += x * x
    mean_sq = jnp.sum(total, axis=1, keepdims=True) / depth
    scale = lax.rsqrt(mean_sq + 1e-06)
    for s in range(pieces):
        g = jnp.concatenate([gain[2 * s : 2 * s + 1], gain[2 * s + 1 : 2 * s + 2]], 1)
        normed[:, s * width : (s + 1) * width] = (gathered[s].astype(F32) * scale * g).astype(BF16)
    sums = [dot(normed[:, :ready], w_head[...]), jnp.zeros((rows, width), F32), jnp.zeros((rows, width), F32)]
    sent = pltpu.make_async_copy(out, out_hbm, done)
    for n, (k, a, b) in enumerate(chunks):
        copies[n].wait()
        sums[k] += dot(normed[:, a:b], w[k, a:b, :])
        if k < 2 and b == depth:
            part = sums[k].astype(BF16)
            for d in range(out.shape[0]):
                out[d, k * rows : (k + 1) * rows] = part[:, (d % 2) * lanes : (d % 2 + 1) * lanes]
            if k == 1:
                sent.start()
    gate_two[...] = sums[2].astype(BF16)
    sent.wait()


def near_kernel(index, near, f, w_hbm, spectra, w_out, spread, sem):
    load = pltpu.make_async_copy(w_hbm.at[:, pl.ds(0, w_out.shape[1])], w_out, sem)
    load.start()
    lanes = spectra.shape[2]
    half = pl.ds(pl.multiple_of((index[0] % 2) * lanes, lanes), lanes)
    spread_out(near.at[:, :, half], spread)
    for which in range(2):
        spectra[which] = spectrum(f, parted(spread, 2, which))
    load.wait()


def mix_kernel(index, arrived, here, one, two, three, spectra, f, i, w_hbm, keep, send, w_tail, gated_all, sums, sem):
    start = w_hbm.shape[1] - w_tail.shape[1]
    load = pltpu.make_async_copy(w_hbm.at[:, pl.ds(start, w_tail.shape[1])], w_tail, sem)
    load.start()
    count, packed, lanes = arrived.shape
    rows = packed // 3
    fresh = count * rows
    values = arrived[:, :rows].reshape(fresh, lanes)
    gate_one = arrived[:, rows : 2 * rows].reshape(fresh, lanes).astype(F32)
    past_one = here[...].astype(F32) + one[...].astype(F32) + two[...].astype(F32) + three[...].astype(F32)
    first = near_to_time(i[0], times_conjugate(spectra[0], dot(f[0], values)))
    gated = (gate_one * (past_one + first)).astype(BF16)
    gated_all[...] = gated
    mine = index[0] % 2
    chip = pl.ds(pl.multiple_of((index[0] - mine) * rows, 2 * rows), 2 * rows)
    second = near_to_time(i[0, chip, :], times_conjugate(spectra[1], dot(f[0], gated)))
    past_two = [arrived[p, 2 * rows :].astype(F32) for p in range(2)]
    for s in range(2, count):
        past_two[s % 2] += arrived[s, 2 * rows :].astype(F32)
    sums[0] = (second + jnp.concatenate(past_two, 0)).reshape(sums.shape[1:])
    sums[1] = gated_all[chip, :].astype(F32).reshape(sums.shape[1:])
    keep[...] = sums[:, mine]
    send[...] = sums[:, 1 - mine]
    load.wait()


def finish_kernel(index, keep, came, gate_two, w_head, w_tail, partial, gated):
    first = index[0] % 2 == 0
    low, high = jnp.where(first, keep[...], came[...]), jnp.where(first, came[...], keep[...])
    both = jnp.concatenate([low, high], 2)
    gated[...] = both[1].astype(BF16)
    mixed_in = (gate_two[...].astype(F32) * both[0]).astype(BF16)
    width = partial.shape[2]
    for d in range(partial.shape[0]):
        start = d * width
        block = w_head
        if start >= w_head.shape[1]:
            start, block = start - w_head.shape[1], w_tail
        partial[d] = dot(mixed_in, block[:, start : start + width]).astype(BF16)


def total_kernel(arrived, out):
    out[...] = jnp.sum(arrived[...].astype(F32), axis=0).astype(BF16)


def call(kernel, out_shape, in_specs, flops, nbytes, scratch=(), limit=LIMIT, out_specs=None):
    return pl.pallas_call(
        kernel,
        out_shape=out_shape,
        in_specs=in_specs,
        out_specs=out_specs or jax.tree.map(lambda _: VMEM, out_shape),
        scratch_shapes=list(scratch),
        cost_estimate=pl.CostEstimate(flops=flops, bytes_accessed=nbytes, transcendentals=0),
        compiler_params=pltpu.CompilerParams(vmem_limit_bytes=limit),
    )


def in_hbm(array):
    return pltpu.with_memory_space_constraint(array, pltpu.HBM)


def exchanged(array, axis):
    return lax.all_to_all(array, axis, split_axis=0, concat_axis=0, tiled=True)


def swapped(array, axis, step):
    return lax.ppermute(array, axis, [(i, i ^ step) for i in range(lax.axis_size(axis))])


def added(a, b):
    return (a.astype(F32) + b.astype(F32)).astype(BF16)


def layer(inputs, gain, w_in, w_out, history, filt_far, filt_near):
    rows, width = inputs.shape
    fresh = filt_near.shape[0]
    ctx_count = lax.axis_size("ctx")
    chan_count = lax.axis_size("chan")
    ctx_index = lax.axis_index("ctx")
    forward, inverse = [jnp.asarray(t) for t in dft_tables(fresh)]
    index = ctx_index.reshape(1).astype(jnp.int32)
    last = (index == ctx_count - 1).astype(jnp.int32)

    unit = fresh * fresh * 4 * width
    w_three = w_in.transpose(1, 0, 2)
    border = lax.ppermute(filt_far, "ctx", [(i, i - 1) for i in range(1, ctx_count)])
    loads = (filt_far, filt_near, history, forward, inverse, gain.reshape(-1, 128))
    copies, own, near, past, f, i, scales = call(
        open_kernel,
        (
            jax.ShapeDtypeStruct((chan_count, rows, width), BF16),
            *(jax.ShapeDtypeStruct(a.shape, a.dtype) for a in loads),
        ),
        [HBM] * 7,
        1 << 10,
        1 << 21,
        scratch=[pltpu.VMEM((rows, width), BF16), pltpu.SemaphoreType.DMA((7 + chan_count,))],
        out_specs=(pl.BlockSpec(memory_space=pl.ANY), *[VMEM] * 6),
    )(*(in_hbm(a) for a in (inputs, *loads)))
    gathered = exchanged(copies, "chan")

    lanes = width // 2
    half = jax.ShapeDtypeStruct((fresh, lanes), F32)
    spread = (2 * fresh, lanes)
    head = jax.ShapeDtypeStruct((9 * width, width), BF16)
    keep_one, send_one, later, w_head = call(
        first_past_kernel,
        (half, half, jax.ShapeDtypeStruct((3, fresh, width), BF16), head),
        [SMEM, SMEM] + [VMEM] * 6 + [HBM],
        unit * 9,
        2 << 20,
        scratch=[pltpu.VMEM((3, 2, *spread), F32), pltpu.SemaphoreType.DMA],
    )(index, last, border, own, near, past, f, i, in_hbm(w_three))
    came_one = swapped(send_one, "ctx", 1)
    keep_two, send_two = call(
        second_past_kernel,
        (half, half),
        [SMEM] + [VMEM] * 3,
        unit * 9,
        1 << 20,
        scratch=[pltpu.VMEM((ctx_count // 2, 2, rows, width), F32)],
    )(index, later, f, i)
    came_two = swapped(send_two, "ctx", 1)
    here = added(keep_one, came_one)
    there = swapped(here, "ctx", 2)

    payload, gate_two = call(
        project_kernel,
        (
            jax.ShapeDtypeStruct((ctx_count, 3 * rows, lanes), BF16),
            jax.ShapeDtypeStruct((rows, width), BF16),
        ),
        [VMEM, VMEM, VMEM, HBM, VMEM, VMEM],
        2 * rows * w_in.size,
        2 * w_in.size,
        scratch=[
            pltpu.VMEM((ctx_count, 3 * rows, lanes), BF16),
            pltpu.VMEM((rows, w_in.shape[0]), BF16),
            pltpu.VMEM(w_three.shape, BF16),
            pltpu.SemaphoreType.DMA((10,)),
            pltpu.SemaphoreType.DMA,
        ],
        out_specs=(pl.BlockSpec(memory_space=pl.ANY), VMEM),
    )(gathered, scales, w_head, in_hbm(w_three), keep_two, came_two)

    here = added(here, there)
    payload, here = lax.optimization_barrier((payload, here))
    others = [swapped(here, "ctx", step) for step in (8, 12, 4)]
    arrived = exchanged(payload, "ctx")
    side = jax.ShapeDtypeStruct((width, w_out.shape[1] // 2), BF16)
    spectra, w_head = call(
        near_kernel,
        (jax.ShapeDtypeStruct((2, 2 * fresh, lanes), F32), side),
        [SMEM, VMEM, VMEM, HBM],
        unit * 2,
        2 << 20,
        scratch=[pltpu.VMEM((1, *spread), F32), pltpu.SemaphoreType.DMA],
    )(index, near, f, in_hbm(w_out))

    block = jax.ShapeDtypeStruct((2, rows, lanes), F32)
    keep, send, w_tail = call(
        mix_kernel,
        (block, block, side),
        [SMEM] + [VMEM] * 8 + [HBM],
        unit * 4,
        4 << 20,
        scratch=[
            pltpu.VMEM((fresh, lanes), BF16),
            pltpu.VMEM((2, 2, rows, lanes), F32),
            pltpu.SemaphoreType.DMA,
        ],
    )(index, arrived, here, *others, spectra, f, i, in_hbm(w_out))
    came = swapped(send, "ctx", 1)
    partial, gated = call(
        finish_kernel,
        (
            jax.ShapeDtypeStruct((chan_count, rows, width), BF16),
            jax.ShapeDtypeStruct((rows, width), BF16),
        ),
        [SMEM] + [VMEM] * 5,
        unit,
        1 << 20,
    )(index, keep, came, gate_two, w_head, w_tail)
    mixed = call(
        total_kernel, jax.ShapeDtypeStruct((rows, width), BF16), [VMEM], 1 << 16, 1 << 17
    )(exchanged(partial, "chan"))
    return (mixed, gated)


def solution(mesh):
    placed = (
        P("ctx", "chan"),
        P(),
        P(None, None, "chan"),
        P("chan", None),
        P("ctx", None, "chan"),
        P("ctx", None, "chan"),
        P(None, None, "chan"),
    )
    return jax.shard_map(
        layer,
        mesh=mesh,
        in_specs=placed,
        out_specs=(P("ctx", "chan"), P("ctx", "chan")),
        check_vma=False,
    )
```

```python
import jax
import jax.numpy as jnp
import numpy as np
from jax import lax
from jax.experimental import pallas as pl
from jax.experimental.pallas import tpu as pltpu
from jax.sharding import PartitionSpec as P

BF16 = jnp.bfloat16
F32 = jnp.float32
VMEM = pl.BlockSpec(memory_space=pltpu.VMEM)
SMEM = pl.BlockSpec(memory_space=pltpu.SMEM)
HBM = pl.BlockSpec(memory_space=pltpu.HBM)
LIMIT = 24 << 20


def split_up(table):
    high = np.asarray(table, np.float32).astype(jnp.bfloat16)
    low = (table - high.astype(np.float64)).astype(np.float32).astype(jnp.bfloat16)
    return np.stack([high, low])


def dft_tables(length):
    order = np.concatenate([np.arange(0, length, 2), np.arange(1, length, 2)])
    theta = np.pi * (order + 0.5) / length
    angle = theta[:, None] * np.arange(length)[None, :]
    forward = np.concatenate([np.cos(angle), np.sin(angle)], 0)
    back = theta[None, :] * (length - 1 - np.arange(length))[:, None]
    inverse = np.concatenate([np.cos(back), -np.sin(back)], 1) / length
    return split_up(forward), split_up(inverse)


def dot(a, b):
    return jnp.dot(a, b, preferred_element_type=F32)


def spectrum(forward, rows):
    half = forward.shape[1] // 2
    return [dot(forward[0, r], rows) + dot(forward[1, r], rows) for r in (slice(half), slice(half, None))]


def back_to_time(inverse, product):
    upper = product.astype(BF16)
    lower = (product - upper.astype(F32)).astype(BF16)
    half = inverse.shape[1] // 2
    return jnp.concatenate(
        [
            dot(inverse[0, r], upper) + dot(inverse[0, r], lower) + dot(inverse[1, r], upper)
            for r in (slice(half), slice(half, None))
        ],
        0,
    )


def halves(rows):
    half = rows.shape[0] // 2
    return rows[:half], rows[half:]


def near_to_time(high, product):
    upper = product.astype(BF16)
    lower = (product - upper.astype(F32)).astype(BF16)
    lanes = product.shape[1]
    both = dot(high, jnp.concatenate([upper, lower], 1))
    return both[:, :lanes] + both[:, lanes:]


def times_conjugate(window, signal):
    (wc, ws), (sc, ss) = window, signal
    return jnp.concatenate([wc * sc + ws * ss, wc * ss - ws * sc], 0)


def spread_out(rows, spread):
    count, kinds, width = rows.shape
    flat = rows[...].reshape(count * kinds, width)
    lanes = spread.shape[2]
    for h in range(width // lanes):
        spread[h] = flat[:, h * lanes : (h + 1) * lanes].astype(F32)


def parted(spread, kinds, which):
    count = spread.shape[1] // kinds
    rows = [spread[h, pl.ds(which, count, stride=kinds), :].astype(BF16) for h in range(spread.shape[0])]
    return jnp.concatenate(rows, 1)


def past_part(own, after, history, f, i):
    quarter = f.shape[1] // 4
    first_cos, first_sin = spectrum(f, own)
    bc, bs = spectrum(f, after)
    window = (
        first_cos + jnp.concatenate([-bs[:quarter], bs[quarter:]], 0),
        first_sin + jnp.concatenate([bc[:quarter], -bc[quarter:]], 0),
    )
    return back_to_time(i, times_conjugate(window, spectrum(f, history)))


def open_kernel(*refs):
    (inputs, *loads), (copies, *kept), (held, sems) = refs[:7], refs[7:14], refs[14:]
    moves = [pltpu.make_async_copy(a, b, sems.at[n]) for n, (a, b) in enumerate(zip([inputs, *loads], [held, *kept]))]
    for move in moves:
        move.start()
    moves[0].wait()
    count = copies.shape[0]
    sent = [pltpu.make_async_copy(held, copies.at[d], sems.at[len(moves) + d]) for d in range(count)]
    for move in sent:
        move.start()
    for move in moves[1:] + sent:
        move.wait()


def first_past_kernel(
    index, last, border, own, near, history, f, i, w_hbm, keep, send, later, w_head, spread, sem
):
    load = pltpu.make_async_copy(w_hbm.at[0, pl.ds(0, w_head.shape[0]), :], w_head, sem)
    load.start()

    @pl.when(last[0] > 0)
    def _():
        spread_out(near, spread.at[1])

    @pl.when(last[0] == 0)
    def _():
        spread_out(border, spread.at[1])

    spread_out(own, spread.at[0])
    spread_out(history, spread.at[2])
    part = past_part(*(parted(spread.at[n], 2, 0) for n in range(3)), f, i)
    lanes = keep.shape[1]
    low, high = part[:, :lanes], part[:, lanes:]
    mine = index[0] % 2
    keep[...] = jnp.where(mine == 0, low, high)
    send[...] = jnp.where(mine == 0, high, low)
    for n in range(3):
        later[n] = parted(spread.at[n], 2, 1)
    load.wait()


def second_past_kernel(index, rows, f, i, keep, send, parts):
    mine = index[0] % 2
    parts[...] = past_part(rows[0], rows[1], rows[2], f, i).reshape(parts.shape)
    half, lanes = keep.shape[0] // 2, keep.shape[1]
    for h in range(2):
        there = pl.ds(h * half, half)
        span = slice(h * lanes, (h + 1) * lanes)
        keep[there] = parts[:, mine, :, span].reshape(half, lanes)
        send[there] = parts[:, 1 - mine, :, span].reshape(half, lanes)


def project_kernel(gathered, gain, w_head, w_hbm, keep, came, out_hbm, gate_two, out, normed, w, sems, done):
    pieces, rows, width = gathered.shape
    depth = pieces * width
    ready = w_head.shape[0]
    step = depth // 4
    chunks = []
    for k in range(3):
        edges = [*range(ready, depth, step), depth] if k == 0 else range(0, depth + 1, step)
        chunks += [(k, a, b) for a, b in zip(edges, edges[1:])]
    copies = []
    for n, (k, a, b) in enumerate(chunks):
        span = pl.ds(a, b - a)
        copies.append(pltpu.make_async_copy(w_hbm.at[k, span, :], w.at[k, span, :], sems.at[n]))
        copies[-1].start()
    lanes = out.shape[2]
    fresh = keep.shape[0]
    pair = (keep[...] + came[...]).astype(BF16)
    for d in range(out.shape[0]):
        start = (d % 2) * (fresh // 2) + (d // 2) * rows
        out[d, 2 * rows :] = pair[start : start + rows]
    total = jnp.zeros((rows, width), F32)
    for s in range(pieces):
        x = gathered[s].astype(F32)
        total += x * x
    mean_sq = jnp.sum(total, axis=1, keepdims=True) / depth
    scale = lax.rsqrt(mean_sq + 1e-06)
    for s in range(pieces):
        g = jnp.concatenate([gain[2 * s : 2 * s + 1], gain[2 * s + 1 : 2 * s + 2]], 1)
        normed[:, s * width : (s + 1) * width] = (gathered[s].astype(F32) * scale * g).astype(BF16)
    sums = [dot(normed[:, :ready], w_head[...]), jnp.zeros((rows, width), F32), jnp.zeros((rows, width), F32)]
    sent = pltpu.make_async_copy(out, out_hbm, done)
    for n, (k, a, b) in enumerate(chunks):
        copies[n].wait()
        sums[k] += dot(normed[:, a:b], w[k, a:b, :])
        if k < 2 and b == depth:
            part = sums[k].astype(BF16)
            for d in range(out.shape[0]):
                out[d, k * rows : (k + 1) * rows] = part[:, (d % 2) * lanes : (d % 2 + 1) * lanes]
            if k == 1:
                sent.start()
    gate_two[...] = sums[2].astype(BF16)
    sent.wait()


def near_kernel(index, near, f, w_hbm, spectra, w_out, spread, sem):
    load = pltpu.make_async_copy(w_hbm.at[:, pl.ds(0, w_out.shape[1])], w_out, sem)
    load.start()
    lanes = spectra.shape[2]
    half = pl.ds(pl.multiple_of((index[0] % 2) * lanes, lanes), lanes)
    spread_out(near.at[:, :, half], spread)
    for which in range(2):
        half = spectra.shape[1] // 2
        spectra[which, :half], spectra[which, half:] = spectrum(f, parted(spread, 2, which))
    load.wait()


def mix_kernel(index, arrived, here, there, spectra, f, i, w_hbm, keep, send, w_tail, gated_all, sums, sem):
    start = w_hbm.shape[1] - w_tail.shape[1]
    load = pltpu.make_async_copy(w_hbm.at[:, pl.ds(start, w_tail.shape[1])], w_tail, sem)
    load.start()
    count, packed, lanes = arrived.shape
    rows = packed // 3
    fresh = count * rows
    values = arrived[:, :rows].reshape(fresh, lanes)
    gate_one = arrived[:, rows : 2 * rows].reshape(fresh, lanes).astype(F32)
    past_one = here[...].astype(F32) + there[...].astype(F32)
    first = near_to_time(i[0], times_conjugate(halves(spectra[0]), halves(dot(f[0], values))))
    gated = (gate_one * (past_one + first)).astype(BF16)
    gated_all[...] = gated
    mine = index[0] % 2
    chip = pl.ds(pl.multiple_of((index[0] - mine) * rows, 2 * rows), 2 * rows)
    second = near_to_time(i[0, chip, :], times_conjugate(halves(spectra[1]), halves(dot(f[0], gated))))
    past_two = [arrived[p, 2 * rows :].astype(F32) for p in range(2)]
    for s in range(2, count):
        past_two[s % 2] += arrived[s, 2 * rows :].astype(F32)
    sums[0] = (second + jnp.concatenate(past_two, 0)).reshape(sums.shape[1:])
    sums[1] = gated_all[chip, :].astype(F32).reshape(sums.shape[1:])
    keep[...] = sums[:, mine]
    send[...] = sums[:, 1 - mine]
    load.wait()


def finish_kernel(index, keep, came, gate_two, w_head, w_tail, partial, gated):
    first = index[0] % 2 == 0
    low, high = jnp.where(first, keep[...], came[...]), jnp.where(first, came[...], keep[...])
    both = jnp.concatenate([low, high], 2)
    gated[...] = both[1].astype(BF16)
    mixed_in = (gate_two[...].astype(F32) * both[0]).astype(BF16)
    width = partial.shape[2]
    for d in range(partial.shape[0]):
        start = d * width
        block = w_head
        if start >= w_head.shape[1]:
            start, block = start - w_head.shape[1], w_tail
        partial[d] = dot(mixed_in, block[:, start : start + width]).astype(BF16)


def total_kernel(arrived, out):
    out[...] = jnp.sum(arrived[...].astype(F32), axis=0).astype(BF16)


def call(kernel, out_shape, in_specs, flops, nbytes, scratch=(), limit=LIMIT, out_specs=None):
    return pl.pallas_call(
        kernel,
        out_shape=out_shape,
        in_specs=in_specs,
        out_specs=out_specs or jax.tree.map(lambda _: VMEM, out_shape),
        scratch_shapes=list(scratch),
        cost_estimate=pl.CostEstimate(flops=flops, bytes_accessed=nbytes, transcendentals=0),
        compiler_params=pltpu.CompilerParams(vmem_limit_bytes=limit),
    )


def in_hbm(array):
    return pltpu.with_memory_space_constraint(array, pltpu.HBM)


def exchanged(array, axis):
    return lax.all_to_all(array, axis, split_axis=0, concat_axis=0, tiled=True)


def swapped(array, axis, step):
    return lax.ppermute(array, axis, [(i, i ^ step) for i in range(lax.axis_size(axis))])


def added(a, b):
    return (a.astype(F32) + b.astype(F32)).astype(BF16)


def layer(inputs, gain, w_in, w_out, history, filt_far, filt_near):
    rows, width = inputs.shape
    fresh = filt_near.shape[0]
    ctx_count = lax.axis_size("ctx")
    chan_count = lax.axis_size("chan")
    ctx_index = lax.axis_index("ctx")
    forward, inverse = [jnp.asarray(t) for t in dft_tables(fresh)]
    index = ctx_index.reshape(1).astype(jnp.int32)
    last = (index == ctx_count - 1).astype(jnp.int32)

    unit = fresh * fresh * 4 * width
    w_three = w_in.transpose(1, 0, 2)
    border = lax.ppermute(filt_far, "ctx", [(i, i - 1) for i in range(1, ctx_count)])
    loads = (filt_far, filt_near, history, forward, inverse, gain.reshape(-1, 128))
    copies, own, near, past, f, i, scales = call(
        open_kernel,
        (
            jax.ShapeDtypeStruct((chan_count, rows, width), BF16),
            *(jax.ShapeDtypeStruct(a.shape, a.dtype) for a in loads),
        ),
        [HBM] * 7,
        1 << 10,
        1 << 21,
        scratch=[pltpu.VMEM((rows, width), BF16), pltpu.SemaphoreType.DMA((7 + chan_count,))],
        out_specs=(pl.BlockSpec(memory_space=pl.ANY), *[VMEM] * 6),
    )(*(in_hbm(a) for a in (inputs, *loads)))
    gathered = exchanged(copies, "chan")

    lanes = width // 2
    half = jax.ShapeDtypeStruct((fresh, lanes), F32)
    spread = (2 * fresh, lanes)
    head = jax.ShapeDtypeStruct((9 * width, width), BF16)
    keep_one, send_one, later, w_head = call(
        first_past_kernel,
        (half, half, jax.ShapeDtypeStruct((3, fresh, width), BF16), head),
        [SMEM, SMEM] + [VMEM] * 6 + [HBM],
        unit * 9,
        2 << 20,
        scratch=[pltpu.VMEM((3, 2, *spread), F32), pltpu.SemaphoreType.DMA],
    )(index, last, border, own, near, past, f, i, in_hbm(w_three))
    came_one = swapped(send_one, "ctx", 1)
    keep_two, send_two = call(
        second_past_kernel,
        (half, half),
        [SMEM] + [VMEM] * 3,
        unit * 9,
        1 << 20,
        scratch=[pltpu.VMEM((ctx_count // 2, 2, rows, width), F32)],
    )(index, later, f, i)
    came_two = swapped(send_two, "ctx", 1)
    here = added(keep_one, came_one)
    there = swapped(here, "ctx", 2)

    payload, gate_two = call(
        project_kernel,
        (
            jax.ShapeDtypeStruct((ctx_count, 3 * rows, lanes), BF16),
            jax.ShapeDtypeStruct((rows, width), BF16),
        ),
        [VMEM, VMEM, VMEM, HBM, VMEM, VMEM],
        2 * rows * w_in.size,
        2 * w_in.size,
        scratch=[
            pltpu.VMEM((ctx_count, 3 * rows, lanes), BF16),
            pltpu.VMEM((rows, w_in.shape[0]), BF16),
            pltpu.VMEM(w_three.shape, BF16),
            pltpu.SemaphoreType.DMA((10,)),
            pltpu.SemaphoreType.DMA,
        ],
        out_specs=(pl.BlockSpec(memory_space=pl.ANY), VMEM),
    )(gathered, scales, w_head, in_hbm(w_three), keep_two, came_two)

    here = added(here, there)
    payload, here = lax.optimization_barrier((payload, here))
    there = swapped(here, "ctx", 8)
    arrived = exchanged(payload, "ctx")
    here = added(here, there)
    there = swapped(here, "ctx", 4)
    side = jax.ShapeDtypeStruct((width, w_out.shape[1] // 2), BF16)
    spectra, w_head = call(
        near_kernel,
        (jax.ShapeDtypeStruct((2, 2 * fresh, lanes), F32), side),
        [SMEM, VMEM, VMEM, HBM],
        unit * 2,
        2 << 20,
        scratch=[pltpu.VMEM((1, *spread), F32), pltpu.SemaphoreType.DMA],
    )(index, near, f, in_hbm(w_out))

    block = jax.ShapeDtypeStruct((2, rows, lanes), F32)
    keep, send, w_tail = call(
        mix_kernel,
        (block, block, side),
        [SMEM] + [VMEM] * 6 + [HBM],
        unit * 4,
        4 << 20,
        scratch=[
            pltpu.VMEM((fresh, lanes), BF16),
            pltpu.VMEM((2, 2, rows, lanes), F32),
            pltpu.SemaphoreType.DMA,
        ],
    )(index, arrived, here, there, spectra, f, i, in_hbm(w_out))
    came = swapped(send, "ctx", 1)
    partial, gated = call(
        finish_kernel,
        (
            jax.ShapeDtypeStruct((chan_count, rows, width), BF16),
            jax.ShapeDtypeStruct((rows, width), BF16),
        ),
        [SMEM] + [VMEM] * 5,
        unit,
        1 << 20,
    )(index, keep, came, gate_two, w_head, w_tail)
    mixed = call(
        total_kernel, jax.ShapeDtypeStruct((rows, width), BF16), [VMEM], 1 << 16, 1 << 17
    )(exchanged(partial, "chan"))
    return (mixed, gated)


def solution(mesh):
    placed = (
        P("ctx", "chan"),
        P(),
        P(None, None, "chan"),
        P("chan", None),
        P("ctx", None, "chan"),
        P("ctx", None, "chan"),
        P(None, None, "chan"),
    )
    return jax.shard_map(
        layer,
        mesh=mesh,
        in_specs=placed,
        out_specs=(P("ctx", "chan"), P("ctx", "chan")),
        check_vma=False,
    )
```

```python
import jax
import jax.numpy as jnp
import numpy as np
from jax import lax
from jax.experimental import pallas as pl
from jax.experimental.pallas import tpu as pltpu
from jax.sharding import PartitionSpec as P

BF16 = jnp.bfloat16
F32 = jnp.float32
VMEM = pl.BlockSpec(memory_space=pltpu.VMEM)
SMEM = pl.BlockSpec(memory_space=pltpu.SMEM)
HBM = pl.BlockSpec(memory_space=pltpu.HBM)
LIMIT = 24 << 20


def split_up(table):
    high = np.asarray(table, np.float32).astype(jnp.bfloat16)
    low = (table - high.astype(np.float64)).astype(np.float32).astype(jnp.bfloat16)
    return high, low


def dft_tables(length):
    order = np.concatenate([np.arange(0, length, 2), np.arange(1, length, 2)])
    theta = np.pi * (order + 0.5) / length
    angle = theta[:, None] * np.arange(length)[None, :]
    forward = np.concatenate([np.cos(angle), np.sin(angle)], 0)
    back = theta[None, :] * (length - 1 - np.arange(length))[:, None]
    inverse = np.concatenate([np.cos(back), -np.sin(back)], 1) / length
    return *split_up(forward), *split_up(inverse)


def dot(a, b):
    return jnp.dot(a, b, preferred_element_type=F32)


def spectrum(forward, rows):
    half = forward[0].shape[0] // 2
    return [sum(dot(table[r], rows) for table in forward) for r in (slice(half), slice(half, None))]


def back_to_time(inverse, product):
    upper = product.astype(BF16)
    lower = (product - upper.astype(F32)).astype(BF16)
    high, low = inverse
    half = high.shape[0] // 2
    return jnp.concatenate(
        [
            dot(high[r], upper) + dot(high[r], lower) + dot(low[r], upper)
            for r in (slice(half), slice(half, None))
        ],
        0,
    )


def halves(rows):
    half = rows.shape[0] // 2
    return rows[:half], rows[half:]


def near_to_time(high, product):
    upper = product.astype(BF16)
    lower = (product - upper.astype(F32)).astype(BF16)
    lanes = product.shape[1]
    both = dot(high, jnp.concatenate([upper, lower], 1))
    return both[:, :lanes] + both[:, lanes:]


def times_conjugate(window, signal):
    (wc, ws), (sc, ss) = window, signal
    return jnp.concatenate([wc * sc + ws * ss, wc * ss - ws * sc], 0)


def spread_out(rows, spread):
    count, kinds, width = rows.shape
    flat = rows[...].reshape(count * kinds, width)
    lanes = spread.shape[2]
    for h in range(width // lanes):
        spread[h] = flat[:, h * lanes : (h + 1) * lanes].astype(F32)


def parted(spread, kinds, which):
    count = spread.shape[1] // kinds
    rows = [spread[h, pl.ds(which, count, stride=kinds), :].astype(BF16) for h in range(spread.shape[0])]
    return jnp.concatenate(rows, 1)


def past_part(own, after, history, f, i):
    quarter = f[0].shape[0] // 4
    first_cos, first_sin = spectrum(f, own)
    bc, bs = spectrum(f, after)
    window = (
        first_cos + jnp.concatenate([-bs[:quarter], bs[quarter:]], 0),
        first_sin + jnp.concatenate([bc[:quarter], -bc[quarter:]], 0),
    )
    return back_to_time(i, times_conjugate(window, spectrum(f, history)))


def open_kernel(*refs):
    (inputs, *loads), (copies, *kept), (held, sems) = refs[:9], refs[9:18], refs[18:]
    moves = [pltpu.make_async_copy(a, b, sems.at[n]) for n, (a, b) in enumerate(zip([inputs, *loads], [held, *kept]))]
    for move in moves:
        move.start()
    moves[0].wait()
    count = copies.shape[0]
    sent = [pltpu.make_async_copy(held, copies.at[d], sems.at[len(moves) + d]) for d in range(count)]
    for move in sent:
        move.start()
    for move in moves[1:] + sent:
        move.wait()


def first_past_kernel(
    index, last, border, own, near, history, fh, fl, ih, il, w_hbm, keep, send, later, w_head, spread, sem
):
    load = pltpu.make_async_copy(w_hbm.at[0, pl.ds(0, w_head.shape[0]), :], w_head, sem)
    load.start()

    @pl.when(last[0] > 0)
    def _():
        spread_out(near, spread.at[1])

    @pl.when(last[0] == 0)
    def _():
        spread_out(border, spread.at[1])

    spread_out(own, spread.at[0])
    spread_out(history, spread.at[2])
    part = past_part(*(parted(spread.at[n], 2, 0) for n in range(3)), (fh, fl), (ih, il))
    lanes = keep.shape[1]
    low, high = part[:, :lanes], part[:, lanes:]
    mine = index[0] % 2
    keep[...] = jnp.where(mine == 0, low, high)
    send[...] = jnp.where(mine == 0, high, low)
    for n in range(3):
        later[n] = parted(spread.at[n], 2, 1)
    load.wait()


def second_past_kernel(index, rows, fh, fl, ih, il, keep, send, parts):
    mine = index[0] % 2
    parts[...] = past_part(rows[0], rows[1], rows[2], (fh, fl), (ih, il)).reshape(parts.shape)
    half, lanes = keep.shape[0] // 2, keep.shape[1]
    for h in range(2):
        there = pl.ds(h * half, half)
        span = slice(h * lanes, (h + 1) * lanes)
        keep[there] = parts[:, mine, :, span].reshape(half, lanes)
        send[there] = parts[:, 1 - mine, :, span].reshape(half, lanes)


def project_kernel(gathered, gain, w_head, w_hbm, keep, came, out_hbm, gate_two, out, normed, w, sems, done):
    pieces, rows, width = gathered.shape
    depth = pieces * width
    ready = w_head.shape[0]
    step = depth // 4
    chunks = []
    for k in range(3):
        edges = [*range(ready, depth, step), depth] if k == 0 else range(0, depth + 1, step)
        chunks += [(k, a, b) for a, b in zip(edges, edges[1:])]
    copies = []
    for n, (k, a, b) in enumerate(chunks):
        span = pl.ds(a, b - a)
        copies.append(pltpu.make_async_copy(w_hbm.at[k, span, :], w.at[k, span, :], sems.at[n]))
        copies[-1].start()
    lanes = out.shape[2]
    fresh = keep.shape[0]
    pair = (keep[...] + came[...]).astype(BF16)
    for d in range(out.shape[0]):
        start = (d % 2) * (fresh // 2) + (d // 2) * rows
        out[d, 2 * rows :] = pair[start : start + rows]
    total = jnp.zeros((rows, width), F32)
    for s in range(pieces):
        x = gathered[s].astype(F32)
        total += x * x
    mean_sq = jnp.sum(total, axis=1, keepdims=True) / depth
    scale = lax.rsqrt(mean_sq + 1e-06)
    for s in range(pieces):
        g = jnp.concatenate([gain[2 * s : 2 * s + 1], gain[2 * s + 1 : 2 * s + 2]], 1)
        normed[:, s * width : (s + 1) * width] = (gathered[s].astype(F32) * scale * g).astype(BF16)
    sums = [dot(normed[:, :ready], w_head[...]), jnp.zeros((rows, width), F32), jnp.zeros((rows, width), F32)]
    sent = pltpu.make_async_copy(out, out_hbm, done)
    for n, (k, a, b) in enumerate(chunks):
        copies[n].wait()
        sums[k] += dot(normed[:, a:b], w[k, a:b, :])
        if k < 2 and b == depth:
            part = sums[k].astype(BF16)
            for d in range(out.shape[0]):
                out[d, k * rows : (k + 1) * rows] = part[:, (d % 2) * lanes : (d % 2 + 1) * lanes]
            if k == 1:
                sent.start()
    gate_two[...] = sums[2].astype(BF16)
    sent.wait()


def near_kernel(index, near_hbm, f, w_hbm, spectra, w_out, near, spread, sems):
    first = pltpu.make_async_copy(near_hbm, near, sems.at[0])
    first.start()
    load = pltpu.make_async_copy(w_hbm, w_out, sems.at[1])
    load.start()
    first.wait()
    lanes = spectra.shape[2]
    half = pl.ds(pl.multiple_of((index[0] % 2) * lanes, lanes), lanes)
    spread_out(near.at[:, :, half], spread)
    for which in range(2):
        half = spectra.shape[1] // 2
        spectra[which, :half], spectra[which, half:] = spectrum((f,), parted(spread, 2, which))
    load.wait()


def mix_kernel(index, arrived, here, there, spectra, f, i, keep, send, gated_all, sums):
    count, packed, lanes = arrived.shape
    rows = packed // 3
    fresh = count * rows
    values = arrived[:, :rows].reshape(fresh, lanes)
    gate_one = arrived[:, rows : 2 * rows].reshape(fresh, lanes).astype(F32)
    past_one = here[...].astype(F32) + there[...].astype(F32)
    first = near_to_time(i[...], times_conjugate(halves(spectra[0]), halves(dot(f[...], values))))
    gated = (gate_one * (past_one + first)).astype(BF16)
    gated_all[...] = gated
    mine = index[0] % 2
    chip = pl.ds(pl.multiple_of((index[0] - mine) * rows, 2 * rows), 2 * rows)
    second = near_to_time(i[chip, :], times_conjugate(halves(spectra[1]), halves(dot(f[...], gated))))
    past_two = [arrived[p, 2 * rows :].astype(F32) for p in range(2)]
    for s in range(2, count):
        past_two[s % 2] += arrived[s, 2 * rows :].astype(F32)
    sums[0] = (second + jnp.concatenate(past_two, 0)).reshape(sums.shape[1:])
    sums[1] = gated_all[chip, :].astype(F32).reshape(sums.shape[1:])
    keep[...] = sums[:, mine]
    send[...] = sums[:, 1 - mine]


def finish_kernel(index, keep, came, gate_two, w_out, partial, gated):
    first = index[0] % 2 == 0
    low, high = jnp.where(first, keep[...], came[...]), jnp.where(first, came[...], keep[...])
    both = jnp.concatenate([low, high], 2)
    gated[...] = both[1].astype(BF16)
    mixed_in = (gate_two[...].astype(F32) * both[0]).astype(BF16)
    width = partial.shape[2]
    for d in range(partial.shape[0]):
        partial[d] = dot(mixed_in, w_out[:, d * width : (d + 1) * width]).astype(BF16)


def total_kernel(arrived, out):
    out[...] = jnp.sum(arrived[...].astype(F32), axis=0).astype(BF16)


def call(kernel, out_shape, in_specs, flops, nbytes, scratch=(), limit=LIMIT, out_specs=None):
    return pl.pallas_call(
        kernel,
        out_shape=out_shape,
        in_specs=in_specs,
        out_specs=out_specs or jax.tree.map(lambda _: VMEM, out_shape),
        scratch_shapes=list(scratch),
        cost_estimate=pl.CostEstimate(flops=flops, bytes_accessed=nbytes, transcendentals=0),
        compiler_params=pltpu.CompilerParams(vmem_limit_bytes=limit),
    )


def in_hbm(array):
    return pltpu.with_memory_space_constraint(array, pltpu.HBM)


def exchanged(array, axis):
    return lax.all_to_all(array, axis, split_axis=0, concat_axis=0, tiled=True)


def swapped(array, axis, step):
    return lax.ppermute(array, axis, [(i, i ^ step) for i in range(lax.axis_size(axis))])


def added(a, b):
    return (a.astype(F32) + b.astype(F32)).astype(BF16)


def layer(inputs, gain, w_in, w_out, history, filt_far, filt_near):
    rows, width = inputs.shape
    fresh = filt_near.shape[0]
    ctx_count = lax.axis_size("ctx")
    chan_count = lax.axis_size("chan")
    ctx_index = lax.axis_index("ctx")
    tables = [jnp.asarray(t) for t in dft_tables(fresh)]
    index = ctx_index.reshape(1).astype(jnp.int32)
    last = (index == ctx_count - 1).astype(jnp.int32)

    unit = fresh * fresh * 4 * width
    w_three = w_in.transpose(1, 0, 2)
    border = lax.ppermute(filt_far, "ctx", [(i, i - 1) for i in range(1, ctx_count)])
    loads = (filt_far, filt_near, history, *tables, gain.reshape(-1, 128))
    copies, own, near, past, fh, fl, ih, il, scales = call(
        open_kernel,
        (
            jax.ShapeDtypeStruct((chan_count, rows, width), BF16),
            *(jax.ShapeDtypeStruct(a.shape, a.dtype) for a in loads),
        ),
        [HBM] * 9,
        1 << 10,
        1 << 21,
        scratch=[pltpu.VMEM((rows, width), BF16), pltpu.SemaphoreType.DMA((9 + chan_count,))],
        out_specs=(pl.BlockSpec(memory_space=pl.ANY), *[VMEM] * 8),
    )(*(in_hbm(a) for a in (inputs, *loads)))
    gathered = exchanged(copies, "chan")

    lanes = width // 2
    half = jax.ShapeDtypeStruct((fresh, lanes), F32)
    spread = (2 * fresh, lanes)
    head = jax.ShapeDtypeStruct((9 * width, width), BF16)
    keep_one, send_one, later, w_head = call(
        first_past_kernel,
        (half, half, jax.ShapeDtypeStruct((3, fresh, width), BF16), head),
        [SMEM, SMEM] + [VMEM] * 8 + [HBM],
        unit * 9,
        2 << 20,
        scratch=[pltpu.VMEM((3, 2, *spread), F32), pltpu.SemaphoreType.DMA],
    )(index, last, border, own, near, past, fh, fl, ih, il, in_hbm(w_three))
    came_one = swapped(send_one, "ctx", 1)
    keep_two, send_two = call(
        second_past_kernel,
        (half, half),
        [SMEM] + [VMEM] * 5,
        unit * 9,
        1 << 20,
        scratch=[pltpu.VMEM((ctx_count // 2, 2, rows, width), F32)],
    )(index, later, fh, fl, ih, il)
    came_two = swapped(send_two, "ctx", 1)
    here = added(keep_one, came_one)
    there = swapped(here, "ctx", 8)

    payload, gate_two = call(
        project_kernel,
        (
            jax.ShapeDtypeStruct((ctx_count, 3 * rows, lanes), BF16),
            jax.ShapeDtypeStruct((rows, width), BF16),
        ),
        [VMEM, VMEM, VMEM, HBM, VMEM, VMEM],
        2 * rows * w_in.size,
        2 * w_in.size,
        scratch=[
            pltpu.VMEM((ctx_count, 3 * rows, lanes), BF16),
            pltpu.VMEM((rows, w_in.shape[0]), BF16),
            pltpu.VMEM(w_three.shape, BF16),
            pltpu.SemaphoreType.DMA((10,)),
            pltpu.SemaphoreType.DMA,
        ],
        out_specs=(pl.BlockSpec(memory_space=pl.ANY), VMEM),
    )(gathered, scales, w_head, in_hbm(w_three), keep_two, came_two)

    here = added(here, there)
    payload, here = lax.optimization_barrier((payload, here))
    there = swapped(here, "ctx", 2)
    arrived = exchanged(payload, "ctx")
    here = added(here, there)
    there = swapped(here, "ctx", 4)
    spectra, w_out = call(
        near_kernel,
        (jax.ShapeDtypeStruct((2, 2 * fresh, lanes), F32), jax.ShapeDtypeStruct(w_out.shape, BF16)),
        [SMEM, HBM, VMEM, HBM],
        unit * 2,
        2 << 20,
        scratch=[pltpu.VMEM(filt_near.shape, BF16), pltpu.VMEM((1, *spread), F32), pltpu.SemaphoreType.DMA((2,))],
    )(index, in_hbm(filt_near), fh, in_hbm(w_out))

    block = jax.ShapeDtypeStruct((2, rows, lanes), F32)
    keep, send = call(
        mix_kernel,
        (block, block),
        [SMEM] + [VMEM] * 6,
        unit * 4,
        4 << 20,
        scratch=[
            pltpu.VMEM((fresh, lanes), BF16),
            pltpu.VMEM((2, 2, rows, lanes), F32),
        ],
    )(index, arrived, here, there, spectra, fh, ih)
    came = swapped(send, "ctx", 1)
    partial, gated = call(
        finish_kernel,
        (
            jax.ShapeDtypeStruct((chan_count, rows, width), BF16),
            jax.ShapeDtypeStruct((rows, width), BF16),
        ),
        [SMEM] + [VMEM] * 4,
        unit,
        1 << 20,
    )(index, keep, came, gate_two, w_out)
    mixed = call(
        total_kernel, jax.ShapeDtypeStruct((rows, width), BF16), [VMEM], 1 << 16, 1 << 17
    )(exchanged(partial, "chan"))
    return (mixed, gated)


def solution(mesh):
    placed = (
        P("ctx", "chan"),
        P(),
        P(None, None, "chan"),
        P("chan", None),
        P("ctx", None, "chan"),
        P("ctx", None, "chan"),
        P(None, None, "chan"),
    )
    return jax.shard_map(
        layer,
        mesh=mesh,
        in_specs=placed,
        out_specs=(P("ctx", "chan"), P("ctx", "chan")),
        check_vma=False,
    )
```

```python
import jax
import jax.numpy as jnp
import numpy as np
from jax import lax
from jax.experimental import pallas as pl
from jax.experimental.pallas import tpu as pltpu
from jax.sharding import PartitionSpec as P

BF16 = jnp.bfloat16
F32 = jnp.float32
VMEM = pl.BlockSpec(memory_space=pltpu.VMEM)
SMEM = pl.BlockSpec(memory_space=pltpu.SMEM)
HBM = pl.BlockSpec(memory_space=pltpu.HBM)
LIMIT = 24 << 20


def split_up(table):
    high = np.asarray(table, np.float32).astype(jnp.bfloat16)
    low = (table - high.astype(np.float64)).astype(np.float32).astype(jnp.bfloat16)
    return high, low


def dft_tables(length):
    order = np.concatenate([np.arange(0, length, 2), np.arange(1, length, 2)])
    theta = np.pi * (order + 0.5) / length
    angle = theta[:, None] * np.arange(length)[None, :]
    forward = np.concatenate([np.cos(angle), np.sin(angle)], 0)
    back = theta[None, :] * (length - 1 - np.arange(length))[:, None]
    inverse = np.concatenate([np.cos(back), -np.sin(back)], 1) / length
    return *split_up(forward), *split_up(inverse)


def dot(a, b):
    return jnp.dot(a, b, preferred_element_type=F32)


def spectrum(forward, rows):
    half = forward[0].shape[0] // 2
    return [sum(dot(table[r], rows) for table in forward) for r in (slice(half), slice(half, None))]


def back_to_time(inverse, product):
    upper = product.astype(BF16)
    lower = (product - upper.astype(F32)).astype(BF16)
    half = inverse.shape[0] // 2
    return jnp.concatenate(
        [
            dot(inverse[r], upper) + dot(inverse[r], lower)
            for r in (slice(half), slice(half, None))
        ],
        0,
    )


def halves(rows):
    half = rows.shape[0] // 2
    return rows[:half], rows[half:]


def near_to_time(high, product):
    upper = product.astype(BF16)
    lower = (product - upper.astype(F32)).astype(BF16)
    lanes = product.shape[1]
    both = dot(high, jnp.concatenate([upper, lower], 1))
    return both[:, :lanes] + both[:, lanes:]


def times_conjugate(window, signal):
    (wc, ws), (sc, ss) = window, signal
    return jnp.concatenate([wc * sc + ws * ss, wc * ss - ws * sc], 0)


def spread_out(rows, spread):
    count, kinds, width = rows.shape
    flat = rows[...].reshape(count * kinds, width)
    lanes = spread.shape[2]
    for h in range(width // lanes):
        spread[h] = flat[:, h * lanes : (h + 1) * lanes].astype(F32)


def parted(spread, kinds, which):
    count = spread.shape[1] // kinds
    rows = [spread[h, pl.ds(which, count, stride=kinds), :].astype(BF16) for h in range(spread.shape[0])]
    return jnp.concatenate(rows, 1)


def past_part(own, after, history, f, i):
    quarter = f[0].shape[0] // 4
    first_cos, first_sin = spectrum(f, own)
    bc, bs = spectrum(f, after)
    window = (
        first_cos + jnp.concatenate([-bs[:quarter], bs[quarter:]], 0),
        first_sin + jnp.concatenate([bc[:quarter], -bc[quarter:]], 0),
    )
    return back_to_time(i, times_conjugate(window, spectrum(f, history)))


def open_kernel(*refs):
    (inputs, *loads), (copies, *kept), (held, sems) = refs[:8], refs[8:16], refs[16:]
    moves = [pltpu.make_async_copy(a, b, sems.at[n]) for n, (a, b) in enumerate(zip([inputs, *loads], [held, *kept]))]
    for move in moves:
        move.start()
    moves[0].wait()
    count = copies.shape[0]
    sent = [pltpu.make_async_copy(held, copies.at[d], sems.at[len(moves) + d]) for d in range(count)]
    for move in sent:
        move.start()
    for move in moves[1:] + sent:
        move.wait()


def first_past_kernel(
    index, last, border, own, near, history, fh, fl, ih, w_hbm, keep, send, later, w_head, spread, sem
):
    load = pltpu.make_async_copy(w_hbm.at[0, pl.ds(0, w_head.shape[0]), :], w_head, sem)
    load.start()

    @pl.when(last[0] > 0)
    def _():
        spread_out(near, spread.at[1])

    @pl.when(last[0] == 0)
    def _():
        spread_out(border, spread.at[1])

    spread_out(own, spread.at[0])
    spread_out(history, spread.at[2])
    part = past_part(*(parted(spread.at[n], 2, 0) for n in range(3)), (fh, fl), ih)
    lanes = keep.shape[1]
    low, high = part[:, :lanes], part[:, lanes:]
    mine = index[0] % 2
    keep[...] = jnp.where(mine == 0, low, high)
    send[...] = jnp.where(mine == 0, high, low)
    for n in range(3):
        later[n] = parted(spread.at[n], 2, 1)
    load.wait()


def second_past_kernel(index, rows, fh, fl, ih, keep, send, parts):
    mine = index[0] % 2
    parts[...] = past_part(rows[0], rows[1], rows[2], (fh, fl), ih).reshape(parts.shape)
    half, lanes = keep.shape[0] // 2, keep.shape[1]
    for h in range(2):
        there = pl.ds(h * half, half)
        span = slice(h * lanes, (h + 1) * lanes)
        keep[there] = parts[:, mine, :, span].reshape(half, lanes)
        send[there] = parts[:, 1 - mine, :, span].reshape(half, lanes)


def project_kernel(gathered, gain, w_head, w_hbm, keep, came, out_hbm, gate_two, out, normed, w, sems, done):
    pieces, rows, width = gathered.shape
    depth = pieces * width
    ready = w_head.shape[0]
    step = depth // 4
    chunks = []
    for k in range(3):
        edges = [*range(ready, depth, step), depth] if k == 0 else range(0, depth + 1, step)
        chunks += [(k, a, b) for a, b in zip(edges, edges[1:])]
    copies = []
    for n, (k, a, b) in enumerate(chunks):
        span = pl.ds(a, b - a)
        copies.append(pltpu.make_async_copy(w_hbm.at[k, span, :], w.at[k, span, :], sems.at[n]))
        copies[-1].start()
    lanes = out.shape[2]
    fresh = keep.shape[0]
    pair = (keep[...] + came[...]).astype(BF16)
    for d in range(out.shape[0]):
        start = (d % 2) * (fresh // 2) + (d // 2) * rows
        out[d, 2 * rows :] = pair[start : start + rows]
    total = jnp.zeros((rows, width), F32)
    for s in range(pieces):
        x = gathered[s].astype(F32)
        total += x * x
    mean_sq = jnp.sum(total, axis=1, keepdims=True) / depth
    scale = lax.rsqrt(mean_sq + 1e-06)
    for s in range(pieces):
        g = jnp.concatenate([gain[2 * s : 2 * s + 1], gain[2 * s + 1 : 2 * s + 2]], 1)
        normed[:, s * width : (s + 1) * width] = (gathered[s].astype(F32) * scale * g).astype(BF16)
    sums = [dot(normed[:, :ready], w_head[...]), jnp.zeros((rows, width), F32), jnp.zeros((rows, width), F32)]
    sent = pltpu.make_async_copy(out, out_hbm, done)
    for n, (k, a, b) in enumerate(chunks):
        copies[n].wait()
        sums[k] += dot(normed[:, a:b], w[k, a:b, :])
        if k < 2 and b == depth:
            part = sums[k].astype(BF16)
            for d in range(out.shape[0]):
                out[d, k * rows : (k + 1) * rows] = part[:, (d % 2) * lanes : (d % 2 + 1) * lanes]
            if k == 1:
                sent.start()
    gate_two[...] = sums[2].astype(BF16)
    sent.wait()


def near_kernel(index, near_hbm, f, w_hbm, spectra, w_out, near, spread, sems):
    first = pltpu.make_async_copy(near_hbm, near, sems.at[0])
    first.start()
    load = pltpu.make_async_copy(w_hbm, w_out, sems.at[1])
    load.start()
    first.wait()
    lanes = spectra.shape[2]
    half = pl.ds(pl.multiple_of((index[0] % 2) * lanes, lanes), lanes)
    spread_out(near.at[:, :, half], spread)
    for which in range(2):
        half = spectra.shape[1] // 2
        spectra[which, :half], spectra[which, half:] = spectrum((f,), parted(spread, 2, which))
    load.wait()


def mix_kernel(index, arrived, here, there, spectra, f, i, keep, send, gated_all, sums):
    count, packed, lanes = arrived.shape
    rows = packed // 3
    fresh = count * rows
    values = arrived[:, :rows].reshape(fresh, lanes)
    gate_one = arrived[:, rows : 2 * rows].reshape(fresh, lanes).astype(F32)
    past_one = here[...].astype(F32) + there[...].astype(F32)
    first = near_to_time(i[...], times_conjugate(halves(spectra[0]), halves(dot(f[...], values))))
    gated = (gate_one * (past_one + first)).astype(BF16)
    gated_all[...] = gated
    mine = index[0] % 2
    chip = pl.ds(pl.multiple_of((index[0] - mine) * rows, 2 * rows), 2 * rows)
    second = near_to_time(i[chip, :], times_conjugate(halves(spectra[1]), halves(dot(f[...], gated))))
    past_two = [arrived[p, 2 * rows :].astype(F32) for p in range(2)]
    for s in range(2, count):
        past_two[s % 2] += arrived[s, 2 * rows :].astype(F32)
    sums[0] = (second + jnp.concatenate(past_two, 0)).reshape(sums.shape[1:])
    sums[1] = gated_all[chip, :].astype(F32).reshape(sums.shape[1:])
    keep[...] = sums[:, mine]
    send[...] = sums[:, 1 - mine]


def finish_kernel(index, keep, came, gate_two, w_out, partial, gated):
    first = index[0] % 2 == 0
    low, high = jnp.where(first, keep[...], came[...]), jnp.where(first, came[...], keep[...])
    both = jnp.concatenate([low, high], 2)
    gated[...] = both[1].astype(BF16)
    mixed_in = (gate_two[...].astype(F32) * both[0]).astype(BF16)
    width = partial.shape[2]
    for d in range(partial.shape[0]):
        partial[d] = dot(mixed_in, w_out[:, d * width : (d + 1) * width]).astype(BF16)


def total_kernel(arrived, out):
    out[...] = jnp.sum(arrived[...].astype(F32), axis=0).astype(BF16)


def call(kernel, out_shape, in_specs, flops, nbytes, scratch=(), limit=LIMIT, out_specs=None):
    return pl.pallas_call(
        kernel,
        out_shape=out_shape,
        in_specs=in_specs,
        out_specs=out_specs or jax.tree.map(lambda _: VMEM, out_shape),
        scratch_shapes=list(scratch),
        cost_estimate=pl.CostEstimate(flops=flops, bytes_accessed=nbytes, transcendentals=0),
        compiler_params=pltpu.CompilerParams(vmem_limit_bytes=limit),
    )


def in_hbm(array):
    return pltpu.with_memory_space_constraint(array, pltpu.HBM)


def exchanged(array, axis):
    return lax.all_to_all(array, axis, split_axis=0, concat_axis=0, tiled=True)


def swapped(array, axis, step):
    return lax.ppermute(array, axis, [(i, i ^ step) for i in range(lax.axis_size(axis))])


def added(a, b):
    return (a.astype(F32) + b.astype(F32)).astype(BF16)


def layer(inputs, gain, w_in, w_out, history, filt_far, filt_near):
    rows, width = inputs.shape
    fresh = filt_near.shape[0]
    ctx_count = lax.axis_size("ctx")
    chan_count = lax.axis_size("chan")
    ctx_index = lax.axis_index("ctx")
    tables = [jnp.asarray(t) for t in dft_tables(fresh)[:3]]
    index = ctx_index.reshape(1).astype(jnp.int32)
    last = (index == ctx_count - 1).astype(jnp.int32)

    unit = fresh * fresh * 4 * width
    w_three = w_in.transpose(1, 0, 2)
    border = lax.ppermute(filt_far, "ctx", [(i, i - 1) for i in range(1, ctx_count)])
    loads = (filt_far, filt_near, history, *tables, gain.reshape(-1, 128))
    copies, own, near, past, fh, fl, ih, scales = call(
        open_kernel,
        (
            jax.ShapeDtypeStruct((chan_count, rows, width), BF16),
            *(jax.ShapeDtypeStruct(a.shape, a.dtype) for a in loads),
        ),
        [HBM] * 8,
        1 << 10,
        1 << 21,
        scratch=[pltpu.VMEM((rows, width), BF16), pltpu.SemaphoreType.DMA((8 + chan_count,))],
        out_specs=(pl.BlockSpec(memory_space=pl.ANY), *[VMEM] * 7),
    )(*(in_hbm(a) for a in (inputs, *loads)))
    gathered = exchanged(copies, "chan")

    lanes = width // 2
    half = jax.ShapeDtypeStruct((fresh, lanes), F32)
    spread = (2 * fresh, lanes)
    head = jax.ShapeDtypeStruct((9 * width, width), BF16)
    keep_one, send_one, later, w_head = call(
        first_past_kernel,
        (half, half, jax.ShapeDtypeStruct((3, fresh, width), BF16), head),
        [SMEM, SMEM] + [VMEM] * 7 + [HBM],
        unit * 9,
        2 << 20,
        scratch=[pltpu.VMEM((3, 2, *spread), F32), pltpu.SemaphoreType.DMA],
    )(index, last, border, own, near, past, fh, fl, ih, in_hbm(w_three))
    came_one = swapped(send_one, "ctx", 1)
    keep_two, send_two = call(
        second_past_kernel,
        (half, half),
        [SMEM] + [VMEM] * 4,
        unit * 9,
        1 << 20,
        scratch=[pltpu.VMEM((ctx_count // 2, 2, rows, width), F32)],
    )(index, later, fh, fl, ih)
    came_two = swapped(send_two, "ctx", 1)
    here = added(keep_one, came_one)
    there = swapped(here, "ctx", 2)

    payload, gate_two = call(
        project_kernel,
        (
            jax.ShapeDtypeStruct((ctx_count, 3 * rows, lanes), BF16),
            jax.ShapeDtypeStruct((rows, width), BF16),
        ),
        [VMEM, VMEM, VMEM, HBM, VMEM, VMEM],
        2 * rows * w_in.size,
        2 * w_in.size,
        scratch=[
            pltpu.VMEM((ctx_count, 3 * rows, lanes), BF16),
            pltpu.VMEM((rows, w_in.shape[0]), BF16),
            pltpu.VMEM(w_three.shape, BF16),
            pltpu.SemaphoreType.DMA((10,)),
            pltpu.SemaphoreType.DMA,
        ],
        out_specs=(pl.BlockSpec(memory_space=pl.ANY), VMEM),
    )(gathered, scales, w_head, in_hbm(w_three), keep_two, came_two)

    here = added(here, there)
    payload, here = lax.optimization_barrier((payload, here))
    there = swapped(here, "ctx", 8)
    arrived = exchanged(payload, "ctx")
    here = added(here, there)
    there = swapped(here, "ctx", 4)
    spectra, w_out = call(
        near_kernel,
        (jax.ShapeDtypeStruct((2, 2 * fresh, lanes), F32), jax.ShapeDtypeStruct(w_out.shape, BF16)),
        [SMEM, HBM, VMEM, HBM],
        unit * 2,
        2 << 20,
        scratch=[pltpu.VMEM(filt_near.shape, BF16), pltpu.VMEM((1, *spread), F32), pltpu.SemaphoreType.DMA((2,))],
    )(index, in_hbm(filt_near), fh, in_hbm(w_out))

    block = jax.ShapeDtypeStruct((2, rows, lanes), F32)
    keep, send = call(
        mix_kernel,
        (block, block),
        [SMEM] + [VMEM] * 6,
        unit * 4,
        4 << 20,
        scratch=[
            pltpu.VMEM((fresh, lanes), BF16),
            pltpu.VMEM((2, 2, rows, lanes), F32),
        ],
    )(index, arrived, here, there, spectra, fh, ih)
    came = swapped(send, "ctx", 1)
    partial, gated = call(
        finish_kernel,
        (
            jax.ShapeDtypeStruct((chan_count, rows, width), BF16),
            jax.ShapeDtypeStruct((rows, width), BF16),
        ),
        [SMEM] + [VMEM] * 4,
        unit,
        1 << 20,
    )(index, keep, came, gate_two, w_out)
    mixed = call(
        total_kernel, jax.ShapeDtypeStruct((rows, width), BF16), [VMEM], 1 << 16, 1 << 17
    )(exchanged(partial, "chan"))
    return (mixed, gated)


def solution(mesh):
    placed = (
        P("ctx", "chan"),
        P(),
        P(None, None, "chan"),
        P("chan", None),
        P("ctx", None, "chan"),
        P("ctx", None, "chan"),
        P(None, None, "chan"),
    )
    return jax.shard_map(
        layer,
        mesh=mesh,
        in_specs=placed,
        out_specs=(P("ctx", "chan"), P("ctx", "chan")),
        check_vma=False,
    )
```
